256 devices in a mesh: gx: 32 (over y_hi, z, core), gy: 8 (over y_lo, x).
Axes of the slice: x: 4, y: 4 (y_hi: 2, y_lo: 2; y = y_hi * 2 + y_lo), z: 8, core: 2. Of those that a mesh axis runs over, the one named last changes fastest.
Arguments:
- state_field: bfloat16 [1, 64, 2048, 2048], P(None, None, 'gx', 'gy'), may hold values from -6 to 6
- spectral_x: bfloat16 [2, 32, 2, 64, 64], P(None, 'gx'), may hold values from -2 to 2
- spectral_y: bfloat16 [2, 32, 2, 64, 64], P(None, 'gy'), may hold values from -2 to 2
- expand_weight: bfloat16 [2, 64, 256], replicated, may hold values from -0.75 to 0.75
- reduce_weight: bfloat16 [2, 256, 64], replicated, may hold values from -0.375 to 0.375
Outputs:
- next_state: bfloat16 [1, 64, 2048, 2048], P(None, None, 'gx', 'gy')
The draws below stay inside these ranges and needn't reach their ends.
All inputs are finite; a program needn't handle non-finite values.
Results may differ from the reference program's by a relative error of at most 0.025.
Values may be sent and summed in bfloat16 or wider, within the bound.
No kernel may reach another device: no remote copies, remote signals or barrier semaphores. Data moves between devices by JAX's collectives and lax.ppermute only.
A program may use at most 64 MiB of HBM per device.

```python
import jax
import jax.numpy as jnp
from jax import lax

NX = 2048
NY = 2048
CH = 64
HID = 256
MODES = 32
LAYERS = 2
ZP = 1


def shard_levels(rng, shape, shards, low, top_value):
    factor_of = 1.0
    for axis_at, blocks in shards:
        draws = jax.random.uniform(jax.random.fold_in(jax.random.fold_in(rng, 6), axis_at), (blocks,), jnp.float32, low / len(shards), top_value / len(shards))
        factor_of = factor_of * jnp.repeat(jnp.exp(draws), shape[axis_at] // blocks).reshape((-1,) + (1,) * (len(shape) - 1 - axis_at))
    return factor_of


def scatter_about(key, extent, width, reach, pieces=(), kind=jnp.bfloat16):
    values = jax.random.normal(key, extent, jnp.float32) * width
    if len(pieces) > 0:
        values = shard_levels(key, extent, pieces, -0.22, 0.18) * values
    return jnp.clip(values, min=-reach, max=reach).astype(kind)


def setup_inputs(seed: int = 0) -> dict:
    key_list = jax.random.split(jax.random.key(seed), 6)
    state_field = scatter_about(key_list[0], (ZP, CH, NX, NY), 1.0, 6.0, ((2, 32), (3, 8)))
    spectral_x = scatter_about(key_list[1], (LAYERS, MODES, 2, CH, CH), 8 ** -0.5, 2.0, ((1, 32),))
    spectral_y = scatter_about(key_list[2], (LAYERS, MODES, 2, CH, CH), 8 ** -0.5, 2.0, ((1, 8),))
    expand_weight = scatter_about(key_list[3], (LAYERS, CH, HID), CH ** -0.5, 0.75)
    reduce_weight = scatter_about(key_list[4], (LAYERS, HID, CH), HID ** -0.5, 0.375)
    return dict(state_field=state_field, spectral_x=spectral_x, spectral_y=spectral_y, expand_weight=expand_weight, reduce_weight=reduce_weight)


def make_tables(length, modes):
    positions = jnp.arange(length, dtype=jnp.int32)
    orders = jnp.arange(modes, dtype=jnp.int32)
    phase = orders[:, None] * positions[None, :] % length
    angle = 2.0 * jnp.pi * phase.astype(jnp.float32) / length
    factor = 1.0 / jnp.sqrt(jnp.float32(length))
    weight_two = jnp.where(orders == 0, 1.0, 2.0).astype(jnp.float32)[:, None]
    forward = jnp.stack([jnp.cos(angle) * factor, -jnp.sin(angle) * factor], axis=1)
    forward = forward.reshape(2 * modes, length).astype(jnp.bfloat16)
    inverse = jnp.stack([weight_two * jnp.cos(angle) * factor, -weight_two * jnp.sin(angle) * factor], axis=1)
    inverse = inverse.reshape(2 * modes, length).T.astype(jnp.bfloat16)
    return (forward, inverse)

def mix_modes(spectrum, weights):
    modes = weights.shape[0]
    shaped = spectrum.reshape((modes, 2) + spectrum.shape[1:]).astype(jnp.float32)
    weights = weights.astype(jnp.float32)
    real_in, imag_in = (shaped[:, 0], shaped[:, 1])
    real_w, imag_w = (weights[:, 0], weights[:, 1])

    def contract_modes(left, right):
        return jnp.einsum('koi,kzin->kzon', left, right)
    real_out = contract_modes(real_w, real_in) - contract_modes(imag_w, imag_in)
    imag_out = contract_modes(real_w, imag_in) + contract_modes(imag_w, real_in)
    joined = jnp.stack([real_out, imag_out], axis=1).astype(jnp.bfloat16)
    return joined.reshape(spectrum.shape)

def reference(state_field, spectral_x, spectral_y, expand_weight, reduce_weight):
    forward_x, inverse_x = make_tables(NX, MODES)
    forward_y, inverse_y = make_tables(NY, MODES)
    state = state_field
    block_rows = 128
    for layer_index in range(LAYERS):
        state_wide = state.astype(jnp.float32)
        spec_x = jnp.einsum('kx,zcxy->kzcy', forward_x.astype(jnp.float32), state_wide).astype(jnp.bfloat16)
        mixed_x = mix_modes(spec_x, spectral_x[layer_index])
        branch_x = jnp.einsum('xk,kzcy->zcxy', inverse_x.astype(jnp.float32), mixed_x.astype(jnp.float32)).astype(jnp.bfloat16)
        spec_y = jnp.einsum('ky,zcxy->kzcx', forward_y.astype(jnp.float32), state_wide).astype(jnp.bfloat16)
        mixed_y = mix_modes(spec_y, spectral_y[layer_index])
        branch_y = jnp.einsum('yk,kzcx->zcxy', inverse_y.astype(jnp.float32), mixed_y.astype(jnp.float32)).astype(jnp.bfloat16)
        total = (branch_x.astype(jnp.float32) + branch_y.astype(jnp.float32)).astype(jnp.bfloat16)
        expand_now = expand_weight[layer_index].astype(jnp.float32)
        reduce_now = reduce_weight[layer_index].astype(jnp.float32)
        blocks_total = jnp.moveaxis(total.reshape(ZP, CH, NX // block_rows, block_rows, NY), 2, 0)
        blocks_state = jnp.moveaxis(state.reshape(ZP, CH, NX // block_rows, block_rows, NY), 2, 0)

        def pointwise(pair):
            total_block, state_block = pair
            hidden = jax.nn.gelu(jnp.einsum('ch,zcxy->zhxy', expand_now, total_block.astype(jnp.float32)), approximate=True)
            hidden = hidden.astype(jnp.bfloat16).astype(jnp.float32)
            update = jnp.einsum('hc,zhxy->zcxy', reduce_now, hidden)
            return (state_block.astype(jnp.float32) + update).astype(jnp.bfloat16)
        result_blocks = lax.map(pointwise, (blocks_total, blocks_state))
        state = jnp.moveaxis(result_blocks, 0, 2).reshape(ZP, CH, NX, NY)
    return state
```

```python
import functools

import jax
import jax.numpy as jnp
import numpy as np
from jax import lax
from jax.experimental import pallas as pl
from jax.experimental.pallas import tpu as pltpu
from jax.sharding import PartitionSpec as P

F32 = jnp.float32
BF16 = jnp.bfloat16
NX = 2048
NY = 2048
CH = 64
HID = 256
MODES = 32
LAYERS = 2
RX = 10
RY = 20
RYP = 24
LINE = 8


def window_tables(length, devices, rank):
    window = length // devices
    k = np.arange(MODES)[:, None]
    p = np.arange(length)[None, :]
    angle = 2.0 * np.pi * ((k * p) % length) / length
    scale = 1.0 / np.sqrt(length)
    weight = np.where(np.arange(MODES) == 0, 1.0, 2.0)[:, None]
    forward = np.concatenate([np.cos(angle), -np.sin(angle)], 0) * scale
    inverse = np.concatenate([weight * np.cos(angle), -weight * np.sin(angle)], 0) * scale
    _, _, vt = np.linalg.svd(forward[:, :window], full_matrices=False)
    basis = vt[:rank]
    basis = basis * np.sign(basis[np.arange(rank), np.abs(basis).argmax(1)])[:, None]
    fwd = np.stack([forward[:, d * window : (d + 1) * window] @ basis.T for d in range(devices)])
    inv = np.stack([inverse[:, d * window : (d + 1) * window] @ basis.T for d in range(devices)])
    return basis, fwd, inv


def bf(x):
    return np.asarray(x, np.float32).astype(jnp.bfloat16)


def make_constants():
    bx, fx, ix = window_tables(NX, 32, RX)
    by, fy, iy = window_tables(NY, 8, RY)
    pairs = RX // 2
    ax = fx.reshape(32, 64, pairs, 2).transpose(3, 1, 2, 0).reshape(128, pairs * 32)
    gx = ix.reshape(32, 2, MODES, pairs, 2)
    u0 = gx[..., 0].transpose(3, 0, 1, 2).reshape(pairs * 32, 64)
    u1 = gx[..., 1].transpose(3, 0, 1, 2)[:, :, ::-1].reshape(pairs * 32, 64)
    ux = np.concatenate([u0, u1], 0)
    pad = ((0, 0), (0, 0), (0, RYP - RY))
    fy, iy = np.pad(fy, pad), np.pad(iy, pad)
    ay = fy.transpose(1, 0, 2).reshape(64, 8 * RYP)
    gy = iy.transpose(0, 2, 1).reshape(8 * RYP, 64)
    cy = np.pad(by, ((0, RYP - RY), (0, 0)))
    bexp = np.repeat(bx, CH, axis=1)
    bexp = np.pad(bexp, ((0, 16 - RX), (0, 0)))
    return dict(
        ax=bf(ax), ux=bf(ux), ay=bf(ay), gy=bf(gy), cy=bf(cy), cyt=bf(cy.T), bexp=bf(bexp)
    )


def dot(a, b):
    return jnp.dot(a, b, preferred_element_type=F32)


def dot_nt(a, b):
    return lax.dot_general(a, b, (((1,), (1,)), ((), ())), preferred_element_type=F32)


def half_mask(rows):
    return lax.broadcasted_iota(jnp.int32, (rows, 128), 1) < 64


def first_kernel(state_ref, bexp_ref, cy_ref, kron_ref, zx_ref, zy_ref, acc_ref):
    g = pl.program_id(0)
    lanes = lax.broadcasted_iota(jnp.int32, (CH, 512), 1)
    rows = lax.broadcasted_iota(jnp.int32, (CH, 512), 0)
    eye = (lanes % CH) == rows
    for r in range(RX):
        row = jnp.broadcast_to(bexp_ref[r : r + 1, :].astype(F32), (CH, 512))
        kron_ref[r * CH : (r + 1) * CH, :] = jnp.where(eye, row, 0.0).astype(BF16)
    state = state_ref[...]
    part = dot_nt(state, kron_ref[...])

    @pl.when(g == 0)
    def _():
        acc_ref[...] = part

    @pl.when(g > 0)
    def _():
        acc_ref[...] += part

    zy_ref[0] = dot(cy_ref[...], state).astype(BF16)

    @pl.when(g == pl.num_programs(0) - 1)
    def _():
        zx_ref[...] = acc_ref[...].astype(BF16)


def first_call(state, c):
    return pl.pallas_call(
        first_kernel,
        name="first",
        grid=(8,),
        in_specs=[
            pl.BlockSpec((256, 512), lambda g: (0, g)),
            pl.BlockSpec((16, 512), lambda g: (0, g)),
            pl.BlockSpec((RYP, 256), lambda g: (0, 0)),
        ],
        out_specs=[
            pl.BlockSpec((RX * CH, 512), lambda g: (0, g)),
            pl.BlockSpec((256, RX * CH), lambda g: (0, 0)),
            pl.BlockSpec((1, RYP, 512), lambda g: (g, 0, 0)),
        ],
        out_shape=[
            jax.ShapeDtypeStruct((RX * CH, 4096), BF16),
            jax.ShapeDtypeStruct((256, RX * CH), BF16),
            jax.ShapeDtypeStruct((8, RYP, 512), BF16),
        ],
        scratch_shapes=[pltpu.VMEM((256, RX * CH), F32)],
        compiler_params=pltpu.CompilerParams(vmem_limit_bytes=48 << 20),
    )(state, c["bexp"], c["cy"])


def mix(xs_ref, ms_ref, core_ref, weight_refs):
    sign = jnp.where(half_mask(CH), 1.0, -1.0)
    for other, w_ref in enumerate(weight_refs):
        core = core_ref[0] if other == 0 else 1 - core_ref[0]
        groups, _, run = w_ref.shape[:3]
        for group in range(groups):
            for place in range(run):
                w = w_ref[group, 0, place].astype(F32)
                full = jnp.concatenate([w * sign, pltpu.roll(w, 64, 1)], axis=0).astype(BF16)
                mode = (group * 2 + core) * run + place
                rows = pl.ds(pl.multiple_of(mode * LINE, LINE), LINE)
                ms_ref[rows, :] = dot_nt(xs_ref[rows, :].astype(BF16), full)


def mid_x_kernel(
    core_ref, recv_ref, w0_ref, w1_ref, ax_ref, ux_ref, send_ref, r_ref, xs_ref, ms_ref, o_ref
):
    pairs = RX // 2
    first = half_mask(MODES)
    for p in range(pairs):
        part = recv_ref[:, :, p * 128 : (p + 1) * 128]
        r_ref[p] = part.reshape(256, 128).astype(F32)
    cols = []
    for y in range(LINE):
        ry = [r_ref[p, pl.ds(y, 32, stride=LINE), :] for p in range(pairs)]
        cols.append(jnp.concatenate(ry, axis=0).astype(BF16))
    spec = dot(ax_ref[...], jnp.concatenate(cols, axis=1))
    for y in range(LINE):
        s = spec[:, y * 128 : (y + 1) * 128]
        x = jnp.where(first, s[0:32], s[96:128])
        x = x + pltpu.roll(jnp.where(first, s[32:64], s[64:96]), 64, 1)
        xs_ref[pl.ds(y, MODES, stride=LINE), :] = x
    mix(xs_ref, ms_ref, core_ref, (w0_ref, w1_ref))
    cols = []
    for y in range(LINE):
        m = ms_ref[pl.ds(y, MODES, stride=LINE), :]
        cols.append(jnp.concatenate([m, pltpu.roll(m, 64, 1)], axis=0).astype(BF16))
    out = dot(ux_ref[...], jnp.concatenate(cols, axis=1))
    for y in range(LINE):
        for p in range(pairs):
            v0 = out[p * 32 : (p + 1) * 32, y * 128 : (y + 1) * 128]
            v1 = out[(pairs + p) * 32 : (pairs + p + 1) * 32, y * 128 : (y + 1) * 128]
            o_ref[p, pl.ds(y, 32, stride=LINE), :] = jnp.where(first, v0, v1)
    for p in range(pairs):
        part = o_ref[p].reshape(32, LINE, 128).astype(BF16)
        send_ref[:, :, p * 128 : (p + 1) * 128] = part


def mid_specs(recv, w, tables, layer):
    whole = lambda a: pl.BlockSpec(a.shape, lambda *_: (0,) * a.ndim)
    weights = pl.BlockSpec((w.shape[0], 1) + w.shape[2:], lambda *_: (0, layer, 0, 0, 0))
    return (
        [pl.BlockSpec(memory_space=pltpu.SMEM), whole(recv), weights, weights]
        + [whole(t) for t in tables],
        whole(recv),
    )


def mid_x(core, recv, w, c, layer):
    in_specs, out_specs = mid_specs(recv, w[0], (c["ax"], c["ux"]), layer)
    return pl.pallas_call(
        mid_x_kernel,
        name="mid_x",
        grid=(1,),
        in_specs=in_specs,
        out_specs=out_specs,
        out_shape=jax.ShapeDtypeStruct(recv.shape, BF16),
        scratch_shapes=[
            pltpu.VMEM((RX // 2, 256, 128), F32),
            pltpu.VMEM((MODES * LINE, 128), F32),
            pltpu.VMEM((MODES * LINE, 128), F32),
            pltpu.VMEM((RX // 2, 256, 128), F32),
        ],
        compiler_params=pltpu.CompilerParams(vmem_limit_bytes=48 << 20),
    )(core, recv, w[0], w[1], c["ax"], c["ux"])


def mid_y_kernel(core_ref, recv_ref, w0_ref, w1_ref, ay_ref, gy_ref, send_ref, xs_ref, ms_ref):
    first = half_mask(MODES)
    spec = dot(ay_ref[...], recv_ref[...].reshape(8 * RYP, 512))
    for b in range(LINE // 2):
        re = spec[0:32, b * 128 : (b + 1) * 128]
        im = spec[32:64, b * 128 : (b + 1) * 128]
        xs_ref[pl.ds(2 * b, MODES, stride=LINE), :] = jnp.where(first, re, pltpu.roll(im, 64, 1))
        xs_ref[pl.ds(2 * b + 1, MODES, stride=LINE), :] = jnp.where(
            first, pltpu.roll(re, 64, 1), im
        )
    mix(xs_ref, ms_ref, core_ref, (w0_ref, w1_ref))
    cols = []
    for b in range(LINE // 2):
        m0 = ms_ref[pl.ds(2 * b, MODES, stride=LINE), :]
        m1 = ms_ref[pl.ds(2 * b + 1, MODES, stride=LINE), :]
        re = jnp.where(first, m0, pltpu.roll(m1, 64, 1))
        im = jnp.where(first, pltpu.roll(m0, 64, 1), m1)
        cols.append(jnp.concatenate([re, im], axis=0).astype(BF16))
    out = dot(gy_ref[...], jnp.concatenate(cols, axis=1))
    send_ref[...] = out.reshape(8, RYP, 512).astype(BF16)


def mid_y(core, recv, w, c, layer):
    in_specs, out_specs = mid_specs(recv, w[0], (c["ay"], c["gy"]), layer)
    return pl.pallas_call(
        mid_y_kernel,
        name="mid_y",
        grid=(1,),
        in_specs=in_specs,
        out_specs=out_specs,
        out_shape=jax.ShapeDtypeStruct(recv.shape, BF16),
        scratch_shapes=[
            pltpu.VMEM((MODES * LINE, 128), F32),
            pltpu.VMEM((MODES * LINE, 128), F32),
        ],
        compiler_params=pltpu.CompilerParams(vmem_limit_bytes=48 << 20),
    )(core, recv, w[0], w[1], c["ay"], c["gy"])


def gelu(x):
    inner = x * (0.7978845608028654 + 0.035677408136300125 * (x * x))
    half = 0.5 * x
    return half + half * jnp.tanh(inner)


def last_kernel(more, *refs):
    yx_ref, kron_ref, yy_ref, cyt_ref, state_ref, we_ref, wr_ref = refs[:7]
    if more:
        cy_ref, out_ref, zx_ref, zy_ref, we4_ref, wr4_ref, acc_ref = refs[7:]
    else:
        out_ref, we4_ref, wr4_ref = refs[7:]
    g = pl.program_id(0)

    @pl.when(g == 0)
    def _():
        we4_ref[...] = jnp.zeros_like(we4_ref)
        wr4_ref[...] = jnp.zeros_like(wr4_ref)
        for j in range(4):
            we4_ref[j * CH : (j + 1) * CH, j * HID : (j + 1) * HID] = we_ref[...]
            wr4_ref[j * HID : (j + 1) * HID, j * CH : (j + 1) * CH] = wr_ref[...]

    kron = kron_ref[...]
    total = dot(yx_ref[...], kron) + dot(cyt_ref[...], yy_ref[0])
    total = total.astype(BF16)
    for j in range(2):
        part = total[:, j * 256 : (j + 1) * 256]
        hidden = gelu(dot(part, we4_ref[...])).astype(BF16)
        update = dot(hidden, wr4_ref[...])
        old = state_ref[:, j * 256 : (j + 1) * 256].astype(F32)
        out_ref[:, j * 256 : (j + 1) * 256] = (old + update).astype(BF16)
    if more:
        state = out_ref[...]
        part = dot_nt(state, kron)

        @pl.when(g == 0)
        def _():
            acc_ref[...] = part

        @pl.when(g > 0)
        def _():
            acc_ref[...] += part

        zy_ref[0] = dot(cy_ref[...], state).astype(BF16)

        @pl.when(g == pl.num_programs(0) - 1)
        def _():
            zx_ref[...] = acc_ref[...].astype(BF16)


def last_call(more, yx, kron, yy, state, we, wr, c):
    in_specs = [
        pl.BlockSpec((256, RX * CH), lambda g: (0, 0)),
        pl.BlockSpec((RX * CH, 512), lambda g: (0, g)),
        pl.BlockSpec((1, RYP, 512), lambda g: (g, 0, 0)),
        pl.BlockSpec((256, RYP), lambda g: (0, 0)),
        pl.BlockSpec((256, 512), lambda g: (0, g)),
        pl.BlockSpec((CH, HID), lambda g: (0, 0)),
        pl.BlockSpec((HID, CH), lambda g: (0, 0)),
    ]
    args = [yx, kron, yy, c["cyt"], state, we, wr]
    out_specs = [pl.BlockSpec((256, 512), lambda g: (0, g))]
    out_shape = [jax.ShapeDtypeStruct((256, 4096), BF16)]
    scratch = [pltpu.VMEM((256, 1024), BF16), pltpu.VMEM((1024, 256), BF16)]
    if more:
        in_specs.append(pl.BlockSpec((RYP, 256), lambda g: (0, 0)))
        args.append(c["cy"])
        out_specs += [
            pl.BlockSpec((256, RX * CH), lambda g: (0, 0)),
            pl.BlockSpec((1, RYP, 512), lambda g: (g, 0, 0)),
        ]
        out_shape += [
            jax.ShapeDtypeStruct((256, RX * CH), BF16),
            jax.ShapeDtypeStruct((8, RYP, 512), BF16),
        ]
        scratch.append(pltpu.VMEM((256, RX * CH), F32))
    return pl.pallas_call(
        functools.partial(last_kernel, more),
        name="last",
        grid=(8,),
        in_specs=in_specs,
        out_specs=out_specs,
        out_shape=out_shape,
        scratch_shapes=scratch,
        compiler_params=pltpu.CompilerParams(vmem_limit_bytes=48 << 20),
    )(*args)


def gather_weights(spectral_x, spectral_y):
    core = lax.rem(lax.axis_index("gx"), 2)
    swap = [(i, i ^ 1) for i in range(32)]
    same_core = [list(range(c, 32, 2)) for c in range(2)]
    own = jnp.concatenate([spectral_x[:, :, 0], spectral_x[:, :, 1]], axis=-1)
    own = jnp.broadcast_to(own[None], (16, LAYERS, 1, CH, 128))
    wx = lax.all_to_all(own, "gx", 0, 0, axis_index_groups=same_core, tiled=True)
    own = lax.dynamic_slice_in_dim(spectral_y, core * 2, 2, 1)
    own = jnp.concatenate([own[:, :, 0], own[:, :, 1]], axis=-1)
    own = jnp.broadcast_to(own[None], (8, LAYERS, 2, CH, 128))
    wy = lax.all_to_all(own, "gy", 0, 0, tiled=True)
    wx = (wx, lax.ppermute(wx, "gx", swap))
    wy = (wy, lax.ppermute(wy, "gx", swap))
    return wx, wy, core.reshape(1).astype(jnp.int32)


def body(state_field, spectral_x, spectral_y, expand_weight, reduce_weight):
    c = {name: jnp.asarray(value) for name, value in make_constants().items()}
    wx, wy, core = gather_weights(spectral_x, spectral_y)
    state = jnp.transpose(state_field[0], (2, 1, 0)).reshape(256, 4096)
    kron, zx, zy = first_call(state, c)
    for l in range(LAYERS):
        recv_x = lax.all_to_all(zx.reshape(32, LINE, RX * CH), "gx", 0, 0, tiled=True)
        recv_y = lax.all_to_all(zy, "gy", 0, 0, tiled=True)
        send_x = mid_x(core, recv_x, wx, c, l)
        send_y = mid_y(core, recv_y, wy, c, l)
        yx = lax.all_to_all(send_x, "gx", 0, 0, tiled=True).reshape(256, RX * CH)
        yy = lax.all_to_all(send_y, "gy", 0, 0, tiled=True)
        more = l + 1 < LAYERS
        got = last_call(more, yx, kron, yy, state, expand_weight[l], reduce_weight[l], c)
        state = got[0]
        if more:
            zx, zy = got[1], got[2]
    return jnp.transpose(state.reshape(256, 64, CH), (2, 1, 0))[None]


def solution(mesh):
    in_specs = (
        P(None, None, "gx", "gy"),
        P(None, "gx", None, None, None),
        P(None, "gy", None, None, None),
        P(),
        P(),
    )
    out_specs = P(None, None, "gx", "gy")
    return jax.shard_map(body, mesh=mesh, in_specs=in_specs, out_specs=out_specs, check_vma=False)
```

```python
import functools

import jax
import jax.numpy as jnp
import numpy as np
from jax import lax
from jax.experimental import pallas as pl
from jax.experimental.pallas import tpu as pltpu
from jax.sharding import PartitionSpec as P

F32 = jnp.float32
BF16 = jnp.bfloat16
NX = 2048
NY = 2048
CH = 64
HID = 256
MODES = 32
LAYERS = 2
RX = 10
RY = 20
RYP = 24
LINE = 8


def window_tables(length, devices, rank):
    window = length // devices
    k = np.arange(MODES)[:, None]
    p = np.arange(length)[None, :]
    angle = 2.0 * np.pi * ((k * p) % length) / length
    scale = 1.0 / np.sqrt(length)
    weight = np.where(np.arange(MODES) == 0, 1.0, 2.0)[:, None]
    forward = np.concatenate([np.cos(angle), -np.sin(angle)], 0) * scale
    inverse = np.concatenate([weight * np.cos(angle), -weight * np.sin(angle)], 0) * scale
    _, _, vt = np.linalg.svd(forward[:, :window], full_matrices=False)
    basis = vt[:rank]
    basis = basis * np.sign(basis[np.arange(rank), np.abs(basis).argmax(1)])[:, None]
    fwd = np.stack([forward[:, d * window : (d + 1) * window] @ basis.T for d in range(devices)])
    inv = np.stack([inverse[:, d * window : (d + 1) * window] @ basis.T for d in range(devices)])
    return basis, fwd, inv


def bf(x):
    return np.asarray(x, np.float32).astype(jnp.bfloat16)


def make_constants():
    bx, fx, ix = window_tables(NX, 32, RX)
    by, fy, iy = window_tables(NY, 8, RY)
    pairs = RX // 2
    ax = fx.reshape(32, 64, pairs, 2).transpose(3, 1, 2, 0).reshape(128, pairs * 32)
    gx = ix.reshape(32, 2, MODES, pairs, 2)
    u0 = gx[..., 0].transpose(3, 0, 1, 2).reshape(pairs * 32, 64)
    u1 = gx[..., 1].transpose(3, 0, 1, 2)[:, :, ::-1].reshape(pairs * 32, 64)
    mid_x = np.zeros((448, 256))
    mid_x[:128, : pairs * 32] = ax
    mid_x[128:, :64] = np.concatenate([u0, u1], 0)
    pad = ((0, 0), (0, 0), (0, RYP - RY))
    fy, iy = np.pad(fy, pad), np.pad(iy, pad)
    mid_y = np.zeros((8, 96, 256))
    for me in range(8):
        order = [(me - s) % 8 for s in range(8)]
        mid_y[me, :64, : 8 * RYP] = fy[order].transpose(1, 0, 2).reshape(64, 8 * RYP)
        mid_y[me, 64 : 64 + RYP, :64] = iy[me].T
    cy = np.pad(by, ((0, RYP - RY), (0, 0)))
    bexp = np.repeat(bx, CH, axis=1)
    bexp = np.pad(bexp, ((0, 16 - RX), (0, 0)))
    return dict(mid_x=bf(mid_x), mid_y=bf(mid_y), cy=bf(cy), bexp=bf(bexp))


def dot(a, b):
    return jnp.dot(a, b, preferred_element_type=F32)


def dot_nt(a, b):
    return lax.dot_general(a, b, (((1,), (1,)), ((), ())), preferred_element_type=F32)


def half_mask(rows):
    return lax.broadcasted_iota(jnp.int32, (rows, 128), 1) < 64


def dot_tn(a, b):
    return lax.dot_general(a, b, (((0,), (0,)), ((), ())), preferred_element_type=F32)


def estimate(us):
    return pl.CostEstimate(flops=int(us * 1e9), bytes_accessed=1 << 20, transcendentals=0)


def params():
    return pltpu.CompilerParams(vmem_limit_bytes=48 << 20)


def first_kernel(field_ref, bexp_ref, cy_ref, kron_ref, state_ref, zx_ref, zy_ref, t_ref, acc_ref):
    g = pl.program_id(0)
    for h in range(2):
        part = field_ref[:, :, h * 128 : (h + 1) * 128].astype(F32)
        t_ref[h] = part.reshape(512, 128)
    for h in range(2):
        for p in range(4):
            two = [t_ref[h, pl.ds(2 * p + j, CH, stride=8), :] for j in range(2)]
            block = jnp.concatenate(two, axis=0).T.astype(BF16)
            state_ref[h * 128 : (h + 1) * 128, p * 128 : (p + 1) * 128] = block
    lanes = lax.broadcasted_iota(jnp.int32, (CH, 512), 1)
    rows = lax.broadcasted_iota(jnp.int32, (CH, 512), 0)
    eye = (lanes % CH) == rows
    for r in range(RX):
        row = jnp.broadcast_to(bexp_ref[r : r + 1, :].astype(F32), (CH, 512))
        kron_ref[r * CH : (r + 1) * CH, :] = jnp.where(eye, row, 0.0).astype(BF16)
    state = state_ref[...]
    part = dot_nt(state, kron_ref[...])

    @pl.when(g == 0)
    def _():
        acc_ref[...] = part

    @pl.when(g > 0)
    def _():
        acc_ref[...] += part

    zy_ref[...] = dot(cy_ref[...], state).astype(BF16)

    @pl.when(g == pl.num_programs(0) - 1)
    def _():
        zx_ref[...] = acc_ref[...].astype(BF16)


def first_call(field, c):
    return pl.pallas_call(
        first_kernel,
        name="first",
        grid=(8,),
        in_specs=[
            pl.BlockSpec((CH, 8, 256), lambda g: (0, g, 0)),
            pl.BlockSpec((16, 512), lambda g: (0, g)),
            pl.BlockSpec((RYP, 256), lambda g: (0, 0)),
        ],
        out_specs=[
            pl.BlockSpec((RX * CH, 512), lambda g: (0, g)),
            pl.BlockSpec((256, 512), lambda g: (0, g)),
            pl.BlockSpec((256, RX * CH), lambda g: (0, 0)),
            pl.BlockSpec((RYP, 512), lambda g: (0, g)),
        ],
        out_shape=[
            jax.ShapeDtypeStruct((RX * CH, 4096), BF16),
            jax.ShapeDtypeStruct((256, 4096), BF16),
            jax.ShapeDtypeStruct((256, RX * CH), BF16),
            jax.ShapeDtypeStruct((RYP, 4096), BF16),
        ],
        scratch_shapes=[pltpu.VMEM((2, 512, 128), F32), pltpu.VMEM((256, RX * CH), F32)],
        compiler_params=params(),
        cost_estimate=estimate(10),
    )(field, c["bexp"], c["cy"])


def mode_weights(w, sign):
    w = w.astype(F32)
    return jnp.concatenate([w * sign, pltpu.roll(w, 64, 1)], axis=0).astype(BF16)


def mix(xs_ref, ms_ref, lines, weights):
    sign = jnp.where(half_mask(CH), 1.0, -1.0)
    for mode, w in weights:
        start = mode * lines
        if not isinstance(start, int):
            start = pl.multiple_of(start, lines)
        rows = pl.ds(start, lines)
        ms_ref[rows, :] = dot_nt(xs_ref[rows, :].astype(BF16), mode_weights(w, sign))


def mid_x_kernel(early, core_ref, recv_ref, w0_ref, w1_ref, tab_ref, *refs):
    send_ref, r_ref, xs_ref, ms_ref, o_ref = refs
    pairs = RX // 2
    first = half_mask(MODES)
    for p in range(pairs):
        part = recv_ref[:, :, p * 128 : (p + 1) * 128]
        r_ref[p] = part.reshape(256, 128).astype(F32)
    cols = []
    for y in range(LINE):
        ry = [r_ref[p, pl.ds(y, 32, stride=LINE), :] for p in range(pairs)]
        cols.append(jnp.concatenate(ry, axis=0).astype(BF16))
    spec = dot(tab_ref[:128, : pairs * 32], jnp.concatenate(cols, axis=1))
    for y in range(LINE):
        s = spec[:, y * 128 : (y + 1) * 128]
        x = jnp.where(first, s[0:32], s[96:128])
        x = x + pltpu.roll(jnp.where(first, s[32:64], s[64:96]), 64, 1)
        xs_ref[pl.ds(y, MODES, stride=LINE), :] = x
    if early:
        core = core_ref[0]
        weights = [(t * 2 + core, w0_ref[t]) for t in range(16)]
        weights += [(t * 2 + 1 - core, w1_ref[t]) for t in range(16)]
    else:
        weights = [(k, w0_ref[k, 0]) for k in range(MODES)]
    mix(xs_ref, ms_ref, LINE, weights)
    cols = []
    for y in range(LINE):
        m = ms_ref[pl.ds(y, MODES, stride=LINE), :]
        cols.append(jnp.concatenate([m, pltpu.roll(m, 64, 1)], axis=0).astype(BF16))
    out = dot(tab_ref[128:, :64], jnp.concatenate(cols, axis=1))
    for y in range(LINE):
        for p in range(pairs):
            v0 = out[p * 32 : (p + 1) * 32, y * 128 : (y + 1) * 128]
            v1 = out[(pairs + p) * 32 : (pairs + p + 1) * 32, y * 128 : (y + 1) * 128]
            o_ref[p, pl.ds(y, 32, stride=LINE), :] = jnp.where(first, v0, v1)
    for p in range(pairs):
        part = o_ref[p].reshape(32, LINE, 128).astype(BF16)
        send_ref[:, :, p * 128 : (p + 1) * 128] = part


def whole(a):
    return pl.BlockSpec(a.shape, lambda *_: (0,) * a.ndim)


def mid_x(early, core, recv, w0, w1, c):
    if early:
        weights = [whole(w0), whole(w1)]
    else:
        weights = [pl.BlockSpec((MODES, 1, CH, 128), lambda i: (0, 1, 0, 0)), whole(w1)]
    return pl.pallas_call(
        functools.partial(mid_x_kernel, early),
        name="mid_x",
        grid=(1,),
        in_specs=[pl.BlockSpec(memory_space=pltpu.SMEM), whole(recv)]
        + weights
        + [whole(c["mid_x"])],
        out_specs=whole(recv),
        out_shape=jax.ShapeDtypeStruct(recv.shape, BF16),
        scratch_shapes=[
            pltpu.VMEM((RX // 2, 256, 128), F32),
            pltpu.VMEM((MODES * LINE, 128), F32),
            pltpu.VMEM((MODES * LINE, 128), F32),
            pltpu.VMEM((RX // 2, 256, 128), F32),
        ],
        compiler_params=params(),
        cost_estimate=estimate(3),
    )(core, recv, w0, w1, c["mid_x"])


def mid_y_kernel(me_ref, *refs):
    z_refs = refs[:8]
    w_ref, tab_ref, out_ref, xs_ref, ms_ref = refs[8:]
    first = half_mask(MODES)
    lines = 64
    for g in range(8):
        z = [ref[:, g * 512 : (g + 1) * 512].astype(F32) for ref in z_refs]
        z = jnp.concatenate(z, axis=0).astype(BF16)
        spec = dot(tab_ref[0, :64, : 8 * RYP], z)
        for b in range(4):
            re = spec[0:32, b * 128 : (b + 1) * 128]
            im = spec[32:64, b * 128 : (b + 1) * 128]
            line = g * 8 + 2 * b
            xs_ref[pl.ds(line, MODES, stride=lines), :] = jnp.where(
                first, re, pltpu.roll(im, 64, 1)
            )
            xs_ref[pl.ds(line + 1, MODES, stride=lines), :] = jnp.where(
                first, pltpu.roll(re, 64, 1), im
            )
    weights = [(src * 4 + j, w_ref[src, 0, j]) for src in range(8) for j in range(4)]
    mix(xs_ref, ms_ref, lines, weights)
    for g in range(8):
        cols = []
        for b in range(4):
            line = g * 8 + 2 * b
            m0 = ms_ref[pl.ds(line, MODES, stride=lines), :]
            m1 = ms_ref[pl.ds(line + 1, MODES, stride=lines), :]
            re = jnp.where(first, m0, pltpu.roll(m1, 64, 1))
            im = jnp.where(first, pltpu.roll(m0, 64, 1), m1)
            cols.append(jnp.concatenate([re, im], axis=0).astype(BF16))
        out = dot(tab_ref[0, 64 : 64 + RYP, :64], jnp.concatenate(cols, axis=1))
        out_ref[g] = out.astype(BF16)


def mid_y(layer, me, zs, w, c):
    table = c["mid_y"]
    return pl.pallas_call(
        mid_y_kernel,
        name="mid_y",
        grid_spec=pltpu.PrefetchScalarGridSpec(
            num_scalar_prefetch=1,
            grid=(1,),
            in_specs=[whole(z) for z in zs]
            + [
                pl.BlockSpec((8, 1, 4, CH, 128), lambda i, me: (0, layer, 0, 0, 0)),
                pl.BlockSpec((1,) + table.shape[1:], lambda i, me: (me[0], 0, 0)),
            ],
            out_specs=pl.BlockSpec((8, RYP, 512), lambda i, me: (0, 0, 0)),
            scratch_shapes=[pltpu.VMEM((MODES * 64, 128), F32)] * 2,
        ),
        out_shape=jax.ShapeDtypeStruct((8, RYP, 512), BF16),
        compiler_params=params(),
        cost_estimate=estimate(6),
    )(me, *zs, w, table)


def gelu(x):
    x = x.astype(BF16)
    inner = x * (0.7978845608028654 + 0.035677408136300125 * (x * x))
    half = 0.5 * x
    return half + half * jnp.tanh(inner)


def last_kernel(more, *refs):
    yx_ref, kron_ref, yy_ref, cy_ref, state_ref, we_ref, wr_ref = refs[:7]
    if more:
        out_ref, zx_ref, zy_ref, we4_ref, wr4_ref, acc_ref = refs[7:]
    else:
        out_ref, we4_ref, wr4_ref, t_ref = refs[7:]
    g = pl.program_id(0)

    @pl.when(g == 0)
    def _():
        we4_ref[...] = jnp.zeros_like(we4_ref)
        wr4_ref[...] = jnp.zeros_like(wr4_ref)
        for j in range(4):
            we4_ref[j * CH : (j + 1) * CH, j * HID : (j + 1) * HID] = we_ref[0]
            wr4_ref[j * CH : (j + 1) * CH, j * HID : (j + 1) * HID] = wr_ref[0]

    kron = kron_ref[...]
    total = dot(yx_ref[...], kron) + dot_tn(cy_ref[...], yy_ref[0])
    total = total.astype(BF16)
    for j in range(2):
        part = total[:, j * 256 : (j + 1) * 256]
        hidden = gelu(dot(part, we4_ref[...])).astype(BF16)
        update = dot_nt(hidden, wr4_ref[...])
        new = state_ref[:, j * 256 : (j + 1) * 256].astype(F32) + update
        if more:
            out_ref[:, j * 256 : (j + 1) * 256] = new.astype(BF16)
            continue
        for h in range(2):
            for p in range(2):
                block = new[h * 128 : (h + 1) * 128, p * 128 : (p + 1) * 128].T
                x = j * 4 + p * 2
                t_ref[h, pl.ds(x, CH, stride=8), :] = block[:CH]
                t_ref[h, pl.ds(x + 1, CH, stride=8), :] = block[CH:]
    if more:
        state = out_ref[...]
        part = dot_nt(state, kron)

        @pl.when(g == 0)
        def _():
            acc_ref[...] = part

        @pl.when(g > 0)
        def _():
            acc_ref[...] += part

        zy_ref[...] = dot(cy_ref[...], state).astype(BF16)

        @pl.when(g == pl.num_programs(0) - 1)
        def _():
            zx_ref[...] = acc_ref[...].astype(BF16)
    else:
        for h in range(2):
            part = t_ref[h].reshape(CH, 8, 128).astype(BF16)
            out_ref[:, :, h * 128 : (h + 1) * 128] = part


def last_call(layer, more, yx, kron, yy, state, we, wr, c):
    in_specs = [
        pl.BlockSpec((256, RX * CH), lambda g: (0, 0)),
        pl.BlockSpec((RX * CH, 512), lambda g: (0, g)),
        pl.BlockSpec((1, RYP, 512), lambda g: (g, 0, 0)),
        pl.BlockSpec((RYP, 256), lambda g: (0, 0)),
        pl.BlockSpec((256, 512), lambda g: (0, g)),
        pl.BlockSpec((1, CH, HID), lambda g: (layer, 0, 0)),
        pl.BlockSpec((1, CH, HID), lambda g: (layer, 0, 0)),
    ]
    scratch = [pltpu.VMEM((256, 1024), BF16)] * 2
    if more:
        out_specs = [
            pl.BlockSpec((256, 512), lambda g: (0, g)),
            pl.BlockSpec((256, RX * CH), lambda g: (0, 0)),
            pl.BlockSpec((RYP, 512), lambda g: (0, g)),
        ]
        out_shape = [
            jax.ShapeDtypeStruct((256, 4096), BF16),
            jax.ShapeDtypeStruct((256, RX * CH), BF16),
            jax.ShapeDtypeStruct((RYP, 4096), BF16),
        ]
        scratch.append(pltpu.VMEM((256, RX * CH), F32))
    else:
        out_specs = [pl.BlockSpec((CH, 8, 256), lambda g: (0, g, 0))]
        out_shape = [jax.ShapeDtypeStruct((CH, 64, 256), BF16)]
        scratch.append(pltpu.VMEM((2, 512, 128), F32))
    return pl.pallas_call(
        functools.partial(last_kernel, more),
        name="last",
        grid=(8,),
        in_specs=in_specs,
        out_specs=out_specs,
        out_shape=out_shape,
        scratch_shapes=scratch,
        compiler_params=params(),
        cost_estimate=estimate(12),
    )(yx, kron, yy, c["cy"], state, we, wr)


def join(w):
    return jnp.concatenate([w[..., 0, :, :], w[..., 1, :, :]], axis=-1)


def body(state_field, spectral_x, spectral_y, expand_weight, reduce_weight):
    c = {name: jnp.asarray(value) for name, value in make_constants().items()}
    core = lax.rem(lax.axis_index("gx"), 2).reshape(1).astype(jnp.int32)
    me = lax.axis_index("gy").reshape(1).astype(jnp.int32)
    own_x = join(spectral_x)[:, 0]
    same_core = [list(range(s, 32, 2)) for s in range(2)]
    early = jnp.broadcast_to(own_x[0][None], (16, CH, 128))
    early = lax.all_to_all(early, "gx", 0, 0, axis_index_groups=same_core, tiled=True)
    swapped = lax.ppermute(early, "gx", [(i, i ^ 1) for i in range(32)])
    wy = lax.all_gather(join(spectral_y), "gy", axis=0)
    wx = lax.all_gather(own_x, "gx", axis=0)
    wr = jnp.swapaxes(reduce_weight, 1, 2)
    kron, state, zx, zy = first_call(state_field[0], c)
    for l in range(LAYERS):
        zs = [zy]
        for s in range(1, 8):
            zs.append(lax.ppermute(zy, "gy", [(i, (i + s) % 8) for i in range(8)]))
        recv = lax.all_to_all(zx.reshape(32, LINE, RX * CH), "gx", 0, 0, tiled=True)
        if l == 0:
            send = mid_x(True, core, recv, early, swapped, c)
        else:
            send = mid_x(False, core, recv, wx, core, c)
        yy = mid_y(l, me, zs, wy, c)
        yx = lax.all_to_all(send, "gx", 0, 0, tiled=True).reshape(256, RX * CH)
        more = l + 1 < LAYERS
        got = last_call(l, more, yx, kron, yy, state, expand_weight, wr, c)
        if more:
            state, zx, zy = got
    return got[0][None]


def solution(mesh):
    in_specs = (
        P(None, None, "gx", "gy"),
        P(None, "gx", None, None, None),
        P(None, "gy", None, None, None),
        P(),
        P(),
    )
    out_specs = P(None, None, "gx", "gy")
    return jax.shard_map(body, mesh=mesh, in_specs=in_specs, out_specs=out_specs, check_vma=False)
```

```python
import functools

import jax
import jax.numpy as jnp
import numpy as np
from jax import lax
from jax.experimental import pallas as pl
from jax.experimental.pallas import tpu as pltpu
from jax.sharding import PartitionSpec as P

F32 = jnp.float32
BF16 = jnp.bfloat16
NX = 2048
NY = 2048
CH = 64
HID = 256
MODES = 32
LAYERS = 2
RX = 10
RY = 20
RYP = 24
GROUP = 64
WIDE = GROUP * CH
LINE = 8


def window_tables(length, devices, rank):
    window = length // devices
    k = np.arange(MODES)[:, None]
    p = np.arange(length)[None, :]
    angle = 2.0 * np.pi * ((k * p) % length) / length
    scale = 1.0 / np.sqrt(length)
    weight = np.where(np.arange(MODES) == 0, 1.0, 2.0)[:, None]
    forward = np.concatenate([np.cos(angle), -np.sin(angle)], 0) * scale
    inverse = np.concatenate([weight * np.cos(angle), -weight * np.sin(angle)], 0) * scale
    _, _, vt = np.linalg.svd(forward[:, :window], full_matrices=False)
    basis = vt[:rank]
    basis = basis * np.sign(basis[np.arange(rank), np.abs(basis).argmax(1)])[:, None]
    fwd = np.stack([forward[:, d * window : (d + 1) * window] @ basis.T for d in range(devices)])
    inv = np.stack([inverse[:, d * window : (d + 1) * window] @ basis.T for d in range(devices)])
    return basis, fwd, inv


SHIFTS = ((1, 0), (0, 1), (0, 3), (1, 2), (0, 2), (1, 1), (1, 3))


def moved(me, flip, step):
    return (me // 4 ^ flip) * 4 + (me + step) % 4


def bf(x):
    return np.asarray(x, np.float32).astype(jnp.bfloat16)


def make_constants():
    bx, fx, ix = window_tables(NX, 32, RX)
    by, fy, iy = window_tables(NY, 8, RY)
    pairs = RX // 2
    ax = fx.reshape(32, 64, pairs, 2).transpose(3, 1, 2, 0).reshape(128, pairs * 32)
    gx = ix.reshape(32, 2, MODES, pairs, 2)
    u0 = gx[..., 0].transpose(3, 0, 1, 2).reshape(pairs * 32, 64)
    u1 = gx[..., 1].transpose(3, 0, 1, 2)[:, :, ::-1].reshape(pairs * 32, 64)
    mid_x = np.zeros((448, 256))
    mid_x[:128, : pairs * 32] = ax
    mid_x[128:, :64] = np.concatenate([u0, u1], 0)
    pad = ((0, 0), (0, 0), (0, RYP - RY))
    fy, iy = np.pad(fy, pad), np.pad(iy, pad)
    mid_y = np.zeros((8, 96, 256))
    for me in range(8):
        order = [moved(me, flip, -step) for flip, step in ((0, 0),) + SHIFTS]
        mid_y[me, :64, : 8 * RYP] = fy[order].transpose(1, 0, 2).reshape(64, 8 * RYP)
        mid_y[me, 64 : 64 + RYP, :64] = iy[me].T
    cy = np.pad(by, ((0, RYP - RY), (0, 0)))
    bexp = np.repeat(bx, CH, axis=1)
    bexp = np.pad(bexp, ((0, 16 - RX), (0, 0)))
    return dict(mid_x=bf(mid_x), mid_y=bf(mid_y), cy=bf(cy), bexp=bf(bexp))


def dot(a, b):
    return jnp.dot(a, b, preferred_element_type=F32)


def dot_nt(a, b):
    return lax.dot_general(a, b, (((1,), (1,)), ((), ())), preferred_element_type=F32)


def half_mask(rows):
    return lax.broadcasted_iota(jnp.int32, (rows, 128), 1) < 64


def dot_tn(a, b):
    return lax.dot_general(a, b, (((0,), (0,)), ((), ())), preferred_element_type=F32)


def estimate(us):
    return pl.CostEstimate(flops=int(us * 1e9), bytes_accessed=1 << 20, transcendentals=0)


def params(mib):
    return pltpu.CompilerParams(vmem_limit_bytes=mib << 20)


def fill_kron(bexp_ref, kron_ref):
    lanes = lax.broadcasted_iota(jnp.int32, (CH, WIDE), 1)
    rows = lax.broadcasted_iota(jnp.int32, (CH, WIDE), 0)
    eye = (lanes % CH) == rows
    for r in range(RX):
        row = jnp.broadcast_to(bexp_ref[r : r + 1, :].astype(F32), (CH, WIDE))
        kron_ref[r * CH : (r + 1) * CH, :] = jnp.where(eye, row, 0.0).astype(BF16)


def coefficients(g, state, kron_ref, cy_ref, acc_ref, zx_ref, zy_ref):
    part = dot_nt(state, kron_ref[...])

    @pl.when(g == 0)
    def _():
        acc_ref[...] = part

    @pl.when(g > 0)
    def _():
        acc_ref[...] += part

    zy_ref[...] = dot(cy_ref[...], state).astype(BF16)

    @pl.when(g == pl.num_programs(0) - 1)
    def _():
        zx_ref[...] = acc_ref[...].astype(BF16)


def first_kernel(field_ref, bexp_ref, cy_ref, state_ref, zx_ref, zy_ref, t_ref, kron_ref, acc_ref):
    for h in range(2):
        part = field_ref[:, :, h * 128 : (h + 1) * 128].astype(F32)
        t_ref[h] = part.reshape(CH * GROUP, 128)
    for h in range(2):
        for p in range(GROUP // 2):
            two = [t_ref[h, pl.ds(2 * p + j, CH, stride=GROUP), :] for j in range(2)]
            block = jnp.concatenate(two, axis=0).T.astype(BF16)
            state_ref[h * 128 : (h + 1) * 128, p * 128 : (p + 1) * 128] = block
    fill_kron(bexp_ref, kron_ref)
    coefficients(pl.program_id(0), state_ref[...], kron_ref, cy_ref, acc_ref, zx_ref, zy_ref)


def first_call(field, c):
    return pl.pallas_call(
        first_kernel,
        name="first",
        grid=(64 // GROUP,),
        in_specs=[
            pl.BlockSpec((CH, GROUP, 256), lambda g: (0, g, 0)),
            pl.BlockSpec((16, WIDE), lambda g: (0, g)),
            pl.BlockSpec((RYP, 256), lambda g: (0, 0)),
        ],
        out_specs=[
            pl.BlockSpec((256, WIDE), lambda g: (0, g)),
            pl.BlockSpec((256, RX * CH), lambda g: (0, 0)),
            pl.BlockSpec((RYP, WIDE), lambda g: (0, g)),
        ],
        out_shape=[
            jax.ShapeDtypeStruct((256, 4096), BF16),
            jax.ShapeDtypeStruct((256, RX * CH), BF16),
            jax.ShapeDtypeStruct((RYP, 4096), BF16),
        ],
        scratch_shapes=[
            pltpu.VMEM((2, CH * GROUP, 128), F32),
            pltpu.VMEM((RX * CH, WIDE), BF16),
            pltpu.VMEM((256, RX * CH), F32),
        ],
        compiler_params=params(36),
        cost_estimate=estimate(10),
    )(field, c["bexp"], c["cy"])


def mode_weights(w, sign):
    w = w.astype(F32)
    return jnp.concatenate([w * sign, pltpu.roll(w, 64, 1)], axis=0).astype(BF16)


def mix(xs_ref, ms_ref, lines, weights):
    sign = jnp.where(half_mask(CH), 1.0, -1.0)
    for mode, w in weights:
        start = mode * lines
        if not isinstance(start, int):
            start = pl.multiple_of(start, lines)
        rows = pl.ds(start, lines)
        ms_ref[rows, :] = dot_nt(xs_ref[rows, :].astype(BF16), mode_weights(w, sign))


def mid_x_kernel(core_ref, recv_ref, w0_ref, w1_ref, tab_ref, *refs):
    send_ref, r_ref, xs_ref, ms_ref, o_ref = refs
    pairs = RX // 2
    first = half_mask(MODES)
    for p in range(pairs):
        part = recv_ref[:, :, p * 128 : (p + 1) * 128]
        r_ref[p] = part.reshape(256, 128).astype(F32)
    cols = []
    for y in range(LINE):
        ry = [r_ref[p, pl.ds(y, 32, stride=LINE), :] for p in range(pairs)]
        cols.append(jnp.concatenate(ry, axis=0).astype(BF16))
    spec = dot(tab_ref[:128, : pairs * 32], jnp.concatenate(cols, axis=1))
    for y in range(LINE):
        s = spec[:, y * 128 : (y + 1) * 128]
        x = jnp.where(first, s[0:32], s[96:128])
        x = x + pltpu.roll(jnp.where(first, s[32:64], s[64:96]), 64, 1)
        xs_ref[pl.ds(y, MODES, stride=LINE), :] = x
    core = core_ref[0]
    weights = [(t * 2 + core, w0_ref[t]) for t in range(16)]
    weights += [(t * 2 + 1 - core, w1_ref[t]) for t in range(16)]
    mix(xs_ref, ms_ref, LINE, weights)
    cols = []
    for y in range(LINE):
        m = ms_ref[pl.ds(y, MODES, stride=LINE), :]
        cols.append(jnp.concatenate([m, pltpu.roll(m, 64, 1)], axis=0).astype(BF16))
    out = dot(tab_ref[128:, :64], jnp.concatenate(cols, axis=1))
    for y in range(LINE):
        for p in range(pairs):
            v0 = out[p * 32 : (p + 1) * 32, y * 128 : (y + 1) * 128]
            v1 = out[(pairs + p) * 32 : (pairs + p + 1) * 32, y * 128 : (y + 1) * 128]
            o_ref[p, pl.ds(y, 32, stride=LINE), :] = jnp.where(first, v0, v1)
    for p in range(pairs):
        part = o_ref[p].reshape(32, LINE, 128).astype(BF16)
        send_ref[:, :, p * 128 : (p + 1) * 128] = part


def whole(a):
    return pl.BlockSpec(a.shape, lambda *_: (0,) * a.ndim)


def mid_x(core, recv, w0, w1, c):
    return pl.pallas_call(
        mid_x_kernel,
        name="mid_x",
        grid=(1,),
        in_specs=[pl.BlockSpec(memory_space=pltpu.SMEM)]
        + [whole(a) for a in (recv, w0, w1, c["mid_x"])],
        out_specs=whole(recv),
        out_shape=jax.ShapeDtypeStruct(recv.shape, BF16),
        scratch_shapes=[
            pltpu.VMEM((RX // 2, 256, 128), F32),
            pltpu.VMEM((MODES * LINE, 128), F32),
            pltpu.VMEM((MODES * LINE, 128), F32),
            pltpu.VMEM((RX // 2, 256, 128), F32),
        ],
        compiler_params=params(16),
        cost_estimate=estimate(3),
    )(core, recv, w0, w1, c["mid_x"])


def mid_y_kernel(me_ref, *refs):
    z_refs = refs[:8]
    w_ref, tab_ref, out_ref, xs_ref, ms_ref = refs[8:]
    first = half_mask(MODES)
    lines = 64
    for g in range(8):
        z = [ref[:, g * 512 : (g + 1) * 512].astype(F32) for ref in z_refs]
        z = jnp.concatenate(z, axis=0).astype(BF16)
        spec = dot(tab_ref[0, :64, : 8 * RYP], z)
        for b in range(4):
            re = spec[0:32, b * 128 : (b + 1) * 128]
            im = spec[32:64, b * 128 : (b + 1) * 128]
            line = g * 8 + 2 * b
            xs_ref[pl.ds(line, MODES, stride=lines), :] = jnp.where(
                first, re, pltpu.roll(im, 64, 1)
            )
            xs_ref[pl.ds(line + 1, MODES, stride=lines), :] = jnp.where(
                first, pltpu.roll(re, 64, 1), im
            )
    weights = [(src * 4 + j, w_ref[src, 0, j]) for src in range(8) for j in range(4)]
    mix(xs_ref, ms_ref, lines, weights)
    for g in range(8):
        cols = []
        for b in range(4):
            line = g * 8 + 2 * b
            m0 = ms_ref[pl.ds(line, MODES, stride=lines), :]
            m1 = ms_ref[pl.ds(line + 1, MODES, stride=lines), :]
            re = jnp.where(first, m0, pltpu.roll(m1, 64, 1))
            im = jnp.where(first, pltpu.roll(m0, 64, 1), m1)
            cols.append(jnp.concatenate([re, im], axis=0).astype(BF16))
        out = dot(tab_ref[0, 64 : 64 + RYP, :64], jnp.concatenate(cols, axis=1))
        out_ref[:, g * 512 : (g + 1) * 512] = out.astype(BF16)


def mid_y(layer, me, zs, w, c):
    table = c["mid_y"]
    return pl.pallas_call(
        mid_y_kernel,
        name="mid_y",
        grid_spec=pltpu.PrefetchScalarGridSpec(
            num_scalar_prefetch=1,
            grid=(1,),
            in_specs=[whole(z) for z in zs]
            + [
                pl.BlockSpec((8, 1, 4, CH, 128), lambda i, me: (0, layer, 0, 0, 0)),
                pl.BlockSpec((1,) + table.shape[1:], lambda i, me: (me[0], 0, 0)),
            ],
            out_specs=pl.BlockSpec((RYP, 4096), lambda i, me: (0, 0)),
            scratch_shapes=[pltpu.VMEM((MODES * 64, 128), F32)] * 2,
        ),
        out_shape=jax.ShapeDtypeStruct((RYP, 4096), BF16),
        compiler_params=params(20),
        cost_estimate=estimate(6),
    )(me, *zs, w, table)


def gelu(x):
    x = x.astype(BF16)
    inner = x * (0.7978845608028654 + 0.035677408136300125 * (x * x))
    half = 0.5 * x
    return half + half * jnp.tanh(inner)


def last_kernel(more, *refs):
    yx_ref, bexp_ref, yy_ref, cy_ref, state_ref, we_ref, wr_ref = refs[:7]
    if more:
        out_ref, zx_ref, zy_ref, kron_ref, we4_ref, wr4_ref, acc_ref = refs[7:]
    else:
        out_ref, kron_ref, we4_ref, wr4_ref, t_ref = refs[7:]
    g = pl.program_id(0)

    @pl.when(g == 0)
    def _():
        we4_ref[...] = jnp.zeros_like(we4_ref)
        wr4_ref[...] = jnp.zeros_like(wr4_ref)
        for j in range(4):
            we4_ref[j * CH : (j + 1) * CH, j * HID : (j + 1) * HID] = we_ref[0]
            wr4_ref[j * CH : (j + 1) * CH, j * HID : (j + 1) * HID] = wr_ref[0]

    fill_kron(bexp_ref, kron_ref)
    basis = cy_ref[...].astype(F32).T.astype(BF16)
    for j in range(WIDE // 256):
        lanes = slice(j * 256, (j + 1) * 256)
        if j % 2 == 0:
            both = slice(j * 256, (j + 2) * 256)
            total = dot(yx_ref[...], kron_ref[:, both]) + dot(basis, yy_ref[:, both])
            total = total.astype(BF16)
            total = jnp.concatenate([total[:, :256], total[:, 256:]], axis=0)
            hidden = gelu(dot(total, we4_ref[...])).astype(BF16)
            updates = dot_nt(hidden, wr4_ref[...])
        update = updates[(j % 2) * 256 : (j % 2 + 1) * 256]
        new = state_ref[:, lanes].astype(F32) + update
        if more:
            out_ref[:, lanes] = new.astype(BF16)
            continue
        for h in range(2):
            for p in range(2):
                block = new[h * 128 : (h + 1) * 128, p * 128 : (p + 1) * 128].T
                x = j * 4 + p * 2
                t_ref[h, pl.ds(x, CH, stride=GROUP), :] = block[:CH]
                t_ref[h, pl.ds(x + 1, CH, stride=GROUP), :] = block[CH:]
    if more:
        coefficients(g, out_ref[...], kron_ref, cy_ref, acc_ref, zx_ref, zy_ref)
    else:
        for h in range(2):
            part = t_ref[h].reshape(CH, GROUP, 128).astype(BF16)
            out_ref[:, :, h * 128 : (h + 1) * 128] = part


def last_call(layer, more, yx, yy, state, we, wr, c):
    in_specs = [
        pl.BlockSpec((256, RX * CH), lambda g: (0, 0)),
        pl.BlockSpec((16, WIDE), lambda g: (0, g)),
        pl.BlockSpec((RYP, WIDE), lambda g: (0, g)),
        pl.BlockSpec((RYP, 256), lambda g: (0, 0)),
        pl.BlockSpec((256, WIDE), lambda g: (0, g)),
        pl.BlockSpec((1, CH, HID), lambda g: (layer, 0, 0)),
        pl.BlockSpec((1, CH, HID), lambda g: (layer, 0, 0)),
    ]
    scratch = [pltpu.VMEM((RX * CH, WIDE), BF16)] + [pltpu.VMEM((256, 1024), BF16)] * 2
    if more:
        out_specs = [
            pl.BlockSpec((256, WIDE), lambda g: (0, g)),
            pl.BlockSpec((256, RX * CH), lambda g: (0, 0)),
            pl.BlockSpec((RYP, WIDE), lambda g: (0, g)),
        ]
        out_shape = [
            jax.ShapeDtypeStruct((256, 4096), BF16),
            jax.ShapeDtypeStruct((256, RX * CH), BF16),
            jax.ShapeDtypeStruct((RYP, 4096), BF16),
        ]
        scratch.append(pltpu.VMEM((256, RX * CH), F32))
    else:
        out_specs = [pl.BlockSpec((CH, GROUP, 256), lambda g: (0, g, 0))]
        out_shape = [jax.ShapeDtypeStruct((CH, 64, 256), BF16)]
        scratch.append(pltpu.VMEM((2, CH * GROUP, 128), F32))
    return pl.pallas_call(
        functools.partial(last_kernel, more),
        name="last",
        grid=(64 // GROUP,),
        in_specs=in_specs,
        out_specs=out_specs,
        out_shape=out_shape,
        scratch_shapes=scratch,
        compiler_params=params(40),
        cost_estimate=estimate(12),
    )(yx, c["bexp"], yy, c["cy"], state, we, wr)


def join(w):
    return jnp.concatenate([w[..., 0, :, :], w[..., 1, :, :]], axis=-1)


def exchange_weights(own):
    same_core = [list(range(s, 32, 2)) for s in range(2)]
    mine = jnp.broadcast_to(own[None], (16, CH, 128))
    mine = lax.all_to_all(mine, "gx", 0, 0, axis_index_groups=same_core, tiled=True)
    return mine, lax.ppermute(mine, "gx", [(i, i ^ 1) for i in range(32)])


def send_y(zy, shifts):
    pairs = [[(i, moved(i, flip, step)) for i in range(8)] for flip, step in shifts]
    return [lax.ppermute(zy, "gy", p) for p in pairs]


def body(state_field, spectral_x, spectral_y, expand_weight, reduce_weight):
    c = {name: jnp.asarray(value) for name, value in make_constants().items()}
    core = lax.rem(lax.axis_index("gx"), 2).reshape(1).astype(jnp.int32)
    me = lax.axis_index("gy").reshape(1).astype(jnp.int32)
    own_x = join(spectral_x)[:, 0]
    wx = exchange_weights(own_x[0])
    wy = lax.all_gather(join(spectral_y), "gy", axis=0)
    wr = jnp.swapaxes(reduce_weight, 1, 2)
    state, zx, zy = first_call(state_field[0], c)
    for l in range(LAYERS):
        early = send_y(zy, SHIFTS[:4])
        recv = lax.all_to_all(zx.reshape(32, LINE, RX * CH), "gx", 0, 0, tiled=True)
        early, recv = lax.optimization_barrier((early, recv))
        send = mid_x(core, recv, wx[0], wx[1], c)
        zy, send = lax.optimization_barrier((zy, send))
        zs = [zy] + early + send_y(zy, SHIFTS[4:])
        yx = lax.all_to_all(send, "gx", 0, 0, tiled=True)
        yy = mid_y(l, me, zs, wy, c)
        more = l + 1 < LAYERS
        if more:
            own, yx = lax.optimization_barrier((own_x[l + 1], yx))
            wx = exchange_weights(own)
        yx = yx.reshape(256, RX * CH)
        got = last_call(l, more, yx, yy, state, expand_weight, wr, c)
        if more:
            state, zx, zy = got
    return got[0][None]


def solution(mesh):
    in_specs = (
        P(None, None, "gx", "gy"),
        P(None, "gx", None, None, None),
        P(None, "gy", None, None, None),
        P(),
        P(),
    )
    out_specs = P(None, None, "gx", "gy")
    return jax.shard_map(body, mesh=mesh, in_specs=in_specs, out_specs=out_specs, check_vma=False)
```

```python
import functools

import jax
import jax.numpy as jnp
import numpy as np
from jax import lax
from jax.experimental import pallas as pl
from jax.experimental.pallas import tpu as pltpu
from jax.sharding import PartitionSpec as P

F32 = jnp.float32
BF16 = jnp.bfloat16
NX = 2048
NY = 2048
CH = 64
HID = 256
MODES = 32
LAYERS = 2
RX = 10
RY = 20
RYP = 24
GROUP = 16
WIDE = GROUP * CH
LINE = 8


def window_tables(length, devices, rank):
    window = length // devices
    k = np.arange(MODES)[:, None]
    p = np.arange(length)[None, :]
    angle = 2.0 * np.pi * ((k * p) % length) / length
    scale = 1.0 / np.sqrt(length)
    weight = np.where(np.arange(MODES) == 0, 1.0, 2.0)[:, None]
    forward = np.concatenate([np.cos(angle), -np.sin(angle)], 0) * scale
    inverse = np.concatenate([weight * np.cos(angle), -weight * np.sin(angle)], 0) * scale
    _, _, vt = np.linalg.svd(forward[:, :window], full_matrices=False)
    basis = vt[:rank]
    basis = basis * np.sign(basis[np.arange(rank), np.abs(basis).argmax(1)])[:, None]
    fwd = np.stack([forward[:, d * window : (d + 1) * window] @ basis.T for d in range(devices)])
    inv = np.stack([inverse[:, d * window : (d + 1) * window] @ basis.T for d in range(devices)])
    return basis, fwd, inv


SHIFTS = ((1, 0), (0, 1), (0, 3), (1, 2), (0, 2), (1, 1), (1, 3))
UNROLL = 4
QUARTER = 16 * 64


def moved(me, flip, step):
    return (me // 4 ^ flip) * 4 + (me + step) % 4


def bf(x):
    return np.asarray(x, np.float32).astype(jnp.bfloat16)


def make_constants():
    bx, fx, ix = window_tables(NX, 32, RX)
    by, fy, iy = window_tables(NY, 8, RY)
    pairs = RX // 2
    ax = fx.reshape(32, 64, pairs, 2).transpose(3, 1, 2, 0).reshape(128, pairs * 32)
    gx = ix.reshape(32, 2, MODES, pairs, 2)
    u0 = gx[..., 0].transpose(3, 0, 1, 2).reshape(pairs * 32, 64)
    u1 = gx[..., 1].transpose(3, 0, 1, 2)[:, :, ::-1].reshape(pairs * 32, 64)
    mid_x = np.zeros((128 + pairs * 32, 256))
    mid_x[:128, : pairs * 32] = ax
    mid_x[128:, :64] = u0
    mid_x[128:, 64:128] = u1
    mid_y = np.zeros((2, 8, RYP, 128))
    mid_y[0, :, :RY, :64] = fy.transpose(0, 2, 1)
    mid_y[1, :, :RY, :64] = iy.transpose(0, 2, 1)
    cy = np.pad(by, ((0, RYP - RY), (0, 0)))
    bx = np.pad(bx, ((0, 16 - RX), (0, 128 - 64)))
    return dict(mid_x=bf(mid_x), mid_y=bf(mid_y), cy=bf(cy), bx=bf(bx))


def dot(a, b):
    return jnp.dot(a, b, preferred_element_type=F32)


def dot_nt(a, b):
    return lax.dot_general(a, b, (((1,), (1,)), ((), ())), preferred_element_type=F32)


def half_mask(rows):
    return lax.broadcasted_iota(jnp.int32, (rows, 128), 1) < 64


def dot_tn(a, b):
    return lax.dot_general(a, b, (((0,), (0,)), ((), ())), preferred_element_type=F32)


def estimate(us):
    return pl.CostEstimate(flops=int(us * 1e9), bytes_accessed=1 << 20, transcendentals=0)


def params(mib):
    return pltpu.CompilerParams(vmem_limit_bytes=mib << 20)


def fill_kron(bx_ref, kron_ref):
    lanes = lax.broadcasted_iota(jnp.int32, (CH, WIDE), 1)
    rows = lax.broadcasted_iota(jnp.int32, (CH, WIDE), 0)
    eye = (lanes % CH) == rows
    x = lax.broadcasted_iota(jnp.int32, (128, WIDE), 1) // CH + GROUP * pl.program_id(0)
    position = lax.broadcasted_iota(jnp.int32, (128, WIDE), 0)
    spread = dot(bx_ref[...], jnp.where(x == position, 1.0, 0.0).astype(BF16))
    for r in range(RX):
        row = jnp.broadcast_to(spread[r : r + 1, :], (CH, WIDE))
        kron_ref[r * CH : (r + 1) * CH, :] = jnp.where(eye, row, 0.0).astype(BF16)


def coefficients(g, state, kron_ref, cy_ref, acc_ref, zx_ref, zy_ref):
    part = dot_nt(state, kron_ref[...])

    @pl.when(g == 0)
    def _():
        acc_ref[...] = part

    @pl.when(g > 0)
    def _():
        acc_ref[...] += part

    zy_ref[0] = dot(cy_ref[...], state).astype(BF16)

    @pl.when(g == pl.num_programs(0) - 1)
    def _():
        zx_ref[...] = acc_ref[...].astype(BF16)


def first_kernel(field_ref, bx_ref, cy_ref, state_ref, zx_ref, zy_ref, t_ref, kron_ref, acc_ref):
    for h in range(2):
        part = field_ref[:, :, h * 128 : (h + 1) * 128].astype(F32)
        t_ref[h] = part.reshape(CH * GROUP, 128)
    for h in range(2):
        for p in range(GROUP // 2):
            two = [t_ref[h, pl.ds(2 * p + j, CH, stride=GROUP), :] for j in range(2)]
            block = jnp.concatenate(two, axis=0).T.astype(BF16)
            state_ref[h * 128 : (h + 1) * 128, p * 128 : (p + 1) * 128] = block
    fill_kron(bx_ref, kron_ref)
    coefficients(pl.program_id(0), state_ref[...], kron_ref, cy_ref, acc_ref, zx_ref, zy_ref)


def first_call(field, c):
    return pl.pallas_call(
        first_kernel,
        name="first",
        grid=(64 // GROUP,),
        in_specs=[
            pl.BlockSpec((CH, GROUP, 256), lambda g: (0, g, 0)),
            pl.BlockSpec((16, 128), lambda g: (0, 0)),
            pl.BlockSpec((RYP, 256), lambda g: (0, 0)),
        ],
        out_specs=[
            pl.BlockSpec((256, WIDE), lambda g: (0, g)),
            pl.BlockSpec((256, RX * CH), lambda g: (0, 0)),
            pl.BlockSpec((1, RYP, WIDE), lambda g: (g, 0, 0)),
        ],
        out_shape=[
            jax.ShapeDtypeStruct((256, 4096), BF16),
            jax.ShapeDtypeStruct((256, RX * CH), BF16),
            jax.ShapeDtypeStruct((4, RYP, QUARTER), BF16),
        ],
        scratch_shapes=[
            pltpu.VMEM((2, CH * GROUP, 128), F32),
            pltpu.VMEM((RX * CH, WIDE), BF16),
            pltpu.VMEM((256, RX * CH), F32),
        ],
        compiler_params=params(36),
        cost_estimate=estimate(10),
    )(field, c["bx"], c["cy"])


def mode_weights(w, sign):
    w = w.astype(F32)
    return jnp.concatenate([w * sign, pltpu.roll(w, 64, 1)], axis=0).astype(BF16)


def mix(xs_ref, ms_ref, lines, steps, weights):
    sign = jnp.where(half_mask(CH), 1.0, -1.0)

    def product(i, _):
        for mode, w in weights(i):
            rows = pl.ds(pl.multiple_of(mode * lines, lines), lines)
            ms_ref[rows, :] = dot_nt(xs_ref[rows, :].astype(BF16), mode_weights(w, sign))

    lax.fori_loop(0, steps, product, None, unroll=UNROLL)


def mid_x_kernel(core_ref, recv_ref, w0_ref, w1_ref, tab_ref, *refs):
    send_ref, r_ref, xs_ref, ms_ref, o_ref = refs
    pairs = RX // 2
    first = half_mask(MODES)
    for p in range(pairs):
        part = recv_ref[:, :, p * 128 : (p + 1) * 128]
        r_ref[p] = part.reshape(256, 128).astype(F32)
    cols = []
    for y in range(LINE):
        ry = [r_ref[p, pl.ds(y, 32, stride=LINE), :] for p in range(pairs)]
        cols.append(jnp.concatenate(ry, axis=0).astype(BF16))
    spec = dot(tab_ref[:128, : pairs * 32], jnp.concatenate(cols, axis=1))
    for y in range(LINE):
        s = spec[:, y * 128 : (y + 1) * 128]
        x = jnp.where(first, s[0:32], s[96:128])
        x = x + pltpu.roll(jnp.where(first, s[32:64], s[64:96]), 64, 1)
        xs_ref[pl.ds(y, MODES, stride=LINE), :] = x
    core = core_ref[0]
    weights = lambda t: [(t * 2 + core, w0_ref[t, 0]), (t * 2 + 1 - core, w1_ref[t, 0])]
    mix(xs_ref, ms_ref, LINE, 16, weights)
    cols = []
    for y in range(LINE):
        m = ms_ref[pl.ds(y, MODES, stride=LINE), :]
        cols.append(jnp.concatenate([m, pltpu.roll(m, 64, 1)], axis=0).astype(BF16))
    cols = jnp.concatenate(cols, axis=1)
    out0 = dot(tab_ref[128:, :64], cols)
    out1 = dot(tab_ref[128:, 64:128], cols)
    for y in range(LINE):
        for p in range(pairs):
            v0 = out0[p * 32 : (p + 1) * 32, y * 128 : (y + 1) * 128]
            v1 = out1[p * 32 : (p + 1) * 32, y * 128 : (y + 1) * 128]
            o_ref[p, pl.ds(y, 32, stride=LINE), :] = jnp.where(first, v0, v1)
    for p in range(pairs):
        part = o_ref[p].reshape(32, LINE, 128).astype(BF16)
        send_ref[:, :, p * 128 : (p + 1) * 128] = part


def whole(a):
    return pl.BlockSpec(a.shape, lambda *_: (0,) * a.ndim)


def mid_x(layer, core, recv, w0, w1, c):
    weights = pl.BlockSpec((16, 1, CH, 128), lambda i: (0, layer, 0, 0))
    return pl.pallas_call(
        mid_x_kernel,
        name="mid_x",
        grid=(1,),
        in_specs=[pl.BlockSpec(memory_space=pltpu.SMEM)]
        + [whole(recv), weights, weights, whole(c["mid_x"])],
        out_specs=whole(recv),
        out_shape=jax.ShapeDtypeStruct(recv.shape, BF16),
        scratch_shapes=[
            pltpu.VMEM((RX // 2, 256, 128), F32),
            pltpu.VMEM((MODES * LINE, 128), F32),
            pltpu.VMEM((MODES * LINE, 128), F32),
            pltpu.VMEM((RX // 2, 256, 128), F32),
        ],
        compiler_params=params(16),
        cost_estimate=estimate(3),
    )(core, recv, w0, w1, c["mid_x"])


def mid_y_kernel(me_ref, *refs):
    z_refs = refs[:8]
    w_ref, tab_ref = refs[8:10]
    out_refs = refs[10:14]
    xs_ref, ms_ref = refs[14:]
    first = half_mask(MODES)
    lines = 16
    half, quarter = me_ref[0] // 4, lax.rem(me_ref[0], 4)
    table = []
    for flip, step in ((0, 0),) + SHIFTS:
        near = half + flip - 2 * flip * half
        table.append(tab_ref[0, near * 4 + lax.rem(quarter + 4 - step, 4)].astype(F32))
    forward = jnp.concatenate(table, axis=0).T[:64].astype(BF16)
    table = [tab_ref[1, half * 4 + lax.rem(quarter + step, 4)].astype(F32) for step in range(4)]
    inverse = jnp.concatenate(table, axis=0)[:, :64].astype(BF16)
    for g in range(2):
        z = [ref[:, g * 512 : (g + 1) * 512].astype(F32) for ref in z_refs]
        z = jnp.concatenate(z, axis=0).astype(BF16)
        spec = dot(forward, z)
        for b in range(4):
            re = spec[0:32, b * 128 : (b + 1) * 128]
            im = spec[32:64, b * 128 : (b + 1) * 128]
            line = g * 8 + 2 * b
            xs_ref[pl.ds(line, MODES, stride=lines), :] = jnp.where(
                first, re, pltpu.roll(im, 64, 1)
            )
            xs_ref[pl.ds(line + 1, MODES, stride=lines), :] = jnp.where(
                first, pltpu.roll(re, 64, 1), im
            )
    weights = lambda src: [(src * 4 + j, w_ref[src, 0, j]) for j in range(4)]
    mix(xs_ref, ms_ref, lines, 8, weights)
    for g in range(2):
        cols = []
        for b in range(4):
            line = g * 8 + 2 * b
            m0 = ms_ref[pl.ds(line, MODES, stride=lines), :]
            m1 = ms_ref[pl.ds(line + 1, MODES, stride=lines), :]
            re = jnp.where(first, m0, pltpu.roll(m1, 64, 1))
            im = jnp.where(first, pltpu.roll(m0, 64, 1), m1)
            cols.append(jnp.concatenate([re, im], axis=0).astype(BF16))
        out = dot(inverse, jnp.concatenate(cols, axis=1)).astype(BF16)
        for step in range(4):
            out_refs[step][:, g * 512 : (g + 1) * 512] = out[step * RYP : (step + 1) * RYP]


def mid_y(layer, me, zs, w, c):
    table = c["mid_y"]
    return pl.pallas_call(
        mid_y_kernel,
        name="mid_y",
        grid_spec=pltpu.PrefetchScalarGridSpec(
            num_scalar_prefetch=1,
            grid=(1,),
            in_specs=[whole(z) for z in zs]
            + [
                pl.BlockSpec((8, 1, 4, CH, 128), lambda i, me: (0, layer, 0, 0, 0)),
                whole(table),
            ],
            out_specs=[pl.BlockSpec((RYP, QUARTER), lambda i, me: (0, 0))] * 4,
            scratch_shapes=[pltpu.VMEM((MODES * 16, 128), F32)] * 2,
        ),
        out_shape=[jax.ShapeDtypeStruct((RYP, QUARTER), BF16)] * 4,
        compiler_params=params(20),
        cost_estimate=estimate(2),
    )(me, *zs, w, table)


def gelu(x):
    x = x.astype(BF16)
    inner = x * (0.7978845608028654 + 0.035677408136300125 * (x * x))
    half = 0.5 * x
    return half + half * jnp.tanh(inner)


def last_kernel(more, *refs):
    me_ref, yx_ref, bx_ref = refs[:3]
    yy_refs = refs[3:7]
    cy_ref, state_ref, we_ref, wr_ref = refs[7:11]
    if more:
        out_ref, zx_ref, zy_ref, kron_ref, we4_ref, wr4_ref, yy_ref, acc_ref = refs[11:]
    else:
        out_ref, kron_ref, we4_ref, wr4_ref, yy_ref, t_ref = refs[11:]
    g = pl.program_id(0)

    @pl.when(g == 0)
    def _():
        we4_ref[...] = jnp.zeros_like(we4_ref)
        wr4_ref[...] = jnp.zeros_like(wr4_ref)
        for j in range(4):
            we4_ref[j * CH : (j + 1) * CH, j * HID : (j + 1) * HID] = we_ref[0]
            wr4_ref[j * CH : (j + 1) * CH, j * HID : (j + 1) * HID] = wr_ref[0]
        for step in range(4):
            yy_ref[lax.rem(me_ref[0] + 4 - step, 4)] = yy_refs[step][...]

    fill_kron(bx_ref, kron_ref)
    basis = cy_ref[...].astype(F32).T.astype(BF16)
    yy = yy_ref[g]
    for j in range(WIDE // 256):
        lanes = slice(j * 256, (j + 1) * 256)
        if j % 2 == 0:
            both = slice(j * 256, (j + 2) * 256)
            total = dot(yx_ref[...], kron_ref[:, both]) + dot(basis, yy[:, both])
            total = total.astype(BF16)
            total = jnp.concatenate([total[:, :256], total[:, 256:]], axis=0)
            hidden = gelu(dot(total, we4_ref[...])).astype(BF16)
            updates = dot_nt(hidden, wr4_ref[...])
        update = updates[(j % 2) * 256 : (j % 2 + 1) * 256]
        new = state_ref[:, lanes].astype(F32) + update
        if more:
            out_ref[:, lanes] = new.astype(BF16)
            continue
        for h in range(2):
            for p in range(2):
                block = new[h * 128 : (h + 1) * 128, p * 128 : (p + 1) * 128].T
                x = j * 4 + p * 2
                t_ref[h, pl.ds(x, CH, stride=GROUP), :] = block[:CH]
                t_ref[h, pl.ds(x + 1, CH, stride=GROUP), :] = block[CH:]
    if more:
        coefficients(g, out_ref[...], kron_ref, cy_ref, acc_ref, zx_ref, zy_ref)
    else:
        for h in range(2):
            part = t_ref[h].reshape(CH, GROUP, 128).astype(BF16)
            out_ref[:, :, h * 128 : (h + 1) * 128] = part


def last_call(layer, more, me, yx, yy, state, we, wr, c):
    in_specs = [
        pl.BlockSpec(memory_space=pltpu.SMEM),
        pl.BlockSpec((256, RX * CH), lambda g: (0, 0)),
        pl.BlockSpec((16, 128), lambda g: (0, 0)),
        *[pl.BlockSpec((RYP, QUARTER), lambda g: (0, 0))] * 4,
        pl.BlockSpec((RYP, 256), lambda g: (0, 0)),
        pl.BlockSpec((256, WIDE), lambda g: (0, g)),
        pl.BlockSpec((1, CH, HID), lambda g: (layer, 0, 0)),
        pl.BlockSpec((1, CH, HID), lambda g: (layer, 0, 0)),
    ]
    scratch = [pltpu.VMEM((RX * CH, WIDE), BF16)] + [pltpu.VMEM((256, 1024), BF16)] * 2
    scratch.append(pltpu.VMEM((4, RYP, QUARTER), BF16))
    if more:
        out_specs = [
            pl.BlockSpec((256, WIDE), lambda g: (0, g)),
            pl.BlockSpec((256, RX * CH), lambda g: (0, 0)),
            pl.BlockSpec((1, RYP, WIDE), lambda g: (g, 0, 0)),
        ]
        out_shape = [
            jax.ShapeDtypeStruct((256, 4096), BF16),
            jax.ShapeDtypeStruct((256, RX * CH), BF16),
            jax.ShapeDtypeStruct((4, RYP, QUARTER), BF16),
        ]
        scratch.append(pltpu.VMEM((256, RX * CH), F32))
    else:
        out_specs = [pl.BlockSpec((CH, GROUP, 256), lambda g: (0, g, 0))]
        out_shape = [jax.ShapeDtypeStruct((CH, 64, 256), BF16)]
        scratch.append(pltpu.VMEM((2, CH * GROUP, 128), F32))
    return pl.pallas_call(
        functools.partial(last_kernel, more),
        name="last",
        grid=(64 // GROUP,),
        in_specs=in_specs,
        out_specs=out_specs,
        out_shape=out_shape,
        scratch_shapes=scratch,
        compiler_params=params(40),
        cost_estimate=estimate(12),
    )(me, yx, c["bx"], *yy, c["cy"], state, we, wr)


def join(w):
    return jnp.concatenate([w[..., 0, :, :], w[..., 1, :, :]], axis=-1)


def exchange_weights(own):
    same_core = [list(range(s, 32, 2)) for s in range(2)]
    mine = jnp.broadcast_to(own[None], (16, LAYERS, CH, 128))
    mine = lax.all_to_all(mine, "gx", 0, 0, axis_index_groups=same_core, tiled=True)
    return mine, lax.ppermute(mine, "gx", [(i, i ^ 1) for i in range(32)])


def permute_y(x, flip, step):
    return lax.ppermute(x, "gy", [(i, moved(i, flip, step)) for i in range(8)])


def body(state_field, spectral_x, spectral_y, expand_weight, reduce_weight):
    c = {name: jnp.asarray(value) for name, value in make_constants().items()}
    core = lax.rem(lax.axis_index("gx"), 2).reshape(1).astype(jnp.int32)
    me = lax.axis_index("gy").reshape(1).astype(jnp.int32)
    own_x, own_y = join(spectral_x)[:, 0], join(spectral_y)
    own_x, own_y = lax.optimization_barrier((own_x, own_y))
    wy = lax.all_gather(own_y, "gy", axis=0)
    wx = exchange_weights(own_x)
    wr = jnp.swapaxes(reduce_weight, 1, 2)
    state, zx, zy = first_call(state_field[0], c)
    for l in range(LAYERS):
        recv = lax.all_to_all(zx.reshape(32, LINE, RX * CH), "gx", 0, 0, tiled=True)
        zs = []
        for flip, step in ((0, 0),) + SHIFTS:
            chunk = lax.dynamic_slice_in_dim(zy, lax.rem(me[0] + step, 4), 1, 0)[0]
            zs.append(permute_y(chunk, flip, step) if flip or step else chunk)
        zs, recv = lax.optimization_barrier((zs, recv))
        send = mid_x(l, core, recv, wx[0], wx[1], c)
        yx = lax.all_to_all(send, "gx", 0, 0, tiled=True).reshape(256, RX * CH)
        yy = mid_y(l, me, zs, wy, c)
        yy = [yy[0]] + [permute_y(yy[step], 0, step) for step in range(1, 4)]
        more = l + 1 < LAYERS
        got = last_call(l, more, me, yx, yy, state, expand_weight, wr, c)
        if more:
            state, zx, zy = got
    return got[0][None]


def solution(mesh):
    in_specs = (
        P(None, None, "gx", "gy"),
        P(None, "gx", None, None, None),
        P(None, "gy", None, None, None),
        P(),
        P(),
    )
    out_specs = P(None, None, "gx", "gy")
    return jax.shard_map(body, mesh=mesh, in_specs=in_specs, out_specs=out_specs, check_vma=False)
```

```python
import functools

import jax
import jax.numpy as jnp
import numpy as np
from jax import lax
from jax.experimental import pallas as pl
from jax.experimental.pallas import tpu as pltpu
from jax.sharding import PartitionSpec as P

F32 = jnp.float32
BF16 = jnp.bfloat16
NX = 2048
NY = 2048
CH = 64
HID = 256
MODES = 32
LAYERS = 2
RX = 10
RY = 20
RYP = 24
GROUP = 16
WIDE = GROUP * CH
LINE = 8


def window_tables(length, devices, rank):
    window = length // devices
    k = np.arange(MODES)[:, None]
    p = np.arange(length)[None, :]
    angle = 2.0 * np.pi * ((k * p) % length) / length
    scale = 1.0 / np.sqrt(length)
    weight = np.where(np.arange(MODES) == 0, 1.0, 2.0)[:, None]
    forward = np.concatenate([np.cos(angle), -np.sin(angle)], 0) * scale
    inverse = np.concatenate([weight * np.cos(angle), -weight * np.sin(angle)], 0) * scale
    _, _, vt = np.linalg.svd(forward[:, :window], full_matrices=False)
    basis = vt[:rank]
    basis = basis * np.sign(basis[np.arange(rank), np.abs(basis).argmax(1)])[:, None]
    fwd = np.stack([forward[:, d * window : (d + 1) * window] @ basis.T for d in range(devices)])
    inv = np.stack([inverse[:, d * window : (d + 1) * window] @ basis.T for d in range(devices)])
    return basis, fwd, inv


SHIFTS = ((1, 0), (0, 1), (0, 3), (1, 2), (0, 2), (1, 1), (1, 3))
UNROLL = 4
QUARTER = 16 * 64


def moved(me, flip, step):
    return (me // 4 ^ flip) * 4 + (me + step) % 4


def bf(x):
    return np.asarray(x, np.float32).astype(jnp.bfloat16)


def make_constants():
    bx, fx, ix = window_tables(NX, 32, RX)
    by, fy, iy = window_tables(NY, 8, RY)
    pairs = RX // 2
    ax = fx.reshape(32, 64, pairs, 2).transpose(3, 1, 2, 0).reshape(128, pairs * 32)
    gx = ix.reshape(32, 2, MODES, pairs, 2)
    u0 = gx[..., 0].transpose(3, 0, 1, 2).reshape(pairs * 32, 64)
    u1 = gx[..., 1].transpose(3, 0, 1, 2)[:, :, ::-1].reshape(pairs * 32, 64)
    mid_x = np.zeros((128 + pairs * 32, 256))
    mid_x[:128, : pairs * 32] = ax
    mid_x[128:, :64] = u0
    mid_x[128:, 64:128] = u1
    mid_y = np.zeros((2, 8, RYP, 128))
    mid_y[0, :, :RY, :64] = fy.transpose(0, 2, 1)
    mid_y[1, :, :RY, :64] = iy.transpose(0, 2, 1)
    cy = np.pad(by, ((0, RYP - RY), (0, 0)))
    bx = np.pad(bx, ((0, 16 - RX), (0, 128 - 64)))
    return dict(mid_x=bf(mid_x), mid_y=bf(mid_y), cy=bf(cy), bx=bf(bx))


def dot(a, b):
    return jnp.dot(a, b, preferred_element_type=F32)


def dot_nt(a, b):
    return lax.dot_general(a, b, (((1,), (1,)), ((), ())), preferred_element_type=F32)


def half_mask(rows):
    return lax.broadcasted_iota(jnp.int32, (rows, 128), 1) < 64


def dot_tn(a, b):
    return lax.dot_general(a, b, (((0,), (0,)), ((), ())), preferred_element_type=F32)


def estimate(us):
    return pl.CostEstimate(flops=int(us * 1e9), bytes_accessed=1 << 20, transcendentals=0)


def params(mib):
    return pltpu.CompilerParams(vmem_limit_bytes=mib << 20)


def fill_kron(bx_ref, kron_ref):
    lanes = lax.broadcasted_iota(jnp.int32, (CH, WIDE), 1)
    rows = lax.broadcasted_iota(jnp.int32, (CH, WIDE), 0)
    eye = (lanes % CH) == rows
    x = lax.broadcasted_iota(jnp.int32, (128, WIDE), 1) // CH + GROUP * pl.program_id(0)
    position = lax.broadcasted_iota(jnp.int32, (128, WIDE), 0)
    spread = dot(bx_ref[...], jnp.where(x == position, 1.0, 0.0).astype(BF16))
    for r in range(RX):
        row = jnp.broadcast_to(spread[r : r + 1, :], (CH, WIDE))
        kron_ref[r * CH : (r + 1) * CH, :] = jnp.where(eye, row, 0.0).astype(BF16)


def coefficients(g, state, kron_ref, cy_ref, acc_ref, zx_ref, zy_ref):
    part = dot_nt(state, kron_ref[...])

    @pl.when(g == 0)
    def _():
        acc_ref[...] = part

    @pl.when(g > 0)
    def _():
        acc_ref[...] += part

    zy_ref[0] = dot(cy_ref[...], state).astype(BF16)

    @pl.when(g == pl.num_programs(0) - 1)
    def _():
        zx_ref[...] = acc_ref[...].astype(BF16)


def first_kernel(field_ref, bx_ref, cy_ref, state_ref, zx_ref, zy_ref, t_ref, kron_ref, acc_ref):
    for h in range(2):
        part = field_ref[:, :, h * 128 : (h + 1) * 128].astype(F32)
        t_ref[h] = part.reshape(CH * GROUP, 128)
    for h in range(2):
        for p in range(GROUP // 2):
            two = [t_ref[h, pl.ds(2 * p + j, CH, stride=GROUP), :] for j in range(2)]
            block = jnp.concatenate(two, axis=0).T.astype(BF16)
            state_ref[h * 128 : (h + 1) * 128, p * 128 : (p + 1) * 128] = block
    fill_kron(bx_ref, kron_ref)
    coefficients(pl.program_id(0), state_ref[...], kron_ref, cy_ref, acc_ref, zx_ref, zy_ref)


def first_call(field, c):
    return pl.pallas_call(
        first_kernel,
        name="first",
        grid=(64 // GROUP,),
        in_specs=[
            pl.BlockSpec((CH, GROUP, 256), lambda g: (0, g, 0)),
            pl.BlockSpec((16, 128), lambda g: (0, 0)),
            pl.BlockSpec((RYP, 256), lambda g: (0, 0)),
        ],
        out_specs=[
            pl.BlockSpec((256, WIDE), lambda g: (0, g)),
            pl.BlockSpec((256, RX * CH), lambda g: (0, 0)),
            pl.BlockSpec((1, RYP, WIDE), lambda g: (g, 0, 0)),
        ],
        out_shape=[
            jax.ShapeDtypeStruct((256, 4096), BF16),
            jax.ShapeDtypeStruct((256, RX * CH), BF16),
            jax.ShapeDtypeStruct((4, RYP, QUARTER), BF16),
        ],
        scratch_shapes=[
            pltpu.VMEM((2, CH * GROUP, 128), F32),
            pltpu.VMEM((RX * CH, WIDE), BF16),
            pltpu.VMEM((256, RX * CH), F32),
        ],
        compiler_params=params(36),
        cost_estimate=estimate(10),
    )(field, c["bx"], c["cy"])


def mode_weights(w, sign):
    w = w.astype(F32)
    return jnp.concatenate([w * sign, pltpu.roll(w, 64, 1)], axis=0).astype(BF16)


def mix(xs_ref, ms_ref, lines, steps, weights):
    sign = jnp.where(half_mask(CH), 1.0, -1.0)

    def product(i, _):
        for mode, w in weights(i):
            rows = pl.ds(pl.multiple_of(mode * lines, lines), lines)
            ms_ref[rows, :] = dot_nt(xs_ref[rows, :].astype(BF16), mode_weights(w, sign))

    lax.fori_loop(0, steps, product, None, unroll=UNROLL)


def mid_x_kernel(
    core_ref, layer_ref, recv_ref, near0_ref, near1_ref, far0_ref, far1_ref, tab_ref, *refs
):
    send_ref, r_ref, xs_ref, ms_ref, o_ref = refs
    pairs = RX // 2
    first = half_mask(MODES)
    for p in range(pairs):
        part = recv_ref[:, :, p * 128 : (p + 1) * 128]
        r_ref[p] = part.reshape(256, 128).astype(F32)
    cols = []
    for y in range(LINE):
        ry = [r_ref[p, pl.ds(y, 32, stride=LINE), :] for p in range(pairs)]
        cols.append(jnp.concatenate(ry, axis=0).astype(BF16))
    spec = dot(tab_ref[:128, : pairs * 32], jnp.concatenate(cols, axis=1))
    for y in range(LINE):
        s = spec[:, y * 128 : (y + 1) * 128]
        x = jnp.where(first, s[0:32], s[96:128])
        x = x + pltpu.roll(jnp.where(first, s[32:64], s[64:96]), 64, 1)
        xs_ref[pl.ds(y, MODES, stride=LINE), :] = x
    core = core_ref[0]
    layer = layer_ref[0]

    def weights(t):
        mine = jnp.where(layer == 0, near0_ref[t].astype(F32), far0_ref[t].astype(F32))
        swapped = jnp.where(layer == 0, near1_ref[t].astype(F32), far1_ref[t].astype(F32))
        return [(t * 2 + core, mine), (t * 2 + 1 - core, swapped)]

    mix(xs_ref, ms_ref, LINE, 16, weights)
    cols = []
    for y in range(LINE):
        m = ms_ref[pl.ds(y, MODES, stride=LINE), :]
        cols.append(jnp.concatenate([m, pltpu.roll(m, 64, 1)], axis=0).astype(BF16))
    cols = jnp.concatenate(cols, axis=1)
    out0 = dot(tab_ref[128:, :64], cols)
    out1 = dot(tab_ref[128:, 64:128], cols)
    for y in range(LINE):
        for p in range(pairs):
            v0 = out0[p * 32 : (p + 1) * 32, y * 128 : (y + 1) * 128]
            v1 = out1[p * 32 : (p + 1) * 32, y * 128 : (y + 1) * 128]
            o_ref[p, pl.ds(y, 32, stride=LINE), :] = jnp.where(first, v0, v1)
    for p in range(pairs):
        part = o_ref[p].reshape(32, LINE, 128).astype(BF16)
        send_ref[:, :, p * 128 : (p + 1) * 128] = part


def whole(a):
    return pl.BlockSpec(a.shape, lambda *_: (0,) * a.ndim)


def mid_x(core, layer, recv, w, c):
    return pl.pallas_call(
        mid_x_kernel,
        name="mid_x",
        grid=(1,),
        in_specs=[pl.BlockSpec(memory_space=pltpu.SMEM)] * 2
        + [whole(a) for a in (recv, *w, c["mid_x"])],
        out_specs=whole(recv),
        out_shape=jax.ShapeDtypeStruct(recv.shape, BF16),
        scratch_shapes=[
            pltpu.VMEM((RX // 2, 256, 128), F32),
            pltpu.VMEM((MODES * LINE, 128), F32),
            pltpu.VMEM((MODES * LINE, 128), F32),
            pltpu.VMEM((RX // 2, 256, 128), F32),
        ],
        compiler_params=params(16),
        cost_estimate=estimate(3),
    )(core, layer, recv, *w, c["mid_x"])


def mid_y_kernel(me_ref, *refs):
    z_refs, w_refs = refs[:8], refs[8:16]
    tab_ref = refs[16]
    out_refs = refs[17:21]
    xs_ref, ms_ref, w_ref = refs[21:]
    first = half_mask(MODES)
    lines = 16
    half, quarter = me_ref[0] // 4, lax.rem(me_ref[0], 4)
    sources = []
    for flip, step in ((0, 0),) + SHIFTS:
        near = half + flip - 2 * flip * half
        sources.append(near * 4 + lax.rem(quarter + 4 - step, 4))
    table = [tab_ref[0, src].astype(F32) for src in sources]
    forward = jnp.concatenate(table, axis=0).T[:64].astype(BF16)
    table = [tab_ref[1, half * 4 + lax.rem(quarter + step, 4)].astype(F32) for step in range(4)]
    inverse = jnp.concatenate(table, axis=0)[:, :64].astype(BF16)
    for g in range(2):
        z = [ref[:, g * 512 : (g + 1) * 512].astype(F32) for ref in z_refs]
        z = jnp.concatenate(z, axis=0).astype(BF16)
        spec = dot(forward, z)
        for b in range(4):
            re = spec[0:32, b * 128 : (b + 1) * 128]
            im = spec[32:64, b * 128 : (b + 1) * 128]
            line = g * 8 + 2 * b
            xs_ref[pl.ds(line, MODES, stride=lines), :] = jnp.where(
                first, re, pltpu.roll(im, 64, 1)
            )
            xs_ref[pl.ds(line + 1, MODES, stride=lines), :] = jnp.where(
                first, pltpu.roll(re, 64, 1), im
            )
    for slot, src in enumerate(sources):
        w_ref[src] = w_refs[slot][0]
    weights = lambda src: [(src * 4 + j, w_ref[src, j]) for j in range(4)]
    mix(xs_ref, ms_ref, lines, 8, weights)
    for g in range(2):
        cols = []
        for b in range(4):
            line = g * 8 + 2 * b
            m0 = ms_ref[pl.ds(line, MODES, stride=lines), :]
            m1 = ms_ref[pl.ds(line + 1, MODES, stride=lines), :]
            re = jnp.where(first, m0, pltpu.roll(m1, 64, 1))
            im = jnp.where(first, pltpu.roll(m0, 64, 1), m1)
            cols.append(jnp.concatenate([re, im], axis=0).astype(BF16))
        out = dot(inverse, jnp.concatenate(cols, axis=1)).astype(BF16)
        for step in range(4):
            out_refs[step][:, g * 512 : (g + 1) * 512] = out[step * RYP : (step + 1) * RYP]


def mid_y(layer, me, zs, w, c):
    return pl.pallas_call(
        mid_y_kernel,
        name="mid_y",
        grid=(1,),
        in_specs=[pl.BlockSpec(memory_space=pltpu.SMEM)]
        + [whole(z) for z in zs]
        + [pl.BlockSpec((1, 4, CH, 128), lambda i: (layer, 0, 0, 0))] * 8
        + [whole(c["mid_y"])],
        out_specs=[pl.BlockSpec((RYP, QUARTER), lambda i: (0, 0))] * 4,
        scratch_shapes=[pltpu.VMEM((MODES * 16, 128), F32)] * 2
        + [pltpu.VMEM((8, 4, CH, 128), BF16)],
        out_shape=[jax.ShapeDtypeStruct((RYP, QUARTER), BF16)] * 4,
        compiler_params=params(20),
        cost_estimate=estimate(2),
    )(me, *zs, *w, c["mid_y"])


def gelu(x):
    x = x.astype(BF16)
    inner = x * (0.7978845608028654 + 0.035677408136300125 * (x * x))
    half = 0.5 * x
    return half + half * jnp.tanh(inner)


def last_kernel(more, *refs):
    me_ref, yx_ref, bx_ref = refs[:3]
    yy_refs = refs[3:7]
    cy_ref, state_ref, we_ref, wr_ref = refs[7:11]
    if more:
        out_ref, zx_ref, zy_ref, kron_ref, we4_ref, wr4_ref, yy_ref, acc_ref = refs[11:]
    else:
        out_ref, kron_ref, we4_ref, wr4_ref, yy_ref, t_ref = refs[11:]
    g = pl.program_id(0)

    @pl.when(g == 0)
    def _():
        we4_ref[...] = jnp.zeros_like(we4_ref)
        wr4_ref[...] = jnp.zeros_like(wr4_ref)
        for j in range(4):
            we4_ref[j * CH : (j + 1) * CH, j * HID : (j + 1) * HID] = we_ref[0]
            wr4_ref[j * CH : (j + 1) * CH, j * HID : (j + 1) * HID] = wr_ref[0]
        for step in range(4):
            yy_ref[lax.rem(me_ref[0] + 4 - step, 4)] = yy_refs[step][...]

    fill_kron(bx_ref, kron_ref)
    basis = cy_ref[...].astype(F32).T.astype(BF16)
    yy = yy_ref[g]
    for j in range(WIDE // 256):
        lanes = slice(j * 256, (j + 1) * 256)
        if j % 2 == 0:
            both = slice(j * 256, (j + 2) * 256)
            total = dot(yx_ref[...], kron_ref[:, both]) + dot(basis, yy[:, both])
            total = total.astype(BF16)
            total = jnp.concatenate([total[:, :256], total[:, 256:]], axis=0)
            hidden = gelu(dot(total, we4_ref[...])).astype(BF16)
            updates = dot_nt(hidden, wr4_ref[...])
        update = updates[(j % 2) * 256 : (j % 2 + 1) * 256]
        new = state_ref[:, lanes].astype(F32) + update
        if more:
            out_ref[:, lanes] = new.astype(BF16)
            continue
        for h in range(2):
            for p in range(2):
                block = new[h * 128 : (h + 1) * 128, p * 128 : (p + 1) * 128].T
                x = j * 4 + p * 2
                t_ref[h, pl.ds(x, CH, stride=GROUP), :] = block[:CH]
                t_ref[h, pl.ds(x + 1, CH, stride=GROUP), :] = block[CH:]
    if more:
        coefficients(g, out_ref[...], kron_ref, cy_ref, acc_ref, zx_ref, zy_ref)
    else:
        for h in range(2):
            part = t_ref[h].reshape(CH, GROUP, 128).astype(BF16)
            out_ref[:, :, h * 128 : (h + 1) * 128] = part


def last_call(layer, more, me, yx, yy, state, we, wr, c):
    in_specs = [
        pl.BlockSpec(memory_space=pltpu.SMEM),
        pl.BlockSpec((256, RX * CH), lambda g: (0, 0)),
        pl.BlockSpec((16, 128), lambda g: (0, 0)),
        *[pl.BlockSpec((RYP, QUARTER), lambda g: (0, 0))] * 4,
        pl.BlockSpec((RYP, 256), lambda g: (0, 0)),
        pl.BlockSpec((256, WIDE), lambda g: (0, g)),
        pl.BlockSpec((1, CH, HID), lambda g: (layer, 0, 0)),
        pl.BlockSpec((1, CH, HID), lambda g: (layer, 0, 0)),
    ]
    scratch = [pltpu.VMEM((RX * CH, WIDE), BF16)] + [pltpu.VMEM((256, 1024), BF16)] * 2
    scratch.append(pltpu.VMEM((4, RYP, QUARTER), BF16))
    if more:
        out_specs = [
            pl.BlockSpec((256, WIDE), lambda g: (0, g)),
            pl.BlockSpec((256, RX * CH), lambda g: (0, 0)),
            pl.BlockSpec((1, RYP, WIDE), lambda g: (g, 0, 0)),
        ]
        out_shape = [
            jax.ShapeDtypeStruct((256, 4096), BF16),
            jax.ShapeDtypeStruct((256, RX * CH), BF16),
            jax.ShapeDtypeStruct((4, RYP, QUARTER), BF16),
        ]
        scratch.append(pltpu.VMEM((256, RX * CH), F32))
    else:
        out_specs = [pl.BlockSpec((CH, GROUP, 256), lambda g: (0, g, 0))]
        out_shape = [jax.ShapeDtypeStruct((CH, 64, 256), BF16)]
        scratch.append(pltpu.VMEM((2, CH * GROUP, 128), F32))
    return pl.pallas_call(
        functools.partial(last_kernel, more),
        name="last",
        grid=(64 // GROUP,),
        in_specs=in_specs,
        out_specs=out_specs,
        out_shape=out_shape,
        scratch_shapes=scratch,
        compiler_params=params(40),
        cost_estimate=estimate(12),
    )(me, yx, c["bx"], *yy, c["cy"], state, we, wr)


def pack_kernel(half_ref, wx_ref, wy_ref, x_ref, y_ref):
    def join(parts):
        return jnp.concatenate([part.astype(F32) for part in parts], axis=1)

    for layer in range(LAYERS):
        for j in range(4):
            y_ref[layer, j] = join([wy_ref[layer, j, i] for i in range(2)]).astype(BF16)
    own = [join([wx_ref[layer, 0, i] for i in range(2)]) for layer in range(LAYERS)]
    mode = jnp.where(half_ref[0] == 0, own[0], own[1]).astype(BF16)
    for i in range(16):
        x_ref[i] = mode


def pack_call(half, spectral_x, spectral_y):
    shapes = (16, CH, 128), (LAYERS, 4, CH, 128)
    out_shape = [jax.ShapeDtypeStruct(shape, BF16) for shape in shapes]
    return pl.pallas_call(
        pack_kernel,
        name="pack",
        grid=(1,),
        in_specs=[pl.BlockSpec(memory_space=pltpu.SMEM), whole(spectral_x), whole(spectral_y)],
        out_specs=[whole(a) for a in out_shape],
        out_shape=out_shape,
        compiler_params=params(16),
        cost_estimate=estimate(2),
    )(half, spectral_x, spectral_y)


def swap_cores(x):
    return lax.ppermute(x, "gx", [(i, i ^ 1) for i in range(32)])


def permute_y(x, flip, step):
    return lax.ppermute(x, "gy", [(i, moved(i, flip, step)) for i in range(8)])


def body(state_field, spectral_x, spectral_y, expand_weight, reduce_weight):
    c = {name: jnp.asarray(value) for name, value in make_constants().items()}
    core = lax.rem(lax.axis_index("gx"), 2).reshape(1).astype(jnp.int32)
    me = lax.axis_index("gy").reshape(1).astype(jnp.int32)
    half = me // 4
    own_x, own_y = pack_call(half, spectral_x, spectral_y)
    same_core = [list(range(s, 32, 2)) for s in range(2)]
    mine = lax.all_to_all(own_x, "gx", 0, 0, axis_index_groups=same_core, tiled=True)
    wy = [own_y] + [permute_y(own_y, flip, step) for flip, step in SHIFTS]
    wr = jnp.swapaxes(reduce_weight, 1, 2)
    state, zx, zy = first_call(state_field[0], c)
    state = pltpu.with_memory_space_constraint(state, pltpu.HBM)
    zx, wy = lax.optimization_barrier((zx, wy))
    for l in range(LAYERS):
        recv = lax.all_to_all(zx.reshape(32, LINE, RX * CH), "gx", 0, 0, tiled=True)
        zs = []
        for flip, step in ((0, 0),) + SHIFTS:
            chunk = lax.dynamic_slice_in_dim(zy, lax.rem(me[0] + step, 4), 1, 0)[0]
            zs.append(permute_y(chunk, flip, step) if flip or step else chunk)
        if l == 0:
            other = permute_y(mine, 1, 0)
            wx = [mine, swap_cores(mine), other, swap_cores(other)]
        zs, recv = lax.optimization_barrier((zs, recv))
        send = mid_x(core, lax.rem(half + l, 2), recv, wx, c)
        yx = lax.all_to_all(send, "gx", 0, 0, tiled=True).reshape(256, RX * CH)
        yy = mid_y(l, me, zs, wy, c)
        yy = [yy[0]] + [permute_y(yy[step], 0, step) for step in range(1, 4)]
        more = l + 1 < LAYERS
        got = last_call(l, more, me, yx, yy, state, expand_weight, wr, c)
        if more:
            state, zx, zy = got
            state = pltpu.with_memory_space_constraint(state, pltpu.HBM)
    return got[0][None]


def solution(mesh):
    in_specs = (
        P(None, None, "gx", "gy"),
        P(None, "gx", None, None, None),
        P(None, "gy", None, None, None),
        P(),
        P(),
    )
    out_specs = P(None, None, "gx", "gy")
    return jax.shard_map(body, mesh=mesh, in_specs=in_specs, out_specs=out_specs, check_vma=False)
```

```python
import functools

import jax
import jax.numpy as jnp
import numpy as np
from jax import lax
from jax.experimental import pallas as pl
from jax.experimental.pallas import tpu as pltpu
from jax.sharding import PartitionSpec as P

F32 = jnp.float32
BF16 = jnp.bfloat16
NX = 2048
NY = 2048
CH = 64
HID = 256
MODES = 32
LAYERS = 2
RX = 10
RY = 20
RYP = 24
ROWS = RYP + 32
GROUP = 16
WIDE = GROUP * CH
LINE = 8


def window_tables(length, devices, rank):
    window = length // devices
    k = np.arange(MODES)[:, None]
    p = np.arange(length)[None, :]
    angle = 2.0 * np.pi * ((k * p) % length) / length
    scale = 1.0 / np.sqrt(length)
    weight = np.where(np.arange(MODES) == 0, 1.0, 2.0)[:, None]
    forward = np.concatenate([np.cos(angle), -np.sin(angle)], 0) * scale
    inverse = np.concatenate([weight * np.cos(angle), -weight * np.sin(angle)], 0) * scale
    _, _, vt = np.linalg.svd(forward[:, :window], full_matrices=False)
    basis = vt[:rank]
    basis = basis * np.sign(basis[np.arange(rank), np.abs(basis).argmax(1)])[:, None]
    fwd = np.stack([forward[:, d * window : (d + 1) * window] @ basis.T for d in range(devices)])
    inv = np.stack([inverse[:, d * window : (d + 1) * window] @ basis.T for d in range(devices)])
    return basis, fwd, inv


SHIFTS = ((1, 0), (0, 1), (0, 3), (1, 2), (0, 2), (1, 1), (1, 3))
UNROLL = 4
QUARTER = 16 * 64


def moved(me, flip, step):
    return (me // 4 ^ flip) * 4 + (me + step) % 4


def bf(x):
    return np.asarray(x, np.float32).astype(jnp.bfloat16)


def make_constants():
    bx, fx, ix = window_tables(NX, 32, RX)
    by, fy, iy = window_tables(NY, 8, RY)
    pairs = RX // 2
    ax = fx.reshape(32, 64, pairs, 2).transpose(3, 1, 2, 0).reshape(128, pairs * 32)
    gx = ix.reshape(32, 2, MODES, pairs, 2)
    u0 = gx[..., 0].transpose(3, 0, 1, 2).reshape(pairs * 32, 64)
    u1 = gx[..., 1].transpose(3, 0, 1, 2)[:, :, ::-1].reshape(pairs * 32, 64)
    mid_x = np.zeros((128 + pairs * 32, 256))
    mid_x[:128, : pairs * 32] = ax
    mid_x[128:, :64] = u0
    mid_x[128:, 64:128] = u1
    mid_y = np.zeros((2, 8, RYP, 128))
    mid_y[0, :, :RY, :64] = fy.transpose(0, 2, 1)
    mid_y[1, :, :RY, :64] = iy.transpose(0, 2, 1)
    cy = np.pad(by, ((0, RYP - RY), (0, 0)))
    bx = np.pad(bx, ((0, 16 - RX), (0, 128 - 64)))
    return dict(mid_x=bf(mid_x), mid_y=bf(mid_y), cy=bf(cy), bx=bf(bx))


def dot(a, b):
    return jnp.dot(a, b, preferred_element_type=F32)


def dot_nt(a, b):
    return lax.dot_general(a, b, (((1,), (1,)), ((), ())), preferred_element_type=F32)


def half_mask(rows):
    return lax.broadcasted_iota(jnp.int32, (rows, 128), 1) < 64


def dot_tn(a, b):
    return lax.dot_general(a, b, (((0,), (0,)), ((), ())), preferred_element_type=F32)


def estimate(us):
    return pl.CostEstimate(flops=int(us * 1e9), bytes_accessed=1 << 20, transcendentals=0)


def params(mib):
    return pltpu.CompilerParams(vmem_limit_bytes=mib << 20)


def fill_kron(bx_ref, kron_ref):
    lanes = lax.broadcasted_iota(jnp.int32, (CH, WIDE), 1)
    rows = lax.broadcasted_iota(jnp.int32, (CH, WIDE), 0)
    eye = (lanes % CH) == rows
    x = lax.broadcasted_iota(jnp.int32, (128, WIDE), 1) // CH + GROUP * pl.program_id(0)
    position = lax.broadcasted_iota(jnp.int32, (128, WIDE), 0)
    spread = dot(bx_ref[...], jnp.where(x == position, 1.0, 0.0).astype(BF16))
    for r in range(RX):
        row = jnp.broadcast_to(spread[r : r + 1, :], (CH, WIDE))
        kron_ref[r * CH : (r + 1) * CH, :] = jnp.where(eye, row, 0.0).astype(BF16)


def coefficients(g, state, kron_ref, cy_ref, wy_ref, acc_ref, zx_ref, zy_ref):
    part = dot_nt(state, kron_ref[...])

    @pl.when(g == 0)
    def _():
        acc_ref[...] = part

    @pl.when(g > 0)
    def _():
        acc_ref[...] += part

    zy_ref[0, :RYP] = dot(cy_ref[...], state).astype(BF16)
    zy_ref[0, RYP:] = wy_ref[0]

    @pl.when(g == pl.num_programs(0) - 1)
    def _():
        zx_ref[...] = acc_ref[...].astype(BF16)


def first_kernel(
    field_ref, bx_ref, cy_ref, wy_ref, state_ref, zx_ref, zy_ref, t_ref, kron_ref, acc_ref
):
    for h in range(2):
        part = field_ref[:, :, h * 128 : (h + 1) * 128].astype(F32)
        t_ref[h] = part.reshape(CH * GROUP, 128)
    for h in range(2):
        for p in range(GROUP // 2):
            two = [t_ref[h, pl.ds(2 * p + j, CH, stride=GROUP), :] for j in range(2)]
            block = jnp.concatenate(two, axis=0).T.astype(BF16)
            state_ref[h * 128 : (h + 1) * 128, p * 128 : (p + 1) * 128] = block
    fill_kron(bx_ref, kron_ref)
    g = pl.program_id(0)
    coefficients(g, state_ref[...], kron_ref, cy_ref, wy_ref, acc_ref, zx_ref, zy_ref)


def first_call(field, wy, c):
    return pl.pallas_call(
        first_kernel,
        name="first",
        grid=(64 // GROUP,),
        in_specs=[
            pl.BlockSpec((CH, GROUP, 256), lambda g: (0, g, 0)),
            pl.BlockSpec((16, 128), lambda g: (0, 0)),
            pl.BlockSpec((RYP, 256), lambda g: (0, 0)),
            pl.BlockSpec((1, ROWS - RYP, QUARTER), lambda g: (0, 0, 0)),
        ],
        out_specs=[
            pl.BlockSpec((256, WIDE), lambda g: (0, g)),
            pl.BlockSpec((256, RX * CH), lambda g: (0, 0)),
            pl.BlockSpec((1, ROWS, WIDE), lambda g: (g, 0, 0)),
        ],
        out_shape=[
            jax.ShapeDtypeStruct((256, 4096), BF16),
            jax.ShapeDtypeStruct((256, RX * CH), BF16),
            jax.ShapeDtypeStruct((4, ROWS, QUARTER), BF16),
        ],
        scratch_shapes=[
            pltpu.VMEM((2, CH * GROUP, 128), F32),
            pltpu.VMEM((RX * CH, WIDE), BF16),
            pltpu.VMEM((256, RX * CH), F32),
        ],
        compiler_params=params(36),
        cost_estimate=estimate(10),
    )(field, c["bx"], c["cy"], wy)


def mode_weights(w, sign):
    w = w.astype(F32)
    return jnp.concatenate([w * sign, pltpu.roll(w, 64, 1)], axis=0).astype(BF16)


def mix(xs_ref, ms_ref, lines, steps, weights):
    sign = jnp.where(half_mask(CH), 1.0, -1.0)

    def product(i, _):
        for mode, w in weights(i):
            rows = pl.ds(pl.multiple_of(mode * lines, lines), lines)
            ms_ref[rows, :] = dot_nt(xs_ref[rows, :].astype(BF16), mode_weights(w, sign))

    lax.fori_loop(0, steps, product, None, unroll=UNROLL)


def mid_x_kernel(
    core_ref, recv_ref, w0_ref, w1_ref, tab_ref, *refs
):
    send_ref, r_ref, xs_ref, ms_ref, o_ref = refs
    pairs = RX // 2
    first = half_mask(MODES)
    for p in range(pairs):
        part = recv_ref[:, :, p * 128 : (p + 1) * 128]
        r_ref[p] = part.reshape(256, 128).astype(F32)
    cols = []
    for y in range(LINE):
        ry = [r_ref[p, pl.ds(y, 32, stride=LINE), :] for p in range(pairs)]
        cols.append(jnp.concatenate(ry, axis=0).astype(BF16))
    spec = dot(tab_ref[:128, : pairs * 32], jnp.concatenate(cols, axis=1))
    for y in range(LINE):
        s = spec[:, y * 128 : (y + 1) * 128]
        x = jnp.where(first, s[0:32], s[96:128])
        x = x + pltpu.roll(jnp.where(first, s[32:64], s[64:96]), 64, 1)
        xs_ref[pl.ds(y, MODES, stride=LINE), :] = x
    core = core_ref[0]
    weights = lambda t: [(t * 2 + core, w0_ref[t, 0]), (t * 2 + 1 - core, w1_ref[t, 0])]
    mix(xs_ref, ms_ref, LINE, 16, weights)
    cols = []
    for y in range(LINE):
        m = ms_ref[pl.ds(y, MODES, stride=LINE), :]
        cols.append(jnp.concatenate([m, pltpu.roll(m, 64, 1)], axis=0).astype(BF16))
    cols = jnp.concatenate(cols, axis=1)
    out0 = dot(tab_ref[128:, :64], cols)
    out1 = dot(tab_ref[128:, 64:128], cols)
    for y in range(LINE):
        for p in range(pairs):
            v0 = out0[p * 32 : (p + 1) * 32, y * 128 : (y + 1) * 128]
            v1 = out1[p * 32 : (p + 1) * 32, y * 128 : (y + 1) * 128]
            o_ref[p, pl.ds(y, 32, stride=LINE), :] = jnp.where(first, v0, v1)
    for p in range(pairs):
        part = o_ref[p].reshape(32, LINE, 128).astype(BF16)
        send_ref[:, :, p * 128 : (p + 1) * 128] = part


def whole(a):
    return pl.BlockSpec(a.shape, lambda *_: (0,) * a.ndim)


def mid_x(layer, core, recv, w0, w1, c):
    weights = pl.BlockSpec((16, 1, CH, 128), lambda i: (0, layer, 0, 0))
    return pl.pallas_call(
        mid_x_kernel,
        name="mid_x",
        grid=(1,),
        in_specs=[pl.BlockSpec(memory_space=pltpu.SMEM)]
        + [whole(recv), weights, weights, whole(c["mid_x"])],
        out_specs=whole(recv),
        out_shape=jax.ShapeDtypeStruct(recv.shape, BF16),
        scratch_shapes=[
            pltpu.VMEM((RX // 2, 256, 128), F32),
            pltpu.VMEM((MODES * LINE, 128), F32),
            pltpu.VMEM((MODES * LINE, 128), F32),
            pltpu.VMEM((RX // 2, 256, 128), F32),
        ],
        compiler_params=params(16),
        cost_estimate=estimate(3),
    )(core, recv, w0, w1, c["mid_x"])


def mid_y_kernel(me_ref, *refs):
    z_refs, tab_ref, out_refs = refs[:8], refs[8], refs[9:13]
    xs_ref, ms_ref, w_ref = refs[13:]
    first = half_mask(MODES)
    lines = 16
    half, quarter = me_ref[0] // 4, lax.rem(me_ref[0], 4)
    sources = []
    for flip, step in ((0, 0),) + SHIFTS:
        near = half + flip - 2 * flip * half
        sources.append(near * 4 + lax.rem(quarter + 4 - step, 4))
    table = [tab_ref[0, src].astype(F32) for src in sources]
    forward = jnp.concatenate(table, axis=0).T[:64].astype(BF16)
    table = [tab_ref[1, half * 4 + lax.rem(quarter + step, 4)].astype(F32) for step in range(4)]
    inverse = jnp.concatenate(table, axis=0)[:, :64].astype(BF16)
    for g in range(2):
        z = [ref[:RYP, g * 512 : (g + 1) * 512].astype(F32) for ref in z_refs]
        z = jnp.concatenate(z, axis=0).astype(BF16)
        spec = dot(forward, z)
        for b in range(4):
            re = spec[0:32, b * 128 : (b + 1) * 128]
            im = spec[32:64, b * 128 : (b + 1) * 128]
            line = g * 8 + 2 * b
            xs_ref[pl.ds(line, MODES, stride=lines), :] = jnp.where(
                first, re, pltpu.roll(im, 64, 1)
            )
            xs_ref[pl.ds(line + 1, MODES, stride=lines), :] = jnp.where(
                first, pltpu.roll(re, 64, 1), im
            )
    for ref, src in zip(z_refs, sources):
        packed = ref[RYP:, :].astype(F32)
        for j in range(4):
            tiles = [packed[j * 8 : (j + 1) * 8, t * 128 : (t + 1) * 128] for t in range(8)]
            w_ref[src, j] = jnp.concatenate(tiles, axis=0).astype(BF16)
    weights = lambda src: [(src * 4 + j, w_ref[src, j]) for j in range(4)]
    mix(xs_ref, ms_ref, lines, 8, weights)
    for g in range(2):
        cols = []
        for b in range(4):
            line = g * 8 + 2 * b
            m0 = ms_ref[pl.ds(line, MODES, stride=lines), :]
            m1 = ms_ref[pl.ds(line + 1, MODES, stride=lines), :]
            re = jnp.where(first, m0, pltpu.roll(m1, 64, 1))
            im = jnp.where(first, pltpu.roll(m0, 64, 1), m1)
            cols.append(jnp.concatenate([re, im], axis=0).astype(BF16))
        out = dot(inverse, jnp.concatenate(cols, axis=1)).astype(BF16)
        for step in range(4):
            out_refs[step][:, g * 512 : (g + 1) * 512] = out[step * RYP : (step + 1) * RYP]


def mid_y(me, zs, c):
    return pl.pallas_call(
        mid_y_kernel,
        name="mid_y",
        grid=(1,),
        in_specs=[pl.BlockSpec(memory_space=pltpu.SMEM)]
        + [whole(z) for z in zs]
        + [whole(c["mid_y"])],
        out_specs=[pl.BlockSpec((RYP, QUARTER), lambda i: (0, 0))] * 4,
        scratch_shapes=[pltpu.VMEM((MODES * 16, 128), F32)] * 2
        + [pltpu.VMEM((8, 4, CH, 128), BF16)],
        out_shape=[jax.ShapeDtypeStruct((RYP, QUARTER), BF16)] * 4,
        compiler_params=params(20),
        cost_estimate=estimate(2),
    )(me, *zs, c["mid_y"])


def gelu(x):
    x = x.astype(BF16)
    inner = x * (0.7978845608028654 + 0.035677408136300125 * (x * x))
    half = 0.5 * x
    return half + half * jnp.tanh(inner)


def last_kernel(more, *refs):
    me_ref, yx_ref, bx_ref = refs[:3]
    yy_refs = refs[3:7]
    cy_ref, state_ref, we_ref, wr_ref = refs[7:11]
    if more:
        wy_ref, out_ref, zx_ref, zy_ref, kron_ref, we4_ref, wr4_ref, yy_ref, acc_ref = refs[11:]
    else:
        out_ref, kron_ref, we4_ref, wr4_ref, yy_ref, t_ref = refs[11:]
    g = pl.program_id(0)

    @pl.when(g == 0)
    def _():
        we4_ref[...] = jnp.zeros_like(we4_ref)
        wr4_ref[...] = jnp.zeros_like(wr4_ref)
        for j in range(4):
            we4_ref[j * CH : (j + 1) * CH, j * HID : (j + 1) * HID] = we_ref[0]
            wr4_ref[j * CH : (j + 1) * CH, j * HID : (j + 1) * HID] = wr_ref[0]
        for step in range(4):
            yy_ref[lax.rem(me_ref[0] + 4 - step, 4)] = yy_refs[step][...]

    fill_kron(bx_ref, kron_ref)
    basis = cy_ref[...].astype(F32).T.astype(BF16)
    yy = yy_ref[g]
    for j in range(WIDE // 256):
        lanes = slice(j * 256, (j + 1) * 256)
        if j % 2 == 0:
            both = slice(j * 256, (j + 2) * 256)
            total = dot(yx_ref[...], kron_ref[:, both]) + dot(basis, yy[:, both])
            total = total.astype(BF16)
            total = jnp.concatenate([total[:, :256], total[:, 256:]], axis=0)
            hidden = gelu(dot(total, we4_ref[...])).astype(BF16)
            updates = dot_nt(hidden, wr4_ref[...])
        update = updates[(j % 2) * 256 : (j % 2 + 1) * 256]
        new = state_ref[:, lanes].astype(F32) + update
        if more:
            out_ref[:, lanes] = new.astype(BF16)
            continue
        for h in range(2):
            for p in range(2):
                block = new[h * 128 : (h + 1) * 128, p * 128 : (p + 1) * 128].T
                x = j * 4 + p * 2
                t_ref[h, pl.ds(x, CH, stride=GROUP), :] = block[:CH]
                t_ref[h, pl.ds(x + 1, CH, stride=GROUP), :] = block[CH:]
    if more:
        coefficients(g, out_ref[...], kron_ref, cy_ref, wy_ref, acc_ref, zx_ref, zy_ref)
    else:
        for h in range(2):
            part = t_ref[h].reshape(CH, GROUP, 128).astype(BF16)
            out_ref[:, :, h * 128 : (h + 1) * 128] = part


def last_call(layer, more, me, yx, yy, state, we, wr, wy, c):
    in_specs = [
        pl.BlockSpec(memory_space=pltpu.SMEM),
        pl.BlockSpec((256, RX * CH), lambda g: (0, 0)),
        pl.BlockSpec((16, 128), lambda g: (0, 0)),
        *[pl.BlockSpec((RYP, QUARTER), lambda g: (0, 0))] * 4,
        pl.BlockSpec((RYP, 256), lambda g: (0, 0)),
        pl.BlockSpec((256, WIDE), lambda g: (0, g)),
        pl.BlockSpec((1, CH, HID), lambda g: (layer, 0, 0)),
        pl.BlockSpec((1, CH, HID), lambda g: (layer, 0, 0)),
    ]
    scratch = [pltpu.VMEM((RX * CH, WIDE), BF16)] + [pltpu.VMEM((256, 1024), BF16)] * 2
    scratch.append(pltpu.VMEM((4, RYP, QUARTER), BF16))
    args = [me, yx, c["bx"], *yy, c["cy"], state, we, wr]
    if more:
        in_specs.append(
            pl.BlockSpec((1, ROWS - RYP, QUARTER), lambda g: (layer + 1, 0, 0))
        )
        args.append(wy)
        out_specs = [
            pl.BlockSpec((256, WIDE), lambda g: (0, g)),
            pl.BlockSpec((256, RX * CH), lambda g: (0, 0)),
            pl.BlockSpec((1, ROWS, WIDE), lambda g: (g, 0, 0)),
        ]
        out_shape = [
            jax.ShapeDtypeStruct((256, 4096), BF16),
            jax.ShapeDtypeStruct((256, RX * CH), BF16),
            jax.ShapeDtypeStruct((4, ROWS, QUARTER), BF16),
        ]
        scratch.append(pltpu.VMEM((256, RX * CH), F32))
    else:
        out_specs = [pl.BlockSpec((CH, GROUP, 256), lambda g: (0, g, 0))]
        out_shape = [jax.ShapeDtypeStruct((CH, 64, 256), BF16)]
        scratch.append(pltpu.VMEM((2, CH * GROUP, 128), F32))
    return pl.pallas_call(
        functools.partial(last_kernel, more),
        name="last",
        grid=(64 // GROUP,),
        in_specs=in_specs,
        out_specs=out_specs,
        out_shape=out_shape,
        scratch_shapes=scratch,
        compiler_params=params(40),
        cost_estimate=estimate(12),
    )(*args)


def pack_kernel(wx_ref, wy_ref, x_ref, y_ref):
    def join(parts):
        return jnp.concatenate([part.astype(F32) for part in parts], axis=1)

    for layer in range(LAYERS):
        own = join([wx_ref[layer, 0, i] for i in range(2)]).astype(BF16)
        for i in range(16):
            x_ref[i, layer] = own
        rows = []
        for j in range(4):
            own = join([wy_ref[layer, j, i] for i in range(2)])
            rows.append(join([own[t * 8 : (t + 1) * 8] for t in range(8)]))
        y_ref[layer] = jnp.concatenate(rows, axis=0).astype(BF16)


def pack_call(spectral_x, spectral_y):
    shapes = (16, LAYERS, CH, 128), (LAYERS, ROWS - RYP, QUARTER)
    out_shape = [jax.ShapeDtypeStruct(shape, BF16) for shape in shapes]
    return pl.pallas_call(
        pack_kernel,
        name="pack",
        grid=(1,),
        in_specs=[whole(spectral_x), whole(spectral_y)],
        out_specs=[whole(a) for a in out_shape],
        out_shape=out_shape,
        compiler_params=params(16),
        cost_estimate=estimate(2),
    )(spectral_x, spectral_y)


def swap_cores(x):
    return lax.ppermute(x, "gx", [(i, i ^ 1) for i in range(32)])


def permute_y(x, flip, step):
    return lax.ppermute(x, "gy", [(i, moved(i, flip, step)) for i in range(8)])


def body(state_field, spectral_x, spectral_y, expand_weight, reduce_weight):
    c = {name: jnp.asarray(value) for name, value in make_constants().items()}
    core = lax.rem(lax.axis_index("gx"), 2).reshape(1).astype(jnp.int32)
    me = lax.axis_index("gy").reshape(1).astype(jnp.int32)
    own_x, wy = pack_call(spectral_x, spectral_y)
    same_core = [list(range(s, 32, 2)) for s in range(2)]
    mine = lax.all_to_all(own_x, "gx", 0, 0, axis_index_groups=same_core, tiled=True)
    swapped = swap_cores(mine)
    wr = jnp.swapaxes(reduce_weight, 1, 2)
    state, zx, zy = first_call(state_field[0], wy, c)
    for l in range(LAYERS):
        state = pltpu.with_memory_space_constraint(state, pltpu.HBM)
        recv = lax.all_to_all(zx.reshape(32, LINE, RX * CH), "gx", 0, 0, tiled=True)
        zs = []
        for flip, step in ((0, 0),) + SHIFTS:
            chunk = lax.dynamic_slice_in_dim(zy, lax.rem(me[0] + step, 4), 1, 0)[0]
            zs.append(permute_y(chunk, flip, step) if flip or step else chunk)
        zs, recv = lax.optimization_barrier((zs, recv))
        send = mid_x(l, core, recv, mine, swapped, c)
        yx = lax.all_to_all(send, "gx", 0, 0, tiled=True).reshape(256, RX * CH)
        yy = mid_y(me, zs, c)
        yy = [yy[0]] + [permute_y(yy[step], 0, step) for step in range(1, 4)]
        more = l + 1 < LAYERS
        got = last_call(l, more, me, yx, yy, state, expand_weight, wr, wy, c)
        if more:
            state, zx, zy = got
    return got[0][None]


def solution(mesh):
    in_specs = (
        P(None, None, "gx", "gy"),
        P(None, "gx", None, None, None),
        P(None, "gy", None, None, None),
        P(),
        P(),
    )
    out_specs = P(None, None, "gx", "gy")
    return jax.shard_map(body, mesh=mesh, in_specs=in_specs, out_specs=out_specs, check_vma=False)
```

```python
import functools

import jax
import jax.numpy as jnp
import numpy as np
from jax import lax
from jax.experimental import pallas as pl
from jax.experimental.pallas import tpu as pltpu
from jax.sharding import PartitionSpec as P

F32 = jnp.float32
BF16 = jnp.bfloat16
NX = 2048
NY = 2048
CH = 64
HID = 256
MODES = 32
LAYERS = 2
RX = 10
RY = 20
RYP = 24
ROWS = RYP + 32
GROUP = 16
WIDE = GROUP * CH
LAST_GROUPS = (64, 16)
EARLY = 5
LINE = 8


def window_tables(length, devices, rank):
    window = length // devices
    k = np.arange(MODES)[:, None]
    p = np.arange(length)[None, :]
    angle = 2.0 * np.pi * ((k * p) % length) / length
    scale = 1.0 / np.sqrt(length)
    weight = np.where(np.arange(MODES) == 0, 1.0, 2.0)[:, None]
    forward = np.concatenate([np.cos(angle), -np.sin(angle)], 0) * scale
    inverse = np.concatenate([weight * np.cos(angle), -weight * np.sin(angle)], 0) * scale
    _, _, vt = np.linalg.svd(forward[:, :window], full_matrices=False)
    basis = vt[:rank]
    basis = basis * np.sign(basis[np.arange(rank), np.abs(basis).argmax(1)])[:, None]
    fwd = np.stack([forward[:, d * window : (d + 1) * window] @ basis.T for d in range(devices)])
    inv = np.stack([inverse[:, d * window : (d + 1) * window] @ basis.T for d in range(devices)])
    return basis, fwd, inv


SHIFTS = ((1, 0), (0, 1), (0, 3), (1, 2), (0, 2), (1, 1), (1, 3))
QUARTER = 16 * 64


def moved(me, flip, step):
    return (me // 4 ^ flip) * 4 + (me + step) % 4


def bf(x):
    return np.asarray(x, np.float32).astype(jnp.bfloat16)


def make_constants():
    bx, fx, ix = window_tables(NX, 32, RX)
    by, fy, iy = window_tables(NY, 8, RY)
    pairs = RX // 2
    ax = fx.reshape(32, 64, pairs, 2).transpose(3, 1, 2, 0).reshape(128, pairs * 32)
    gx = ix.reshape(32, 2, MODES, pairs, 2)
    u0 = gx[..., 0].transpose(3, 0, 1, 2).reshape(pairs * 32, 64)
    u1 = gx[..., 1].transpose(3, 0, 1, 2)[:, :, ::-1].reshape(pairs * 32, 64)
    mid_x = np.zeros((128 + pairs * 32, 256))
    mid_x[:128, : pairs * 32] = ax
    mid_x[128:, :64] = u0
    mid_x[128:, 64:128] = u1
    mid_y = np.zeros((2, 8, RYP, 128))
    mid_y[0, :, :RY, :64] = fy.transpose(0, 2, 1)
    mid_y[1, :, :RY, :64] = iy.transpose(0, 2, 1)
    cy = np.pad(by, ((0, RYP - RY), (0, 0)))
    bx = np.pad(bx, ((0, 16 - RX), (0, 128 - 64)))
    return dict(mid_x=bf(mid_x), mid_y=bf(mid_y), cy=bf(cy), bx=bf(bx))


def dot(a, b):
    return jnp.dot(a, b, preferred_element_type=F32)


def dot_nt(a, b):
    return lax.dot_general(a, b, (((1,), (1,)), ((), ())), preferred_element_type=F32)


def half_mask(rows):
    return lax.broadcasted_iota(jnp.int32, (rows, 128), 1) < 64


def dot_tn(a, b):
    return lax.dot_general(a, b, (((0,), (0,)), ((), ())), preferred_element_type=F32)


def estimate(us):
    return pl.CostEstimate(flops=int(us * 1e9), bytes_accessed=1 << 20, transcendentals=0)


def params(mib):
    return pltpu.CompilerParams(vmem_limit_bytes=mib << 20)


def fill_kron(bx_ref, kron_ref):
    wide = kron_ref.shape[1]
    lanes = lax.broadcasted_iota(jnp.int32, (CH, wide), 1)
    rows = lax.broadcasted_iota(jnp.int32, (CH, wide), 0)
    eye = (lanes % CH) == rows
    x = (lax.broadcasted_iota(jnp.int32, (128, wide), 1) + wide * pl.program_id(0)) // CH
    position = lax.broadcasted_iota(jnp.int32, (128, wide), 0)
    spread = dot(bx_ref[...], jnp.where(x == position, 1.0, 0.0).astype(BF16))
    for r in range(RX):
        row = jnp.broadcast_to(spread[r : r + 1, :], (CH, wide))
        kron_ref[r * CH : (r + 1) * CH, :] = jnp.where(eye, row, 0.0).astype(BF16)


def coefficients(g, state, kron_ref, cy_ref, wy_ref, acc_ref, zx_ref, zy_ref):
    part = dot_nt(state, kron_ref[...])

    @pl.when(g == 0)
    def _():
        acc_ref[...] = part

    @pl.when(g > 0)
    def _():
        acc_ref[...] += part

    for q in range(zy_ref.shape[0]):
        part = state[:, q * QUARTER : (q + 1) * QUARTER]
        zy_ref[q, :RYP] = dot(cy_ref[...], part).astype(BF16)
        zy_ref[q, RYP:] = wy_ref[0]

    @pl.when(g == pl.num_programs(0) - 1)
    def _():
        zx_ref[...] = acc_ref[...].astype(BF16)


def first_kernel(
    field_ref, bx_ref, cy_ref, wy_ref, state_ref, zx_ref, zy_ref, t_ref, kron_ref, acc_ref
):
    for h in range(2):
        part = field_ref[:, :, h * 128 : (h + 1) * 128].astype(F32)
        t_ref[h] = part.reshape(CH * GROUP, 128)
    for h in range(2):
        for p in range(GROUP // 2):
            two = [t_ref[h, pl.ds(2 * p + j, CH, stride=GROUP), :] for j in range(2)]
            block = jnp.concatenate(two, axis=0).T.astype(BF16)
            state_ref[h * 128 : (h + 1) * 128, p * 128 : (p + 1) * 128] = block
    fill_kron(bx_ref, kron_ref)
    g = pl.program_id(0)
    coefficients(g, state_ref[...], kron_ref, cy_ref, wy_ref, acc_ref, zx_ref, zy_ref)


def first_call(field, wy, c):
    return pl.pallas_call(
        first_kernel,
        name="first",
        grid=(64 // GROUP,),
        in_specs=[
            pl.BlockSpec((CH, GROUP, 256), lambda g: (0, g, 0)),
            pl.BlockSpec((16, 128), lambda g: (0, 0)),
            pl.BlockSpec((RYP, 256), lambda g: (0, 0)),
            pl.BlockSpec((1, ROWS - RYP, QUARTER), lambda g: (0, 0, 0)),
        ],
        out_specs=[
            pl.BlockSpec((256, WIDE), lambda g: (0, g)),
            pl.BlockSpec((256, RX * CH), lambda g: (0, 0)),
            pl.BlockSpec((1, ROWS, WIDE), lambda g: (g, 0, 0)),
        ],
        out_shape=[
            jax.ShapeDtypeStruct((256, 4096), BF16),
            jax.ShapeDtypeStruct((256, RX * CH), BF16),
            jax.ShapeDtypeStruct((4, ROWS, QUARTER), BF16),
        ],
        scratch_shapes=[
            pltpu.VMEM((2, CH * GROUP, 128), F32),
            pltpu.VMEM((RX * CH, WIDE), BF16),
            pltpu.VMEM((256, RX * CH), F32),
        ],
        compiler_params=params(36),
        cost_estimate=estimate(10),
    )(field, c["bx"], c["cy"], wy)


def mode_weights(w, sign):
    w = w.astype(F32)
    return jnp.concatenate([w * sign, pltpu.roll(w, 64, 1)], axis=0).astype(BF16)


def mix(xs_ref, ms_ref, lines, steps, unroll, weights):
    sign = jnp.where(half_mask(CH), 1.0, -1.0)

    def product(i, _):
        for mode, w in weights(i):
            rows = pl.ds(pl.multiple_of(mode * lines, lines), lines)
            ms_ref[rows, :] = dot_nt(xs_ref[rows, :].astype(BF16), mode_weights(w, sign))

    lax.fori_loop(0, steps, product, None, unroll=unroll)


def mid_x_kernel(
    core_ref, recv_ref, w0_ref, w1_ref, tab_ref, *refs
):
    send_ref, r_ref, xs_ref, ms_ref, o_ref = refs
    pairs = RX // 2
    first = half_mask(MODES)
    for p in range(pairs):
        part = recv_ref[:, :, p * 128 : (p + 1) * 128]
        r_ref[p] = part.reshape(256, 128).astype(F32)
    cols = []
    for y in range(LINE):
        ry = [r_ref[p, pl.ds(y, 32, stride=LINE), :] for p in range(pairs)]
        cols.append(jnp.concatenate(ry, axis=0).astype(BF16))
    spec = dot(tab_ref[:128, : pairs * 32], jnp.concatenate(cols, axis=1))
    for y in range(LINE):
        s = spec[:, y * 128 : (y + 1) * 128]
        x = jnp.where(first, s[0:32], s[96:128])
        x = x + pltpu.roll(jnp.where(first, s[32:64], s[64:96]), 64, 1)
        xs_ref[pl.ds(y, MODES, stride=LINE), :] = x
    core = core_ref[0]
    weights = lambda t: [(t * 2 + core, w0_ref[t, 0]), (t * 2 + 1 - core, w1_ref[t, 0])]
    mix(xs_ref, ms_ref, LINE, 16, 8, weights)
    cols = []
    for y in range(LINE):
        m = ms_ref[pl.ds(y, MODES, stride=LINE), :]
        cols.append(jnp.concatenate([m, pltpu.roll(m, 64, 1)], axis=0).astype(BF16))
    cols = jnp.concatenate(cols, axis=1)
    out0 = dot(tab_ref[128:, :64], cols)
    out1 = dot(tab_ref[128:, 64:128], cols)
    for y in range(LINE):
        for p in range(pairs):
            v0 = out0[p * 32 : (p + 1) * 32, y * 128 : (y + 1) * 128]
            v1 = out1[p * 32 : (p + 1) * 32, y * 128 : (y + 1) * 128]
            o_ref[p, pl.ds(y, 32, stride=LINE), :] = jnp.where(first, v0, v1)
    for p in range(pairs):
        part = o_ref[p].reshape(32, LINE, 128).astype(BF16)
        send_ref[:, :, p * 128 : (p + 1) * 128] = part


def whole(a):
    return pl.BlockSpec(a.shape, lambda *_: (0,) * a.ndim)


def mid_x(layer, core, recv, w0, w1, c):
    weights = pl.BlockSpec((16, 1, CH, 128), lambda i: (0, layer, 0, 0))
    return pl.pallas_call(
        mid_x_kernel,
        name="mid_x",
        grid=(1,),
        in_specs=[pl.BlockSpec(memory_space=pltpu.SMEM)]
        + [whole(recv), weights, weights, whole(c["mid_x"])],
        out_specs=whole(recv),
        out_shape=jax.ShapeDtypeStruct(recv.shape, BF16),
        scratch_shapes=[
            pltpu.VMEM((RX // 2, 256, 128), F32),
            pltpu.VMEM((MODES * LINE, 128), F32),
            pltpu.VMEM((MODES * LINE, 128), F32),
            pltpu.VMEM((RX // 2, 256, 128), F32),
        ],
        compiler_params=params(16),
        cost_estimate=estimate(3),
    )(core, recv, w0, w1, c["mid_x"])


def mid_y_kernel(me_ref, *refs):
    z_refs, tab_ref, out_refs = refs[:8], refs[8], refs[9:13]
    xs_ref, ms_ref, w_ref = refs[13:]
    first = half_mask(MODES)
    lines = 16
    half, quarter = me_ref[0] // 4, lax.rem(me_ref[0], 4)
    sources = []
    for flip, step in ((0, 0),) + SHIFTS:
        near = half + flip - 2 * flip * half
        sources.append(near * 4 + lax.rem(quarter + 4 - step, 4))
    table = [tab_ref[0, src].astype(F32) for src in sources]
    forward = jnp.concatenate(table, axis=0).T[:64].astype(BF16)
    table = [tab_ref[1, half * 4 + lax.rem(quarter + step, 4)].astype(F32) for step in range(4)]
    inverse = jnp.concatenate(table, axis=0)[:, :64].astype(BF16)
    for g in range(2):
        z = [ref[:RYP, g * 512 : (g + 1) * 512].astype(F32) for ref in z_refs]
        z = jnp.concatenate(z, axis=0).astype(BF16)
        spec = dot(forward, z)
        for b in range(4):
            re = spec[0:32, b * 128 : (b + 1) * 128]
            im = spec[32:64, b * 128 : (b + 1) * 128]
            line = g * 8 + 2 * b
            xs_ref[pl.ds(line, MODES, stride=lines), :] = jnp.where(
                first, re, pltpu.roll(im, 64, 1)
            )
            xs_ref[pl.ds(line + 1, MODES, stride=lines), :] = jnp.where(
                first, pltpu.roll(re, 64, 1), im
            )
    for ref, src in zip(z_refs, sources):
        packed = ref[RYP:, :].astype(F32)
        for j in range(4):
            tiles = [packed[j * 8 : (j + 1) * 8, t * 128 : (t + 1) * 128] for t in range(8)]
            w_ref[src, j] = jnp.concatenate(tiles, axis=0).astype(BF16)
    weights = lambda src: [(src * 4 + j, w_ref[src, j]) for j in range(4)]
    mix(xs_ref, ms_ref, lines, 8, 4, weights)
    for g in range(2):
        cols = []
        for b in range(4):
            line = g * 8 + 2 * b
            m0 = ms_ref[pl.ds(line, MODES, stride=lines), :]
            m1 = ms_ref[pl.ds(line + 1, MODES, stride=lines), :]
            re = jnp.where(first, m0, pltpu.roll(m1, 64, 1))
            im = jnp.where(first, pltpu.roll(m0, 64, 1), m1)
            cols.append(jnp.concatenate([re, im], axis=0).astype(BF16))
        out = dot(inverse, jnp.concatenate(cols, axis=1)).astype(BF16)
        for step in range(4):
            out_refs[step][:, g * 512 : (g + 1) * 512] = out[step * RYP : (step + 1) * RYP]


def mid_y(me, zs, c):
    return pl.pallas_call(
        mid_y_kernel,
        name="mid_y",
        grid=(1,),
        in_specs=[pl.BlockSpec(memory_space=pltpu.SMEM)]
        + [whole(z) for z in zs]
        + [whole(c["mid_y"])],
        out_specs=[pl.BlockSpec((RYP, QUARTER), lambda i: (0, 0))] * 4,
        scratch_shapes=[pltpu.VMEM((MODES * 16, 128), F32)] * 2
        + [pltpu.VMEM((8, 4, CH, 128), BF16)],
        out_shape=[jax.ShapeDtypeStruct((RYP, QUARTER), BF16)] * 4,
        compiler_params=params(20),
        cost_estimate=estimate(2),
    )(me, *zs, c["mid_y"])


def gelu(x):
    x = x.astype(BF16)
    inner = x * (0.7978845608028654 + 0.035677408136300125 * (x * x))
    half = 0.5 * x
    return half + half * jnp.tanh(inner)


def last_kernel(more, group, *refs):
    me_ref, yx_ref, bx_ref = refs[:3]
    yy_refs = refs[3:7]
    cy_ref, state_ref, we_ref, wr_ref = refs[7:11]
    if more:
        wy_ref, out_ref, zx_ref, zy_ref, kron_ref, we4_ref, wr4_ref, yy_ref, acc_ref = refs[11:]
    else:
        out_ref, kron_ref, we4_ref, wr4_ref, yy_ref, t_ref = refs[11:]
    g = pl.program_id(0)

    @pl.when(g == 0)
    def _():
        we4_ref[...] = jnp.zeros_like(we4_ref)
        wr4_ref[...] = jnp.zeros_like(wr4_ref)
        for j in range(4):
            we4_ref[j * CH : (j + 1) * CH, j * HID : (j + 1) * HID] = we_ref[0]
            wr4_ref[j * CH : (j + 1) * CH, j * HID : (j + 1) * HID] = wr_ref[0]
        for step in range(4):
            yy_ref[lax.rem(me_ref[0] + 4 - step, 4)] = yy_refs[step][...]

    fill_kron(bx_ref, kron_ref)
    basis = cy_ref[...].astype(F32).T.astype(BF16)
    for j in range(group // 4):
        lanes = slice(j * 256, (j + 1) * 256)
        if j % 2 == 0:
            both = slice(j * 256, (j + 2) * 256)
            yy = yy_ref[g * (group // 16) + j // 4, :, j % 4 * 256 : (j % 4 + 2) * 256]
            total = dot(yx_ref[...], kron_ref[:, both]) + dot(basis, yy)
            total = total.astype(BF16)
            total = jnp.concatenate([total[:, :256], total[:, 256:]], axis=0)
            hidden = gelu(dot(total, we4_ref[...])).astype(BF16)
            updates = dot_nt(hidden, wr4_ref[...])
        update = updates[(j % 2) * 256 : (j % 2 + 1) * 256]
        new = state_ref[:, lanes].astype(F32) + update
        if more:
            out_ref[:, lanes] = new.astype(BF16)
            continue
        for h in range(2):
            for p in range(2):
                block = new[h * 128 : (h + 1) * 128, p * 128 : (p + 1) * 128].T
                x = j * 4 + p * 2
                t_ref[h, pl.ds(x, CH, stride=group), :] = block[:CH]
                t_ref[h, pl.ds(x + 1, CH, stride=group), :] = block[CH:]
    if more:
        coefficients(g, out_ref[...], kron_ref, cy_ref, wy_ref, acc_ref, zx_ref, zy_ref)
    else:
        for h in range(2):
            part = t_ref[h].reshape(CH, group, 128).astype(BF16)
            out_ref[:, :, h * 128 : (h + 1) * 128] = part


def last_call(layer, more, me, yx, yy, state, we, wr, wy, c):
    group = LAST_GROUPS[layer]
    wide = group * CH
    in_specs = [
        pl.BlockSpec(memory_space=pltpu.SMEM),
        pl.BlockSpec((256, RX * CH), lambda g: (0, 0)),
        pl.BlockSpec((16, 128), lambda g: (0, 0)),
        *[pl.BlockSpec((RYP, QUARTER), lambda g: (0, 0))] * 4,
        pl.BlockSpec((RYP, 256), lambda g: (0, 0)),
        pl.BlockSpec((256, wide), lambda g: (0, g)),
        pl.BlockSpec((1, CH, HID), lambda g: (layer, 0, 0)),
        pl.BlockSpec((1, CH, HID), lambda g: (layer, 0, 0)),
    ]
    scratch = [pltpu.VMEM((RX * CH, wide), BF16)] + [pltpu.VMEM((256, 1024), BF16)] * 2
    scratch.append(pltpu.VMEM((4, RYP, QUARTER), BF16))
    args = [me, yx, c["bx"], *yy, c["cy"], state, we, wr]
    if more:
        in_specs.append(
            pl.BlockSpec((1, ROWS - RYP, QUARTER), lambda g: (layer + 1, 0, 0))
        )
        args.append(wy)
        out_specs = [
            pl.BlockSpec((256, wide), lambda g: (0, g)),
            pl.BlockSpec((256, RX * CH), lambda g: (0, 0)),
            pl.BlockSpec((group // 16, ROWS, QUARTER), lambda g: (g, 0, 0)),
        ]
        out_shape = [
            jax.ShapeDtypeStruct((256, 4096), BF16),
            jax.ShapeDtypeStruct((256, RX * CH), BF16),
            jax.ShapeDtypeStruct((4, ROWS, QUARTER), BF16),
        ]
        scratch.append(pltpu.VMEM((256, RX * CH), F32))
    else:
        out_specs = [pl.BlockSpec((CH, group, 256), lambda g: (0, g, 0))]
        out_shape = [jax.ShapeDtypeStruct((CH, 64, 256), BF16)]
        scratch.append(pltpu.VMEM((2, CH * group, 128), F32))
    return pl.pallas_call(
        functools.partial(last_kernel, more, group),
        name="last",
        grid=(64 // group,),
        in_specs=in_specs,
        out_specs=out_specs,
        out_shape=out_shape,
        scratch_shapes=scratch,
        compiler_params=params(40),
        cost_estimate=estimate(12),
    )(*args)


def pack_kernel(wx_ref, wy_ref, x_ref, y_ref):
    def join(parts):
        return jnp.concatenate([part.astype(F32) for part in parts], axis=1)

    for layer in range(LAYERS):
        own = join([wx_ref[layer, 0, i] for i in range(2)]).astype(BF16)
        for i in range(16):
            x_ref[i, layer] = own
        rows = []
        for j in range(4):
            own = join([wy_ref[layer, j, i] for i in range(2)])
            rows.append(join([own[t * 8 : (t + 1) * 8] for t in range(8)]))
        y_ref[layer] = jnp.concatenate(rows, axis=0).astype(BF16)


def pack_call(spectral_x, spectral_y):
    shapes = (16, LAYERS, CH, 128), (LAYERS, ROWS - RYP, QUARTER)
    out_shape = [jax.ShapeDtypeStruct(shape, BF16) for shape in shapes]
    return pl.pallas_call(
        pack_kernel,
        name="pack",
        grid=(1,),
        in_specs=[whole(spectral_x), whole(spectral_y)],
        out_specs=[whole(a) for a in out_shape],
        out_shape=out_shape,
        compiler_params=params(16),
        cost_estimate=estimate(2),
    )(spectral_x, spectral_y)


def swap_cores(x):
    return lax.ppermute(x, "gx", [(i, i ^ 1) for i in range(32)])


def permute_y(x, flip, step):
    return lax.ppermute(x, "gy", [(i, moved(i, flip, step)) for i in range(8)])


def body(state_field, spectral_x, spectral_y, expand_weight, reduce_weight):
    c = {name: jnp.asarray(value) for name, value in make_constants().items()}
    core = lax.rem(lax.axis_index("gx"), 2).reshape(1).astype(jnp.int32)
    me = lax.axis_index("gy").reshape(1).astype(jnp.int32)
    own_x, wy = pack_call(spectral_x, spectral_y)
    same_core = [list(range(s, 32, 2)) for s in range(2)]
    mine = lax.all_to_all(own_x, "gx", 0, 0, axis_index_groups=same_core, tiled=True)
    swapped = swap_cores(mine)
    wr = jnp.swapaxes(reduce_weight, 1, 2)
    state, zx, zy = first_call(state_field[0], wy, c)
    for l in range(LAYERS):
        state = pltpu.with_memory_space_constraint(state, pltpu.HBM)
        zs = []
        for flip, step in ((0, 0),) + SHIFTS:
            chunk = lax.dynamic_slice_in_dim(zy, lax.rem(me[0] + step, 4), 1, 0)[0]
            zs.append(permute_y(chunk, flip, step) if flip or step else chunk)
        if l == 0:
            zx, early = lax.optimization_barrier((zx, zs[:EARLY]))
            zs = early + zs[EARLY:]
        recv = lax.all_to_all(zx.reshape(32, LINE, RX * CH), "gx", 0, 0, tiled=True)
        zs, recv = lax.optimization_barrier((zs, recv))
        send = mid_x(l, core, recv, mine, swapped, c)
        yx = lax.all_to_all(send, "gx", 0, 0, tiled=True).reshape(256, RX * CH)
        yy = mid_y(me, zs, c)
        yy = [yy[0]] + [permute_y(yy[step], 0, step) for step in range(1, 4)]
        more = l + 1 < LAYERS
        got = last_call(l, more, me, yx, yy, state, expand_weight, wr, wy, c)
        if more:
            state, zx, zy = got
    return got[0][None]


def solution(mesh):
    in_specs = (
        P(None, None, "gx", "gy"),
        P(None, "gx", None, None, None),
        P(None, "gy", None, None, None),
        P(),
        P(),
    )
    out_specs = P(None, None, "gx", "gy")
    return jax.shard_map(body, mesh=mesh, in_specs=in_specs, out_specs=out_specs, check_vma=False)
```

```python
import functools

import jax
import jax.numpy as jnp
import numpy as np
from jax import lax
from jax.experimental import pallas as pl
from jax.experimental.pallas import tpu as pltpu
from jax.sharding import PartitionSpec as P

F32 = jnp.float32
BF16 = jnp.bfloat16
NX = 2048
NY = 2048
CH = 64
HID = 256
MODES = 32
LAYERS = 2
RX = 10
RY = 20
RYP = 24
ROWS = RYP + 32
GROUP = 16
WIDE = GROUP * CH
LAST_GROUPS = (64, 16)
EARLY = 5
LINE = 8


def window_tables(length, devices, rank):
    window = length // devices
    k = np.arange(MODES)[:, None]
    p = np.arange(length)[None, :]
    angle = 2.0 * np.pi * ((k * p) % length) / length
    scale = 1.0 / np.sqrt(length)
    weight = np.where(np.arange(MODES) == 0, 1.0, 2.0)[:, None]
    forward = np.concatenate([np.cos(angle), -np.sin(angle)], 0) * scale
    inverse = np.concatenate([weight * np.cos(angle), -weight * np.sin(angle)], 0) * scale
    _, _, vt = np.linalg.svd(forward[:, :window], full_matrices=False)
    basis = vt[:rank]
    basis = basis * np.sign(basis[np.arange(rank), np.abs(basis).argmax(1)])[:, None]
    fwd = np.stack([forward[:, d * window : (d + 1) * window] @ basis.T for d in range(devices)])
    inv = np.stack([inverse[:, d * window : (d + 1) * window] @ basis.T for d in range(devices)])
    return basis, fwd, inv


SHIFTS = ((1, 0), (0, 1), (0, 3), (1, 2), (0, 2), (1, 1), (1, 3))
QUARTER = 16 * 64


def moved(me, flip, step):
    return (me // 4 ^ flip) * 4 + (me + step) % 4


def bf(x):
    return np.asarray(x, np.float32).astype(jnp.bfloat16)


def make_constants():
    bx, fx, ix = window_tables(NX, 32, RX)
    by, fy, iy = window_tables(NY, 8, RY)
    pairs = RX // 2
    ax = fx.reshape(32, 64, pairs, 2).transpose(3, 1, 2, 0).reshape(128, pairs * 32)
    gx = ix.reshape(32, 2, MODES, pairs, 2)
    u0 = gx[..., 0].transpose(3, 0, 1, 2).reshape(pairs * 32, 64)
    u1 = gx[..., 1].transpose(3, 0, 1, 2)[:, :, ::-1].reshape(pairs * 32, 64)
    mid_x = np.zeros((128 + pairs * 32, 256))
    mid_x[:128, : pairs * 32] = ax
    mid_x[128:, :64] = u0
    mid_x[128:, 64:128] = u1
    mid_y = np.zeros((2, 8, RYP, 128))
    mid_y[0, :, :RY, :64] = fy.transpose(0, 2, 1)
    mid_y[1, :, :RY, :64] = iy.transpose(0, 2, 1)
    cy = np.pad(by, ((0, RYP - RY), (0, 0)))
    bx = np.pad(bx, ((0, 16 - RX), (0, 128 - 64)))
    return dict(mid_x=bf(mid_x), mid_y=bf(mid_y), cy=bf(cy), bx=bf(bx))


def dot(a, b):
    return jnp.dot(a, b, preferred_element_type=F32)


def dot_nt(a, b):
    return lax.dot_general(a, b, (((1,), (1,)), ((), ())), preferred_element_type=F32)


def half_mask(rows):
    return lax.broadcasted_iota(jnp.int32, (rows, 128), 1) < 64


def dot_tn(a, b):
    return lax.dot_general(a, b, (((0,), (0,)), ((), ())), preferred_element_type=F32)


def estimate(us):
    return pl.CostEstimate(flops=int(us * 1e9), bytes_accessed=1 << 20, transcendentals=0)


def params(mib):
    return pltpu.CompilerParams(vmem_limit_bytes=mib << 20)


def fill_kron(bx_ref, kron_ref):
    wide = kron_ref.shape[1]
    lanes = lax.broadcasted_iota(jnp.int32, (CH, wide), 1)
    rows = lax.broadcasted_iota(jnp.int32, (CH, wide), 0)
    eye = (lanes % CH) == rows
    x = (lax.broadcasted_iota(jnp.int32, (128, wide), 1) + wide * pl.program_id(0)) // CH
    position = lax.broadcasted_iota(jnp.int32, (128, wide), 0)
    spread = dot(bx_ref[...], jnp.where(x == position, 1.0, 0.0).astype(BF16))
    for r in range(RX):
        row = jnp.broadcast_to(spread[r : r + 1, :], (CH, wide))
        kron_ref[r * CH : (r + 1) * CH, :] = jnp.where(eye, row, 0.0).astype(BF16)


def coefficients(g, state, kron_ref, cy_ref, wy_ref, acc_ref, zx_ref, zy_ref):
    part = dot_nt(state, kron_ref[...])

    @pl.when(g == 0)
    def _():
        acc_ref[...] = part

    @pl.when(g > 0)
    def _():
        acc_ref[...] += part

    for q in range(zy_ref.shape[0]):
        part = state[:, q * QUARTER : (q + 1) * QUARTER]
        zy_ref[q, :RYP] = dot(cy_ref[...], part).astype(BF16)
        zy_ref[q, RYP:] = wy_ref[0]

    @pl.when(g == pl.num_programs(0) - 1)
    def _():
        zx_ref[...] = acc_ref[...].astype(BF16)


def first_kernel(
    field_ref, bx_ref, cy_ref, wy_ref, state_ref, zx_ref, zy_ref, t_ref, kron_ref, acc_ref
):
    for h in range(2):
        part = field_ref[:, :, h * 128 : (h + 1) * 128].astype(F32)
        t_ref[h] = part.reshape(CH * GROUP, 128)
    for h in range(2):
        for p in range(GROUP // 2):
            two = [t_ref[h, pl.ds(2 * p + j, CH, stride=GROUP), :] for j in range(2)]
            block = jnp.concatenate(two, axis=0).T.astype(BF16)
            state_ref[h * 128 : (h + 1) * 128, p * 128 : (p + 1) * 128] = block
    fill_kron(bx_ref, kron_ref)
    g = pl.program_id(0)
    coefficients(g, state_ref[...], kron_ref, cy_ref, wy_ref, acc_ref, zx_ref, zy_ref)


def first_call(field, wy, c):
    return pl.pallas_call(
        first_kernel,
        name="first",
        grid=(64 // GROUP,),
        in_specs=[
            pl.BlockSpec((CH, GROUP, 256), lambda g: (0, g, 0)),
            pl.BlockSpec((16, 128), lambda g: (0, 0)),
            pl.BlockSpec((RYP, 256), lambda g: (0, 0)),
            pl.BlockSpec((1, ROWS - RYP, QUARTER), lambda g: (0, 0, 0)),
        ],
        out_specs=[
            pl.BlockSpec((256, WIDE), lambda g: (0, g)),
            pl.BlockSpec((256, RX * CH), lambda g: (0, 0)),
            pl.BlockSpec((1, ROWS, WIDE), lambda g: (g, 0, 0)),
        ],
        out_shape=[
            jax.ShapeDtypeStruct((256, 4096), BF16),
            jax.ShapeDtypeStruct((256, RX * CH), BF16),
            jax.ShapeDtypeStruct((4, ROWS, QUARTER), BF16),
        ],
        scratch_shapes=[
            pltpu.VMEM((2, CH * GROUP, 128), F32),
            pltpu.VMEM((RX * CH, WIDE), BF16),
            pltpu.VMEM((256, RX * CH), F32),
        ],
        compiler_params=params(36),
        cost_estimate=estimate(10),
    )(field, c["bx"], c["cy"], wy)


def mode_weights(w, sign):
    w = w.astype(F32)
    return jnp.concatenate([w * sign, pltpu.roll(w, 64, 1)], axis=0).astype(BF16)


def mix(xs_ref, ms_ref, lines, steps, unroll, weights):
    sign = jnp.where(half_mask(CH), 1.0, -1.0)

    def product(i, _):
        for mode, w in weights(i):
            rows = pl.ds(pl.multiple_of(mode * lines, lines), lines)
            ms_ref[rows, :] = dot_nt(xs_ref[rows, :].astype(BF16), mode_weights(w, sign))

    lax.fori_loop(0, steps, product, None, unroll=unroll)


def mid_x_kernel(
    core_ref, recv_ref, w0_ref, w1_ref, tab_ref, *refs
):
    send_ref, r_ref, xs_ref, ms_ref, o_ref = refs
    pairs = RX // 2
    first = half_mask(MODES)
    for p in range(pairs):
        part = recv_ref[:, :, p * 128 : (p + 1) * 128]
        r_ref[p] = part.reshape(256, 128).astype(F32)
    cols = []
    for y in range(LINE):
        ry = [r_ref[p, pl.ds(y, 32, stride=LINE), :] for p in range(pairs)]
        cols.append(jnp.concatenate(ry, axis=0).astype(BF16))
    spec = dot(tab_ref[:128, : pairs * 32], jnp.concatenate(cols, axis=1))
    for y in range(LINE):
        s = spec[:, y * 128 : (y + 1) * 128]
        x = jnp.where(first, s[0:32], s[96:128])
        x = x + pltpu.roll(jnp.where(first, s[32:64], s[64:96]), 64, 1)
        xs_ref[pl.ds(y, MODES, stride=LINE), :] = x
    core = core_ref[0]
    weights = lambda t: [(t * 2 + core, w0_ref[t, 0]), (t * 2 + 1 - core, w1_ref[t, 0])]
    mix(xs_ref, ms_ref, LINE, 16, 8, weights)
    cols = []
    for y in range(LINE):
        m = ms_ref[pl.ds(y, MODES, stride=LINE), :]
        cols.append(jnp.concatenate([m, pltpu.roll(m, 64, 1)], axis=0).astype(BF16))
    cols = jnp.concatenate(cols, axis=1)
    out0 = dot(tab_ref[128:, :64], cols)
    out1 = dot(tab_ref[128:, 64:128], cols)
    for y in range(LINE):
        for p in range(pairs):
            v0 = out0[p * 32 : (p + 1) * 32, y * 128 : (y + 1) * 128]
            v1 = out1[p * 32 : (p + 1) * 32, y * 128 : (y + 1) * 128]
            o_ref[p, pl.ds(y, 32, stride=LINE), :] = jnp.where(first, v0, v1)
    for p in range(pairs):
        part = o_ref[p].reshape(32, LINE, 128).astype(BF16)
        send_ref[:, :, p * 128 : (p + 1) * 128] = part


def whole(a):
    return pl.BlockSpec(a.shape, lambda *_: (0,) * a.ndim)


def mid_x(layer, core, recv, w0, w1, c):
    weights = pl.BlockSpec((16, 1, CH, 128), lambda i: (0, layer, 0, 0))
    return pl.pallas_call(
        mid_x_kernel,
        name="mid_x",
        grid=(1,),
        in_specs=[pl.BlockSpec(memory_space=pltpu.SMEM)]
        + [whole(recv), weights, weights, whole(c["mid_x"])],
        out_specs=whole(recv),
        out_shape=jax.ShapeDtypeStruct(recv.shape, BF16),
        scratch_shapes=[
            pltpu.VMEM((RX // 2, 256, 128), F32),
            pltpu.VMEM((MODES * LINE, 128), F32),
            pltpu.VMEM((MODES * LINE, 128), F32),
            pltpu.VMEM((RX // 2, 256, 128), F32),
        ],
        compiler_params=params(16),
        cost_estimate=estimate(3),
    )(core, recv, w0, w1, c["mid_x"])


def mid_y_kernel(me_ref, *refs):
    z_refs, tab_ref, out_refs = refs[:8], refs[8], refs[9:13]
    xs_ref, ms_ref, w_ref = refs[13:]
    first = half_mask(MODES)
    lines = 16
    half, quarter = me_ref[0] // 4, lax.rem(me_ref[0], 4)
    sources = []
    for flip, step in ((0, 0),) + SHIFTS:
        near = half + flip - 2 * flip * half
        sources.append(near * 4 + lax.rem(quarter + 4 - step, 4))
    table = [tab_ref[0, src].astype(F32) for src in sources]
    forward = jnp.concatenate(table, axis=0).T[:64].astype(BF16)
    table = [tab_ref[1, half * 4 + lax.rem(quarter + step, 4)].astype(F32) for step in range(4)]
    inverse = jnp.concatenate(table, axis=0)[:, :64].astype(BF16)
    for g in range(2):
        z = [ref[:RYP, g * 512 : (g + 1) * 512].astype(F32) for ref in z_refs]
        z = jnp.concatenate(z, axis=0).astype(BF16)
        spec = dot(forward, z)
        for b in range(4):
            re = spec[0:32, b * 128 : (b + 1) * 128]
            im = spec[32:64, b * 128 : (b + 1) * 128]
            line = g * 8 + 2 * b
            xs_ref[pl.ds(line, MODES, stride=lines), :] = jnp.where(
                first, re, pltpu.roll(im, 64, 1)
            )
            xs_ref[pl.ds(line + 1, MODES, stride=lines), :] = jnp.where(
                first, pltpu.roll(re, 64, 1), im
            )
    for ref, src in zip(z_refs, sources):
        packed = ref[RYP:, :].astype(F32)
        for j in range(4):
            tiles = [packed[j * 8 : (j + 1) * 8, t * 128 : (t + 1) * 128] for t in range(8)]
            w_ref[src, j] = jnp.concatenate(tiles, axis=0).astype(BF16)
    weights = lambda src: [(src * 4 + j, w_ref[src, j]) for j in range(4)]
    mix(xs_ref, ms_ref, lines, 8, 4, weights)
    for g in range(2):
        cols = []
        for b in range(4):
            line = g * 8 + 2 * b
            m0 = ms_ref[pl.ds(line, MODES, stride=lines), :]
            m1 = ms_ref[pl.ds(line + 1, MODES, stride=lines), :]
            re = jnp.where(first, m0, pltpu.roll(m1, 64, 1))
            im = jnp.where(first, pltpu.roll(m0, 64, 1), m1)
            cols.append(jnp.concatenate([re, im], axis=0).astype(BF16))
        out = dot(inverse, jnp.concatenate(cols, axis=1)).astype(BF16)
        for step in range(4):
            out_refs[step][:, g * 512 : (g + 1) * 512] = out[step * RYP : (step + 1) * RYP]


def mid_y(me, zs, c):
    return pl.pallas_call(
        mid_y_kernel,
        name="mid_y",
        grid=(1,),
        in_specs=[pl.BlockSpec(memory_space=pltpu.SMEM)]
        + [whole(z) for z in zs]
        + [whole(c["mid_y"])],
        out_specs=[pl.BlockSpec((RYP, QUARTER), lambda i: (0, 0))] * 4,
        scratch_shapes=[pltpu.VMEM((MODES * 16, 128), F32)] * 2
        + [pltpu.VMEM((8, 4, CH, 128), BF16)],
        out_shape=[jax.ShapeDtypeStruct((RYP, QUARTER), BF16)] * 4,
        compiler_params=params(20),
        cost_estimate=estimate(2),
    )(me, *zs, c["mid_y"])


def gelu(x):
    x = x.astype(BF16)
    inner = x * (0.7978845608028654 + 0.035677408136300125 * (x * x))
    half = 0.5 * x
    return half + half * jnp.tanh(inner)


def last_kernel(more, group, *refs):
    me_ref, yx_ref, bx_ref = refs[:3]
    yy_refs = refs[3:7]
    cy_ref, state_ref, we_ref, wr_ref = refs[7:11]
    if more:
        wy_ref, out_ref, zx_ref, zy_ref, kron_ref, we4_ref, wr4_ref, yy_ref, acc_ref = refs[11:]
    else:
        out_ref, kron_ref, we4_ref, wr4_ref, yy_ref, t_ref = refs[11:]
    g = pl.program_id(0)

    @pl.when(g == 0)
    def _():
        we4_ref[...] = jnp.zeros_like(we4_ref)
        wr4_ref[...] = jnp.zeros_like(wr4_ref)
        for j in range(4):
            we4_ref[j * CH : (j + 1) * CH, j * HID : (j + 1) * HID] = we_ref[0]
            wr4_ref[j * CH : (j + 1) * CH, j * HID : (j + 1) * HID] = wr_ref[0]
        for step in range(4):
            yy_ref[lax.rem(me_ref[0] + 4 - step, 4)] = yy_refs[step][...]

    fill_kron(bx_ref, kron_ref)
    basis = cy_ref[...].astype(F32).T.astype(BF16)
    for j in range(group // 4):
        lanes = slice(j * 256, (j + 1) * 256)
        if j % 2 == 0:
            both = slice(j * 256, (j + 2) * 256)
            yy = yy_ref[g * (group // 16) + j // 4, :, j % 4 * 256 : (j % 4 + 2) * 256]
            total = dot(yx_ref[...], kron_ref[:, both]) + dot(basis, yy)
            total = total.astype(BF16)
            total = jnp.concatenate([total[:, :256], total[:, 256:]], axis=0)
            hidden = gelu(dot(total, we4_ref[...])).astype(BF16)
            updates = dot_nt(hidden, wr4_ref[...])
        update = updates[(j % 2) * 256 : (j % 2 + 1) * 256]
        new = state_ref[:, lanes].astype(F32) + update
        if more:
            out_ref[:, lanes] = new.astype(BF16)
            continue
        for h in range(2):
            for p in range(2):
                block = new[h * 128 : (h + 1) * 128, p * 128 : (p + 1) * 128].T
                x = j * 4 + p * 2
                t_ref[h, pl.ds(x, CH, stride=group), :] = block[:CH]
                t_ref[h, pl.ds(x + 1, CH, stride=group), :] = block[CH:]
    if more:
        coefficients(g, out_ref[...], kron_ref, cy_ref, wy_ref, acc_ref, zx_ref, zy_ref)
    else:
        for h in range(2):
            part = t_ref[h].reshape(CH, group, 128).astype(BF16)
            out_ref[:, :, h * 128 : (h + 1) * 128] = part


def last_call(layer, more, me, yx, yy, state, we, wr, wy, c):
    group = LAST_GROUPS[layer]
    wide = group * CH
    in_specs = [
        pl.BlockSpec(memory_space=pltpu.SMEM),
        pl.BlockSpec((256, RX * CH), lambda g: (0, 0)),
        pl.BlockSpec((16, 128), lambda g: (0, 0)),
        *[pl.BlockSpec((RYP, QUARTER), lambda g: (0, 0))] * 4,
        pl.BlockSpec((RYP, 256), lambda g: (0, 0)),
        pl.BlockSpec((256, wide), lambda g: (0, g)),
        pl.BlockSpec((1, CH, HID), lambda g: (layer, 0, 0)),
        pl.BlockSpec((1, CH, HID), lambda g: (layer, 0, 0)),
    ]
    scratch = [pltpu.VMEM((RX * CH, wide), BF16)] + [pltpu.VMEM((256, 1024), BF16)] * 2
    scratch.append(pltpu.VMEM((4, RYP, QUARTER), BF16))
    args = [me, yx, c["bx"], *yy, c["cy"], state, we, wr]
    if more:
        in_specs.append(
            pl.BlockSpec((1, ROWS - RYP, QUARTER), lambda g: (layer + 1, 0, 0))
        )
        args.append(wy)
        out_specs = [
            pl.BlockSpec((256, wide), lambda g: (0, g)),
            pl.BlockSpec((256, RX * CH), lambda g: (0, 0)),
            pl.BlockSpec((group // 16, ROWS, QUARTER), lambda g: (g, 0, 0)),
        ]
        out_shape = [
            jax.ShapeDtypeStruct((256, 4096), BF16),
            jax.ShapeDtypeStruct((256, RX * CH), BF16),
            jax.ShapeDtypeStruct((4, ROWS, QUARTER), BF16),
        ]
        scratch.append(pltpu.VMEM((256, RX * CH), F32))
    else:
        out_specs = [pl.BlockSpec((CH, group, 256), lambda g: (0, g, 0))]
        out_shape = [jax.ShapeDtypeStruct((CH, 64, 256), BF16)]
        scratch.append(pltpu.VMEM((2, CH * group, 128), F32))
    return pl.pallas_call(
        functools.partial(last_kernel, more, group),
        name="last",
        grid=(64 // group,),
        in_specs=in_specs,
        out_specs=out_specs,
        out_shape=out_shape,
        scratch_shapes=scratch,
        compiler_params=params(40),
        cost_estimate=estimate(12),
    )(*args)


def join(parts):
    return jnp.concatenate([part.astype(F32) for part in parts], axis=1)


def pack_x_kernel(w_ref, out_ref):
    for layer in range(LAYERS):
        own = join([w_ref[layer, 0, i] for i in range(2)]).astype(BF16)
        for i in range(16):
            out_ref[i, layer] = own


def pack_y_kernel(w_ref, out_ref):
    for layer in range(LAYERS):
        rows = []
        for j in range(4):
            own = join([w_ref[layer, j, i] for i in range(2)])
            rows.append(join([own[t * 8 : (t + 1) * 8] for t in range(8)]))
        out_ref[layer] = jnp.concatenate(rows, axis=0).astype(BF16)


def pack_call(kernel, name, weights, shape):
    out_shape = jax.ShapeDtypeStruct(shape, BF16)
    return pl.pallas_call(
        kernel,
        name=name,
        grid=(1,),
        in_specs=[whole(weights)],
        out_specs=whole(out_shape),
        out_shape=out_shape,
        compiler_params=params(16),
        cost_estimate=estimate(1),
    )(weights)


def swap_cores(x):
    return lax.ppermute(x, "gx", [(i, i ^ 1) for i in range(32)])


def permute_y(x, flip, step):
    return lax.ppermute(x, "gy", [(i, moved(i, flip, step)) for i in range(8)])


def body(state_field, spectral_x, spectral_y, expand_weight, reduce_weight):
    c = {name: jnp.asarray(value) for name, value in make_constants().items()}
    core = lax.rem(lax.axis_index("gx"), 2).reshape(1).astype(jnp.int32)
    me = lax.axis_index("gy").reshape(1).astype(jnp.int32)
    own_x = pack_call(pack_x_kernel, "pack_x", spectral_x, (16, LAYERS, CH, 128))
    own_x, spectral_y = lax.optimization_barrier((own_x, spectral_y))
    wy = pack_call(pack_y_kernel, "pack_y", spectral_y, (LAYERS, ROWS - RYP, QUARTER))
    same_core = [list(range(s, 32, 2)) for s in range(2)]
    mine = lax.all_to_all(own_x, "gx", 0, 0, axis_index_groups=same_core, tiled=True)
    swapped = swap_cores(mine)
    wr = jnp.swapaxes(reduce_weight, 1, 2)
    state, zx, zy = first_call(state_field[0], wy, c)
    for l in range(LAYERS):
        state = pltpu.with_memory_space_constraint(state, pltpu.HBM)
        zs = []
        for flip, step in ((0, 0),) + SHIFTS:
            chunk = lax.dynamic_slice_in_dim(zy, lax.rem(me[0] + step, 4), 1, 0)[0]
            zs.append(permute_y(chunk, flip, step) if flip or step else chunk)
        if l == 0:
            zx, early = lax.optimization_barrier((zx, zs[:EARLY]))
            zs = early + zs[EARLY:]
        recv = lax.all_to_all(zx.reshape(32, LINE, RX * CH), "gx", 0, 0, tiled=True)
        zs, recv = lax.optimization_barrier((zs, recv))
        send = mid_x(l, core, recv, mine, swapped, c)
        yx = lax.all_to_all(send, "gx", 0, 0, tiled=True).reshape(256, RX * CH)
        yy = mid_y(me, zs, c)
        yy = [yy[0]] + [permute_y(yy[step], 0, step) for step in range(1, 4)]
        more = l + 1 < LAYERS
        got = last_call(l, more, me, yx, yy, state, expand_weight, wr, wy, c)
        if more:
            state, zx, zy = got
    return got[0][None]


def solution(mesh):
    in_specs = (
        P(None, None, "gx", "gy"),
        P(None, "gx", None, None, None),
        P(None, "gy", None, None, None),
        P(),
        P(),
    )
    out_specs = P(None, None, "gx", "gy")
    return jax.shard_map(body, mesh=mesh, in_specs=in_specs, out_specs=out_specs, check_vma=False)
```

```python
import functools

import jax
import jax.numpy as jnp
import numpy as np
from jax import lax
from jax.experimental import pallas as pl
from jax.experimental.pallas import tpu as pltpu
from jax.sharding import PartitionSpec as P

F32 = jnp.float32
BF16 = jnp.bfloat16
NX = 2048
NY = 2048
CH = 64
HID = 256
MODES = 32
LAYERS = 2
RX = 10
RY = 20
RYP = 24
ROWS = RYP + 32
GROUP = 16
WIDE = GROUP * CH
LAST_GROUPS = (64, 16)
LINE = 8


def window_tables(length, devices, rank):
    window = length // devices
    k = np.arange(MODES)[:, None]
    p = np.arange(length)[None, :]
    angle = 2.0 * np.pi * ((k * p) % length) / length
    scale = 1.0 / np.sqrt(length)
    weight = np.where(np.arange(MODES) == 0, 1.0, 2.0)[:, None]
    forward = np.concatenate([np.cos(angle), -np.sin(angle)], 0) * scale
    inverse = np.concatenate([weight * np.cos(angle), -weight * np.sin(angle)], 0) * scale
    _, _, vt = np.linalg.svd(forward[:, :window], full_matrices=False)
    basis = vt[:rank]
    basis = basis * np.sign(basis[np.arange(rank), np.abs(basis).argmax(1)])[:, None]
    fwd = np.stack([forward[:, d * window : (d + 1) * window] @ basis.T for d in range(devices)])
    inv = np.stack([inverse[:, d * window : (d + 1) * window] @ basis.T for d in range(devices)])
    return basis, fwd, inv


SHIFTS = ((1, 0), (0, 1), (0, 3), (1, 2), (0, 2), (1, 1), (1, 3))
QUARTER = 16 * 64


def moved(me, flip, step):
    return (me // 4 ^ flip) * 4 + (me + step) % 4


def bf(x):
    return np.asarray(x, np.float32).astype(jnp.bfloat16)


def make_constants():
    bx, fx, ix = window_tables(NX, 32, RX)
    by, fy, iy = window_tables(NY, 8, RY)
    pairs = RX // 2
    ax = fx.reshape(32, 64, pairs, 2).transpose(3, 1, 2, 0).reshape(128, pairs * 32)
    gx = ix.reshape(32, 2, MODES, pairs, 2)
    u0 = gx[..., 0].transpose(3, 0, 1, 2).reshape(pairs * 32, 64)
    u1 = gx[..., 1].transpose(3, 0, 1, 2)[:, :, ::-1].reshape(pairs * 32, 64)
    mid_x = np.zeros((128 + pairs * 32, 256))
    mid_x[:128, : pairs * 32] = ax
    mid_x[128:, :64] = u0
    mid_x[128:, 64:128] = u1
    mid_y = np.zeros((2, 8, RYP, 128))
    mid_y[0, :, :RY, :64] = fy.transpose(0, 2, 1)
    mid_y[1, :, :RY, :64] = iy.transpose(0, 2, 1)
    cy = np.pad(by, ((0, RYP - RY), (0, 0)))
    bx = np.pad(bx, ((0, 16 - RX), (0, 128 - 64)))
    return dict(mid_x=bf(mid_x), mid_y=bf(mid_y), cy=bf(cy), bx=bf(bx))


def dot(a, b):
    return jnp.dot(a, b, preferred_element_type=F32)


def dot_nt(a, b):
    return lax.dot_general(a, b, (((1,), (1,)), ((), ())), preferred_element_type=F32)


def half_mask(rows):
    return lax.broadcasted_iota(jnp.int32, (rows, 128), 1) < 64


def dot_tn(a, b):
    return lax.dot_general(a, b, (((0,), (0,)), ((), ())), preferred_element_type=F32)


def estimate(us):
    return pl.CostEstimate(flops=int(us * 1e9), bytes_accessed=1 << 20, transcendentals=0)


def params(mib):
    return pltpu.CompilerParams(vmem_limit_bytes=mib << 20)


def fill_kron(bx_ref, kron_ref):
    wide = kron_ref.shape[1]
    lanes = lax.broadcasted_iota(jnp.int32, (CH, wide), 1)
    rows = lax.broadcasted_iota(jnp.int32, (CH, wide), 0)
    eye = (lanes % CH) == rows
    x = (lax.broadcasted_iota(jnp.int32, (128, wide), 1) + wide * pl.program_id(0)) // CH
    position = lax.broadcasted_iota(jnp.int32, (128, wide), 0)
    spread = dot(bx_ref[...], jnp.where(x == position, 1.0, 0.0).astype(BF16))
    for r in range(RX):
        row = jnp.broadcast_to(spread[r : r + 1, :], (CH, wide))
        kron_ref[r * CH : (r + 1) * CH, :] = jnp.where(eye, row, 0.0).astype(BF16)


def coefficients(g, state, kron_ref, cy_ref, wy_ref, acc_ref, zx_ref, zy_ref):
    part = dot_nt(state, kron_ref[...])

    @pl.when(g == 0)
    def _():
        acc_ref[...] = part

    @pl.when(g > 0)
    def _():
        acc_ref[...] += part

    for q in range(zy_ref.shape[0]):
        part = state[:, q * QUARTER : (q + 1) * QUARTER]
        zy_ref[q, :RYP] = dot(cy_ref[...], part).astype(BF16)
        zy_ref[q, RYP:] = wy_ref[0]

    @pl.when(g == pl.num_programs(0) - 1)
    def _():
        zx_ref[...] = acc_ref[...].astype(BF16)


def first_kernel(
    field_ref, bx_ref, cy_ref, wy_ref, state_ref, zx_ref, zy_ref, t_ref, kron_ref, acc_ref
):
    for h in range(2):
        part = field_ref[:, :, h * 128 : (h + 1) * 128].astype(F32)
        t_ref[h] = part.reshape(CH * GROUP, 128)
    for h in range(2):
        for p in range(GROUP // 2):
            two = [t_ref[h, pl.ds(2 * p + j, CH, stride=GROUP), :] for j in range(2)]
            block = jnp.concatenate(two, axis=0).T.astype(BF16)
            state_ref[h * 128 : (h + 1) * 128, p * 128 : (p + 1) * 128] = block
    fill_kron(bx_ref, kron_ref)
    g = pl.program_id(0)
    coefficients(g, state_ref[...], kron_ref, cy_ref, wy_ref, acc_ref, zx_ref, zy_ref)


def first_call(field, wy, c):
    return pl.pallas_call(
        first_kernel,
        name="first",
        grid=(64 // GROUP,),
        in_specs=[
            pl.BlockSpec((CH, GROUP, 256), lambda g: (0, g, 0)),
            pl.BlockSpec((16, 128), lambda g: (0, 0)),
            pl.BlockSpec((RYP, 256), lambda g: (0, 0)),
            pl.BlockSpec((1, ROWS - RYP, QUARTER), lambda g: (0, 0, 0)),
        ],
        out_specs=[
            pl.BlockSpec((256, WIDE), lambda g: (0, g)),
            pl.BlockSpec((256, RX * CH), lambda g: (0, 0)),
            pl.BlockSpec((1, ROWS, WIDE), lambda g: (g, 0, 0)),
        ],
        out_shape=[
            jax.ShapeDtypeStruct((256, 4096), BF16),
            jax.ShapeDtypeStruct((256, RX * CH), BF16),
            jax.ShapeDtypeStruct((4, ROWS, QUARTER), BF16),
        ],
        scratch_shapes=[
            pltpu.VMEM((2, CH * GROUP, 128), F32),
            pltpu.VMEM((RX * CH, WIDE), BF16),
            pltpu.VMEM((256, RX * CH), F32),
        ],
        compiler_params=params(36),
        cost_estimate=estimate(10),
    )(field, c["bx"], c["cy"], wy)


def mode_weights(w, sign):
    w = w.astype(F32)
    return jnp.concatenate([w * sign, pltpu.roll(w, 64, 1)], axis=0).astype(BF16)


def mix(xs_ref, ms_ref, lines, steps, unroll, weights):
    sign = jnp.where(half_mask(CH), 1.0, -1.0)

    def product(i, _):
        for mode, w in weights(i):
            rows = pl.ds(pl.multiple_of(mode * lines, lines), lines)
            ms_ref[rows, :] = dot_nt(xs_ref[rows, :].astype(BF16), mode_weights(w, sign))

    lax.fori_loop(0, steps, product, None, unroll=unroll)


def mid_x_kernel(
    core_ref, recv_ref, w0_ref, w1_ref, tab_ref, *refs
):
    send_ref, r_ref, xs_ref, ms_ref, o_ref = refs
    pairs = RX // 2
    first = half_mask(MODES)
    for p in range(pairs):
        part = recv_ref[:, :, p * 128 : (p + 1) * 128]
        r_ref[p] = part.reshape(256, 128).astype(F32)
    cols = []
    for y in range(LINE):
        ry = [r_ref[p, pl.ds(y, 32, stride=LINE), :] for p in range(pairs)]
        cols.append(jnp.concatenate(ry, axis=0).astype(BF16))
    spec = dot(tab_ref[:128, : pairs * 32], jnp.concatenate(cols, axis=1))
    for y in range(LINE):
        s = spec[:, y * 128 : (y + 1) * 128]
        x = jnp.where(first, s[0:32], s[96:128])
        x = x + pltpu.roll(jnp.where(first, s[32:64], s[64:96]), 64, 1)
        xs_ref[pl.ds(y, MODES, stride=LINE), :] = x
    core = core_ref[0]
    weights = lambda t: [(t * 2 + core, w0_ref[t, 0]), (t * 2 + 1 - core, w1_ref[t, 0])]
    mix(xs_ref, ms_ref, LINE, 16, 8, weights)
    cols = []
    for y in range(LINE):
        m = ms_ref[pl.ds(y, MODES, stride=LINE), :]
        cols.append(jnp.concatenate([m, pltpu.roll(m, 64, 1)], axis=0).astype(BF16))
    cols = jnp.concatenate(cols, axis=1)
    out0 = dot(tab_ref[128:, :64], cols)
    out1 = dot(tab_ref[128:, 64:128], cols)
    for y in range(LINE):
        for p in range(pairs):
            v0 = out0[p * 32 : (p + 1) * 32, y * 128 : (y + 1) * 128]
            v1 = out1[p * 32 : (p + 1) * 32, y * 128 : (y + 1) * 128]
            o_ref[p, pl.ds(y, 32, stride=LINE), :] = jnp.where(first, v0, v1)
    for p in range(pairs):
        part = o_ref[p].reshape(32, LINE, 128).astype(BF16)
        send_ref[:, :, p * 128 : (p + 1) * 128] = part


def whole(a):
    return pl.BlockSpec(a.shape, lambda *_: (0,) * a.ndim)


def mid_x(layer, core, recv, w0, w1, c):
    weights = pl.BlockSpec((16, 1, CH, 128), lambda i: (0, layer, 0, 0))
    return pl.pallas_call(
        mid_x_kernel,
        name="mid_x",
        grid=(1,),
        in_specs=[pl.BlockSpec(memory_space=pltpu.SMEM)]
        + [whole(recv), weights, weights, whole(c["mid_x"])],
        out_specs=whole(recv),
        out_shape=jax.ShapeDtypeStruct(recv.shape, BF16),
        scratch_shapes=[
            pltpu.VMEM((RX // 2, 256, 128), F32),
            pltpu.VMEM((MODES * LINE, 128), F32),
            pltpu.VMEM((MODES * LINE, 128), F32),
            pltpu.VMEM((RX // 2, 256, 128), F32),
        ],
        compiler_params=params(16),
        cost_estimate=estimate(3),
    )(core, recv, w0, w1, c["mid_x"])


def mid_y_kernel(me_ref, *refs):
    z_refs, tab_ref, out_refs = refs[:8], refs[8], refs[9:13]
    xs_ref, ms_ref, w_ref = refs[13:]
    first = half_mask(MODES)
    lines = 16
    half, quarter = me_ref[0] // 4, lax.rem(me_ref[0], 4)
    sources = []
    for flip, step in ((0, 0),) + SHIFTS:
        near = half + flip - 2 * flip * half
        sources.append(near * 4 + lax.rem(quarter + 4 - step, 4))
    table = [tab_ref[0, src].astype(F32) for src in sources]
    forward = jnp.concatenate(table, axis=0).T[:64].astype(BF16)
    table = [tab_ref[1, half * 4 + lax.rem(quarter + step, 4)].astype(F32) for step in range(4)]
    inverse = jnp.concatenate(table, axis=0)[:, :64].astype(BF16)
    for g in range(2):
        z = [ref[:RYP, g * 512 : (g + 1) * 512].astype(F32) for ref in z_refs]
        z = jnp.concatenate(z, axis=0).astype(BF16)
        spec = dot(forward, z)
        for b in range(4):
            re = spec[0:32, b * 128 : (b + 1) * 128]
            im = spec[32:64, b * 128 : (b + 1) * 128]
            line = g * 8 + 2 * b
            xs_ref[pl.ds(line, MODES, stride=lines), :] = jnp.where(
                first, re, pltpu.roll(im, 64, 1)
            )
            xs_ref[pl.ds(line + 1, MODES, stride=lines), :] = jnp.where(
                first, pltpu.roll(re, 64, 1), im
            )
    for ref, src in zip(z_refs, sources):
        packed = ref[RYP:, :].astype(F32)
        for j in range(4):
            tiles = [packed[j * 8 : (j + 1) * 8, t * 128 : (t + 1) * 128] for t in range(8)]
            w_ref[src, j] = jnp.concatenate(tiles, axis=0).astype(BF16)
    weights = lambda src: [(src * 4 + j, w_ref[src, j]) for j in range(4)]
    mix(xs_ref, ms_ref, lines, 8, 4, weights)
    for g in range(2):
        cols = []
        for b in range(4):
            line = g * 8 + 2 * b
            m0 = ms_ref[pl.ds(line, MODES, stride=lines), :]
            m1 = ms_ref[pl.ds(line + 1, MODES, stride=lines), :]
            re = jnp.where(first, m0, pltpu.roll(m1, 64, 1))
            im = jnp.where(first, pltpu.roll(m0, 64, 1), m1)
            cols.append(jnp.concatenate([re, im], axis=0).astype(BF16))
        out = dot(inverse, jnp.concatenate(cols, axis=1)).astype(BF16)
        for step in range(4):
            out_refs[step][:, g * 512 : (g + 1) * 512] = out[step * RYP : (step + 1) * RYP]


def mid_y(me, zs, c):
    return pl.pallas_call(
        mid_y_kernel,
        name="mid_y",
        grid=(1,),
        in_specs=[pl.BlockSpec(memory_space=pltpu.SMEM)]
        + [whole(z) for z in zs]
        + [whole(c["mid_y"])],
        out_specs=[pl.BlockSpec((RYP, QUARTER), lambda i: (0, 0))] * 4,
        scratch_shapes=[pltpu.VMEM((MODES * 16, 128), F32)] * 2
        + [pltpu.VMEM((8, 4, CH, 128), BF16)],
        out_shape=[jax.ShapeDtypeStruct((RYP, QUARTER), BF16)] * 4,
        compiler_params=params(20),
        cost_estimate=estimate(2),
    )(me, *zs, c["mid_y"])


def gelu(x):
    x = x.astype(BF16)
    inner = x * (0.7978845608028654 + 0.035677408136300125 * (x * x))
    half = 0.5 * x
    return half + half * jnp.tanh(inner)


def last_kernel(more, group, *refs):
    me_ref, yx_ref, bx_ref = refs[:3]
    yy_refs = refs[3:7]
    cy_ref, state_ref, we_ref, wr_ref = refs[7:11]
    if more:
        wy_ref, out_ref, zx_ref, zy_ref, kron_ref, we4_ref, wr4_ref, yy_ref, acc_ref = refs[11:]
    else:
        out_ref, kron_ref, we4_ref, wr4_ref, yy_ref, t_ref = refs[11:]
    g = pl.program_id(0)

    @pl.when(g == 0)
    def _():
        we4_ref[...] = jnp.zeros_like(we4_ref)
        wr4_ref[...] = jnp.zeros_like(wr4_ref)
        for j in range(4):
            we4_ref[j * CH : (j + 1) * CH, j * HID : (j + 1) * HID] = we_ref[0]
            wr4_ref[j * CH : (j + 1) * CH, j * HID : (j + 1) * HID] = wr_ref[0]
        for step in range(4):
            yy_ref[lax.rem(me_ref[0] + 4 - step, 4)] = yy_refs[step][...]

    fill_kron(bx_ref, kron_ref)
    basis = cy_ref[...].astype(F32).T.astype(BF16)
    for j in range(group // 4):
        lanes = slice(j * 256, (j + 1) * 256)
        if j % 2 == 0:
            both = slice(j * 256, (j + 2) * 256)
            yy = yy_ref[g * (group // 16) + j // 4, :, j % 4 * 256 : (j % 4 + 2) * 256]
            total = dot(yx_ref[...], kron_ref[:, both]) + dot(basis, yy)
            total = total.astype(BF16)
            total = jnp.concatenate([total[:, :256], total[:, 256:]], axis=0)
            hidden = gelu(dot(total, we4_ref[...])).astype(BF16)
            updates = dot_nt(hidden, wr4_ref[...])
        update = updates[(j % 2) * 256 : (j % 2 + 1) * 256]
        new = state_ref[:, lanes].astype(F32) + update
        if more:
            out_ref[:, lanes] = new.astype(BF16)
            continue
        for h in range(2):
            for p in range(2):
                block = new[h * 128 : (h + 1) * 128, p * 128 : (p + 1) * 128].T
                x = j * 4 + p * 2
                t_ref[h, pl.ds(x, CH, stride=group), :] = block[:CH]
                t_ref[h, pl.ds(x + 1, CH, stride=group), :] = block[CH:]
    if more:
        coefficients(g, out_ref[...], kron_ref, cy_ref, wy_ref, acc_ref, zx_ref, zy_ref)
    else:
        for h in range(2):
            part = t_ref[h].reshape(CH, group, 128).astype(BF16)
            out_ref[:, :, h * 128 : (h + 1) * 128] = part


def last_call(layer, more, me, yx, yy, state, we, wr, wy, c):
    group = LAST_GROUPS[layer]
    wide = group * CH
    in_specs = [
        pl.BlockSpec(memory_space=pltpu.SMEM),
        pl.BlockSpec((256, RX * CH), lambda g: (0, 0)),
        pl.BlockSpec((16, 128), lambda g: (0, 0)),
        *[pl.BlockSpec((RYP, QUARTER), lambda g: (0, 0))] * 4,
        pl.BlockSpec((RYP, 256), lambda g: (0, 0)),
        pl.BlockSpec((256, wide), lambda g: (0, g)),
        pl.BlockSpec((1, CH, HID), lambda g: (layer, 0, 0)),
        pl.BlockSpec((1, CH, HID), lambda g: (layer, 0, 0)),
    ]
    scratch = [pltpu.VMEM((RX * CH, wide), BF16)] + [pltpu.VMEM((256, 1024), BF16)] * 2
    scratch.append(pltpu.VMEM((4, RYP, QUARTER), BF16))
    args = [me, yx, c["bx"], *yy, c["cy"], state, we, wr]
    if more:
        in_specs.append(
            pl.BlockSpec((1, ROWS - RYP, QUARTER), lambda g: (layer + 1, 0, 0))
        )
        args.append(wy)
        out_specs = [
            pl.BlockSpec((256, wide), lambda g: (0, g)),
            pl.BlockSpec((256, RX * CH), lambda g: (0, 0)),
            pl.BlockSpec((group // 16, ROWS, QUARTER), lambda g: (g, 0, 0)),
        ]
        out_shape = [
            jax.ShapeDtypeStruct((256, 4096), BF16),
            jax.ShapeDtypeStruct((256, RX * CH), BF16),
            jax.ShapeDtypeStruct((4, ROWS, QUARTER), BF16),
        ]
        scratch.append(pltpu.VMEM((256, RX * CH), F32))
    else:
        out_specs = [pl.BlockSpec((CH, group, 256), lambda g: (0, g, 0))]
        out_shape = [jax.ShapeDtypeStruct((CH, 64, 256), BF16)]
        scratch.append(pltpu.VMEM((2, CH * group, 128), F32))
    return pl.pallas_call(
        functools.partial(last_kernel, more, group),
        name="last",
        grid=(64 // group,),
        in_specs=in_specs,
        out_specs=out_specs,
        out_shape=out_shape,
        scratch_shapes=scratch,
        compiler_params=params(40),
        cost_estimate=estimate(12),
    )(*args)


def join(parts):
    return jnp.concatenate([part.astype(F32) for part in parts], axis=1)


def pack_x_kernel(w_ref, out_ref):
    for layer in range(LAYERS):
        own = join([w_ref[layer, 0, i] for i in range(2)]).astype(BF16)
        for i in range(16):
            out_ref[i, layer] = own


def pack_y_kernel(w_ref, out_ref):
    for layer in range(LAYERS):
        rows = []
        for j in range(4):
            own = join([w_ref[layer, j, i] for i in range(2)])
            rows.append(join([own[t * 8 : (t + 1) * 8] for t in range(8)]))
        out_ref[layer] = jnp.concatenate(rows, axis=0).astype(BF16)


def pack_call(kernel, name, weights, shape):
    out_shape = jax.ShapeDtypeStruct(shape, BF16)
    return pl.pallas_call(
        kernel,
        name=name,
        grid=(1,),
        in_specs=[whole(weights)],
        out_specs=whole(out_shape),
        out_shape=out_shape,
        compiler_params=params(16),
        cost_estimate=estimate(1),
    )(weights)


def swap_cores(x):
    return lax.ppermute(x, "gx", [(i, i ^ 1) for i in range(32)])


def permute_y(x, flip, step):
    return lax.ppermute(x, "gy", [(i, moved(i, flip, step)) for i in range(8)])


def body(state_field, spectral_x, spectral_y, expand_weight, reduce_weight):
    c = {name: jnp.asarray(value) for name, value in make_constants().items()}
    core = lax.rem(lax.axis_index("gx"), 2).reshape(1).astype(jnp.int32)
    me = lax.axis_index("gy").reshape(1).astype(jnp.int32)
    own_x = pack_call(pack_x_kernel, "pack_x", spectral_x, (16, LAYERS, CH, 128))
    own_x, spectral_y = lax.optimization_barrier((own_x, spectral_y))
    wy = pack_call(pack_y_kernel, "pack_y", spectral_y, (LAYERS, ROWS - RYP, QUARTER))
    same_core = [list(range(s, 32, 2)) for s in range(2)]
    mine = lax.all_to_all(own_x, "gx", 0, 0, axis_index_groups=same_core, tiled=True)
    swapped = swap_cores(mine)
    wr = jnp.swapaxes(reduce_weight, 1, 2)
    state, zx, zy = first_call(state_field[0], wy, c)
    for l in range(LAYERS):
        state = pltpu.with_memory_space_constraint(state, pltpu.HBM)
        zs = []
        for flip, step in ((0, 0),) + SHIFTS:
            chunk = lax.dynamic_slice_in_dim(zy, lax.rem(me[0] + step, 4), 1, 0)[0]
            zs.append(permute_y(chunk, flip, step) if flip or step else chunk)
        recv = lax.all_to_all(zx.reshape(32, LINE, RX * CH), "gx", 0, 0, tiled=True)
        zs, recv = lax.optimization_barrier((zs, recv))
        send = mid_x(l, core, recv, mine, swapped, c)
        yx = lax.all_to_all(send, "gx", 0, 0, tiled=True).reshape(256, RX * CH)
        yy = mid_y(me, zs, c)
        yy = [yy[0]] + [permute_y(yy[step], 0, step) for step in range(1, 4)]
        more = l + 1 < LAYERS
        got = last_call(l, more, me, yx, yy, state, expand_weight, wr, wy, c)
        if more:
            state, zx, zy = got
    return got[0][None]


def solution(mesh):
    in_specs = (
        P(None, None, "gx", "gy"),
        P(None, "gx", None, None, None),
        P(None, "gy", None, None, None),
        P(),
        P(),
    )
    out_specs = P(None, None, "gx", "gy")
    return jax.shard_map(body, mesh=mesh, in_specs=in_specs, out_specs=out_specs, check_vma=False)
```
